32 devices in a mesh: dp: 8 (over y, x, core), tensor: 4 (over z).
Axes of the slice: x: 2, y: 2, z: 4, core: 2. Of those that a mesh axis runs over, the one named last changes fastest.
Arguments:
- layer_input: bfloat16 [16384, 768], P(('dp', 'tensor')), may hold values from -12 to 12
- segments: int32 [16384], P('dp'), may hold values from 0 to 63, never falling along the last dimension, each value on 1 to 1024 neighbouring positions
- w_qkv: bfloat16 [3, 768, 768], P(None, None, 'tensor'), may hold values from -0.21875 to 0.21875
- bias_qv: bfloat16 [2, 768], P(None, 'tensor'), may hold values from -1.5 to 1.5
- w_out: bfloat16 [768, 768], P('tensor'), may hold values from -1.25 to 1.25
- b_out: bfloat16 [768], replicated, may hold values from -1.5 to 1.5
- gain_attn: bfloat16 [768], replicated, may hold values from 0.5 to 1.5
- shift_attn: bfloat16 [768], replicated, may hold values from -1.5 to 1.5
- w_in: bfloat16 [768, 3072], P(None, 'tensor'), may hold values from -0.21875 to 0.21875
- b_in: bfloat16 [3072], P('tensor'), may hold values from -1.5 to 1.5
- w_down: bfloat16 [3072, 768], P('tensor'), may hold values from -0.109375 to 0.109375
- b_down: bfloat16 [768], replicated, may hold values from -1.5 to 1.5
- gain_ffn: bfloat16 [768], replicated, may hold values from 0.5 to 1.5
- shift_ffn: bfloat16 [768], replicated, may hold values from -1.5 to 1.5
- act_scale: float32 [4], replicated, may hold values from 4 to 77
- out_grad: bfloat16 [16384, 768], P(('dp', 'tensor')), may hold values from -6 to 6
Outputs:
- layer_output: bfloat16 [16384, 768], P(('dp', 'tensor'))
- input_grad: float32 [16384, 768], P(('dp', 'tensor'))
- grad_qkv: float32 [3, 768, 768], P(None, None, 'tensor')
- grad_bias_qv: float32 [2, 768], P(None, 'tensor')
- grad_out: float32 [768, 768], P('tensor')
- grad_b_out: float32 [768], replicated
- grad_gain_attn: float32 [768], replicated
- grad_shift_attn: float32 [768], replicated
- grad_in: float32 [768, 3072], P(None, 'tensor')
- grad_b_in: float32 [3072], P('tensor')
- grad_down: float32 [3072, 768], P('tensor')
- grad_b_down: float32 [768], replicated
- grad_gain_ffn: float32 [768], replicated
- grad_shift_ffn: float32 [768], replicated
- new_scale: float32 [4], replicated
- batch_max: float32 [4], replicated
The draws below stay inside these ranges and needn't reach their ends.
Inputs may be any that keep to these rules, and one draw needn't show every extreme that they name: `segments`: segment ids never fall along the tokens; each document has 1 to 1024 tokens and one has exactly 1024; attention stays within each row of 1024 tokens.
All inputs are finite; a program needn't handle non-finite values.
Results may differ from the reference program's by a relative error of at most 0.013.
The reference program's roundings to bfloat16 on the way count: a program that leaves them out, or rounds other values in their place, can miss the bound.
Values may be sent and summed in bfloat16 or wider, within the bound.
No kernel may reach another device: no remote copies, remote signals or barrier semaphores. Data moves between devices by JAX's collectives and lax.ppermute only.
A program may use at most 192 MiB of HBM per device.

```python
import math
import jax
import jax.numpy as jnp
import numpy as np
from jax import lax

D = 768
HEADS = 12
HEAD = 64
FF = 3072
LEN = 1024
ROWS = 16
TOKENS = 16384
DOCS = 64


def draw_layer_input(key, part):
    position = jnp.arange(TOKENS, dtype=jnp.float32)[:, None]
    row_rise = 1.0 + 2.0 * position / (TOKENS - 1)
    base_draw = jnp.clip(jax.random.normal(key, (TOKENS, D), jnp.float32), -4.0, 4.0)
    return (base_draw * row_rise).astype(jnp.bfloat16)


def draw_act_scale(key, part):
    levels = jnp.array([5.0, 64.0, 64.0, 64.0], jnp.float32)
    return levels * jax.random.uniform(key, (4,), jnp.float32, 0.8, 1.2)


def steps_of(stream_key, extent, split, low, largest):
    loudness = 1.0
    for dim, parts in split:
        draws = jax.random.uniform(jax.random.fold_in(jax.random.fold_in(stream_key, 6), dim), (parts,), jnp.float32, low / len(split), largest / len(split))
        loudness = loudness * jnp.repeat(jnp.exp(draws), extent[dim] // parts).reshape((-1,) + (1,) * (len(extent) - 1 - dim))
    return loudness


def split_up(count, total, bound, lean):
    weights = [(1 << 20) // math.isqrt(grade ** lean) + 1 for grade in range(2, count + 1)]
    surplus, holding = total - bound - (count - 1), [1] * (count - 1)
    while surplus > 0:
        movable = [i for i in range(count - 1) if holding[i] < bound]
        whole, budget = sum([weights[i] for i in movable]), surplus
        for i in movable:
            more = min(bound - holding[i], max(1, budget * weights[i] // whole), surplus)
            holding[i] = holding[i] + more
            surplus = surplus - more
    return np.array([bound] + holding)


def ragged(key, number_of, total, bound, slope):
    if number_of == 2:
        one = jax.random.randint(key, (), max(1, total - bound), min(bound, total - 1) + 1)
        return jnp.stack([one, total - one])
    tallies = jnp.asarray(split_up(number_of, total, bound, slope), jnp.int32)
    twos = (number_of - 1) // 2
    donor, taker = tallies[1:1 + 2 * twos:2], tallies[2:2 + 2 * twos:2]
    margin = jnp.minimum(donor - 1, bound - taker)
    moved = jax.random.randint(jax.random.fold_in(key, 1), (twos,), 0, 1 << 20) % (margin + 1)
    tallies = tallies.at[1:1 + 2 * twos:2].set(donor - moved).at[2:2 + 2 * twos:2].set(taker + moved)
    return tallies[jax.random.permutation(jax.random.fold_in(key, 2), number_of)]


def noise(rng, shape, scale, limit, pieces=(), kind=jnp.bfloat16):
    entries = scale * jax.random.normal(rng, shape, jnp.float32)
    if pieces:
        entries = entries * steps_of(rng, shape, pieces, -0.22, 0.18)
    return jnp.clip(entries, -limit, limit).astype(kind)


def setup_inputs(seed: int = 0) -> dict:
    streams_of = jax.random.split(jax.random.key(seed), 17)
    layer_input = draw_layer_input(jax.random.fold_in(streams_of[16], 71), 0)
    segments = jnp.searchsorted(jnp.cumsum(ragged(streams_of[1], DOCS, TOKENS, LEN, 1)), jnp.arange(TOKENS), side="right").astype(jnp.int32)
    w_qkv = noise(streams_of[2], (3, D, D), D ** -0.5, 0.21875, ((2, 4),))
    bias_qv = noise(streams_of[3], (2, D), 0.3, 1.5, ((1, 4),))
    w_out = noise(streams_of[4], (D, D), (D // 32) ** -0.5, 1.25, ((0, 4),))
    b_out = noise(streams_of[5], (D,), 0.3, 1.5)
    gain_attn = jnp.clip(1.0 + 0.1 * jax.random.normal(streams_of[6], (D,), jnp.float32), 0.5, 1.5).astype(jnp.bfloat16)
    shift_attn = noise(streams_of[7], (D,), 0.3, 1.5)
    w_in = noise(streams_of[8], (D, FF), D ** -0.5, 0.21875, ((1, 4),))
    b_in = noise(streams_of[9], (FF,), 0.3, 1.5, ((0, 4),))
    w_down = noise(streams_of[10], (FF, D), FF ** -0.5, 0.109375, ((0, 4),))
    b_down = noise(streams_of[11], (D,), 0.3, 1.5)
    gain_ffn = jnp.clip(1.0 + 0.1 * jax.random.normal(streams_of[12], (D,), jnp.float32), 0.5, 1.5).astype(jnp.bfloat16)
    shift_ffn = noise(streams_of[13], (D,), 0.3, 1.5)
    act_scale = draw_act_scale(jax.random.fold_in(streams_of[16], 71), 0)
    out_grad = noise(streams_of[15], (TOKENS, D), 1.0, 6.0, ((0, 32),))
    return dict(layer_input=layer_input, segments=segments, w_qkv=w_qkv, bias_qv=bias_qv, w_out=w_out, b_out=b_out, gain_attn=gain_attn, shift_attn=shift_attn, w_in=w_in, b_in=b_in, w_down=w_down, b_down=b_down, gain_ffn=gain_ffn, shift_ffn=shift_ffn, act_scale=act_scale, out_grad=out_grad)


HIGH = lax.Precision.HIGHEST
EPSILON = 1e-12
DECAY = 0.9999
MASKED = -1e+30

@jax.custom_vjp
def low(v):
    return lax.optimization_barrier(v.astype(jnp.bfloat16)).astype(jnp.float32)

@jax.custom_vjp
def low_back(v):
    return v

def low_keep(v):
    return (low(v), None)

def low_pass(kept, grad):
    return (grad,)

def back_keep(v):
    return (v, None)

def back_low(kept, grad):
    return (low(grad),)
low.defvjp(low_keep, low_pass)
low_back.defvjp(back_keep, back_low)

def layer_norm(resid, gain, shift):
    row_mean = lax.optimization_barrier(jnp.mean(resid, axis=-1, keepdims=True))
    centred = resid - row_mean
    spread = lax.optimization_barrier(jnp.mean(centred * centred, axis=-1, keepdims=True))
    return centred * lax.rsqrt(spread + EPSILON) * gain + shift

def row_attention(row_proj, row_segs):
    queries = row_proj[0].reshape(LEN, HEADS, HEAD)
    key_rows = row_proj[1].reshape(LEN, HEADS, HEAD)
    value_rows = row_proj[2].reshape(LEN, HEADS, HEAD)
    same_doc = row_segs[:, None] == row_segs[None, :]
    raw_scores = jnp.einsum('qhd,khd->hqk', queries, key_rows, precision=HIGH)
    scores = jnp.where(same_doc[None], low_back(raw_scores) * HEAD ** (-0.5), MASKED)
    row_top = lax.optimization_barrier(jnp.max(scores, axis=-1, keepdims=True))
    exponent = jnp.exp(scores - row_top)
    attention = exponent / lax.optimization_barrier(jnp.sum(exponent, axis=-1, keepdims=True))
    context = jnp.einsum('hqk,khd->qhd', low(attention), value_rows, precision=HIGH)
    return context.reshape(LEN, D)

def forward(params, segments, act_scale):
    x_full, w_qkv, bias_qv, w_out, b_out, gain_attn, shift_attn, w_in, b_in, w_down, b_down, gain_ffn, shift_ffn = params
    x_quant = low(jnp.clip(x_full, -act_scale[0], act_scale[0]))
    bias_all = jnp.stack([bias_qv[0], jnp.zeros_like(bias_qv[0]), bias_qv[1]])
    projected = jnp.einsum('td,cde->cte', x_quant, w_qkv, precision=HIGH)
    proj = low(low_back(projected) + bias_all[:, None, :])
    row_proj = jnp.swapaxes(proj.reshape(3, ROWS, LEN, D), 0, 1)
    checked = jax.checkpoint(row_attention)
    context = lax.map(lambda row_pair: checked(row_pair[0], row_pair[1]), (row_proj, segments.reshape(ROWS, LEN))).reshape(TOKENS, D)
    ctx_quant = low(jnp.clip(low_back(context), -act_scale[1], act_scale[1]))
    attn_out = low_back(jnp.dot(ctx_quant, w_out, precision=HIGH, preferred_element_type=jnp.float32)) + b_out
    hidden = layer_norm(x_full + attn_out, gain_attn, shift_attn)
    hid_quant = low(jnp.clip(hidden, -act_scale[2], act_scale[2]))
    pre_act = low_back(jnp.dot(hid_quant, w_in, precision=HIGH, preferred_element_type=jnp.float32)) + b_in
    activated = jax.nn.gelu(pre_act, approximate=False)
    act_quant = low(jnp.clip(activated, -act_scale[3], act_scale[3]))
    ffn_out = low_back(jnp.dot(act_quant, w_down, precision=HIGH, preferred_element_type=jnp.float32)) + b_down
    final = layer_norm(hidden + ffn_out, gain_ffn, shift_ffn)
    maxima = jnp.stack([jnp.max(jnp.abs(x_full)), jnp.max(jnp.abs(context)), jnp.max(jnp.abs(hidden)), jnp.max(jnp.abs(activated))])
    return (final, maxima)

def reference(layer_input, segments, w_qkv, bias_qv, w_out, b_out, gain_attn, shift_attn, w_in, b_in, w_down, b_down, gain_ffn, shift_ffn, act_scale, out_grad):
    params = tuple((array.astype(jnp.float32) for array in (layer_input, w_qkv, bias_qv, w_out, b_out, gain_attn, shift_attn, w_in, b_in, w_down, b_down, gain_ffn, shift_ffn)))

    def apply_layer(inner):
        return forward(inner, segments, act_scale)
    result, pullback, maxima = jax.vjp(apply_layer, params, has_aux=True)
    gradients = pullback(out_grad.astype(jnp.float32))[0]
    new_scale = DECAY * act_scale + (1.0 - DECAY) * maxima
    return (result.astype(jnp.bfloat16), gradients[0], gradients[1], gradients[2], gradients[3], gradients[4], gradients[5], gradients[6], gradients[7], gradients[8], gradients[9], gradients[10], gradients[11], gradients[12], new_scale, maxima)
```

```python
import functools
import math

import jax
import jax.numpy as jnp
from jax import lax
from jax.experimental import pallas as pl
from jax.experimental.pallas import tpu as pltpu
from jax.sharding import PartitionSpec as P

HEAD = 64
LEN = 1024
HALF = LEN // 2
BLOCK = 256
ROWS_PIECE = 200

EPSILON = 1e-12
DECAY = 0.9999
MASKED = -1e30
JOINT = ("dp", "tensor")
BF16 = jnp.bfloat16
F32 = jnp.float32


def norm_forward(resid, gain, shift):
    row_mean = jnp.mean(resid, axis=-1, keepdims=True)
    centred = resid - row_mean
    spread = jnp.mean(centred * centred, axis=-1, keepdims=True)
    inverse = lax.rsqrt(spread + EPSILON)
    normed = centred * inverse
    return (normed * gain + shift, normed, inverse)


def norm_backward(upstream, normed, inverse, gain):
    scaled = upstream * gain
    mean_first = jnp.mean(scaled, axis=-1, keepdims=True)
    mean_second = jnp.mean(scaled * normed, axis=-1, keepdims=True)
    return inverse * (scaled - mean_first - normed * mean_second)


def nt(a, b):
    return lax.dot_general(a, b, (((1,), (1,)), ((), ())), preferred_element_type=F32)


def nn(a, b):
    return lax.dot_general(a, b, (((1,), (0,)), ((), ())), preferred_element_type=F32)


def tn(a, b):
    return lax.dot_general(a, b, (((0,), (0,)), ((), ())), preferred_element_type=F32)


def attend_kernel(q_ref, k_ref, v_ref, seg_col_ref, seg_row_ref, ctx_ref, lse_ref):
    low = lax.broadcasted_iota(jnp.int32, (BLOCK, 2 * HEAD), 1) < HEAD
    keys = k_ref[...]
    values = v_ref[...]
    for block in range(LEN // BLOCK):
        rows = pl.ds(block * BLOCK, BLOCK)
        queries = q_ref[rows, :] * jnp.asarray(HEAD**-0.5, BF16)
        same = seg_col_ref[rows, :] == seg_row_ref[...]
        parts, logs = [], []
        for head in range(2):
            own = low if head == 0 else jnp.logical_not(low)
            scores = nt(jnp.where(own, queries, jnp.zeros_like(queries)), keys)
            scores = jnp.where(same, scores, MASKED)
            top = jnp.max(scores, axis=-1, keepdims=True)
            exponent = jnp.exp(scores - top)
            total = jnp.sum(exponent, axis=-1, keepdims=True)
            attention = (exponent * (1.0 / total)).astype(BF16)
            parts.append(nn(attention, values))
            logs.append(top + jnp.log(total))
        ctx_ref[rows, :] = jnp.where(low, parts[0], parts[1])
        lse_ref[0, rows, :] = jnp.concatenate(logs, axis=1)


def attend(proj, seg_col, seg_row, pairs_of_heads):
    n = pairs_of_heads
    return pl.pallas_call(
        attend_kernel,
        grid=(n,),
        in_specs=[
            pl.BlockSpec((LEN, 2 * HEAD), lambda i: (0, i)),
            pl.BlockSpec((LEN, 2 * HEAD), lambda i: (0, n + i)),
            pl.BlockSpec((LEN, 2 * HEAD), lambda i: (0, 2 * n + i)),
            pl.BlockSpec((LEN, 1), lambda i: (0, 0)),
            pl.BlockSpec((1, LEN), lambda i: (0, 0)),
        ],
        out_specs=[
            pl.BlockSpec((LEN, 2 * HEAD), lambda i: (0, i)),
            pl.BlockSpec((1, LEN, 2), lambda i: (i, 0, 0)),
        ],
        out_shape=[
            jax.ShapeDtypeStruct((LEN, n * 2 * HEAD), F32),
            jax.ShapeDtypeStruct((n, LEN, 2), F32),
        ],
        name="attend",
    )(proj, proj, proj, seg_col, seg_row)


def attend_back_kernel(
    q_ref,
    k_ref,
    v_ref,
    g_ref,
    lse_ref,
    inner_ref,
    seg_col_ref,
    seg_row_ref,
    dq_ref,
    dk_ref,
    dv_ref,
    sum_ref,
    acc_ref,
):
    low = lax.broadcasted_iota(jnp.int32, (BLOCK, 2 * HEAD), 1) < HEAD
    queries = q_ref[...]
    grads = g_ref[...]
    value_sum = jnp.zeros((1, 2 * HEAD), F32)
    for block in range(LEN // BLOCK):
        rows = pl.ds(block * BLOCK, BLOCK)
        keys = k_ref[rows, :]
        scaled_keys = keys * jnp.asarray(HEAD**-0.5, BF16)
        values = v_ref[rows, :]
        same = seg_col_ref[rows, :] == seg_row_ref[...]
        value_parts, key_parts = [], []
        for head in range(2):
            own = low if head == 0 else jnp.logical_not(low)
            zero = jnp.zeros_like(keys)
            scores = nt(jnp.where(own, scaled_keys, zero), queries)
            logs = lse_ref[0, head : head + 1, :]
            attention = jnp.where(same, jnp.exp(scores - logs), 0.0)
            value_parts.append(nn(attention.astype(BF16), grads))
            grad_attention = nt(jnp.where(own, values, zero), grads)
            inner = inner_ref[0, head : head + 1, :]
            grad_score = (attention * (grad_attention - inner) * HEAD**-0.5).astype(BF16)
            key_parts.append(nn(grad_score, queries))
            part = tn(grad_score, jnp.where(own, keys, zero))
            if block == 0 and head == 0:
                acc_ref[...] = part
            else:
                acc_ref[...] += part
        grad_value = jnp.where(low, value_parts[0], value_parts[1])
        value_sum += jnp.sum(grad_value, axis=0, keepdims=True)
        dv_ref[rows, :] = grad_value.astype(BF16)
        dk_ref[rows, :] = jnp.where(low, key_parts[0], key_parts[1]).astype(BF16)
    grad_query = acc_ref[...]
    dq_ref[...] = grad_query.astype(BF16)
    sum_ref[0, 0:1, :] = jnp.sum(grad_query, axis=0, keepdims=True)
    sum_ref[0, 1:2, :] = value_sum


def attend_back(proj, grad_ctx, lse, inner, seg_col, seg_row, pairs_of_heads):
    n = pairs_of_heads
    wide = jax.ShapeDtypeStruct((LEN, n * 2 * HEAD), BF16)
    return pl.pallas_call(
        attend_back_kernel,
        grid=(n,),
        in_specs=[
            pl.BlockSpec((LEN, 2 * HEAD), lambda i: (0, i)),
            pl.BlockSpec((LEN, 2 * HEAD), lambda i: (0, n + i)),
            pl.BlockSpec((LEN, 2 * HEAD), lambda i: (0, 2 * n + i)),
            pl.BlockSpec((LEN, 2 * HEAD), lambda i: (0, i)),
            pl.BlockSpec((1, 2, LEN), lambda i: (i, 0, 0)),
            pl.BlockSpec((1, 2, LEN), lambda i: (i, 0, 0)),
            pl.BlockSpec((LEN, 1), lambda i: (0, 0)),
            pl.BlockSpec((1, LEN), lambda i: (0, 0)),
        ],
        out_specs=[
            pl.BlockSpec((LEN, 2 * HEAD), lambda i: (0, i)),
            pl.BlockSpec((LEN, 2 * HEAD), lambda i: (0, i)),
            pl.BlockSpec((LEN, 2 * HEAD), lambda i: (0, i)),
            pl.BlockSpec((1, 2, 2 * HEAD), lambda i: (i, 0, 0)),
        ],
        out_shape=[wide, wide, wide, jax.ShapeDtypeStruct((n, 2, 2 * HEAD), F32)],
        scratch_shapes=[pltpu.VMEM((LEN, 2 * HEAD), F32)],
        name="attend_back",
    )(proj, proj, proj, grad_ctx, lse, inner, seg_col, seg_row)


class Links:
    def __init__(self, dp, depths):
        self.dp, self.depths = dp, depths
        self.planes = dp // 2
        place = lax.axis_index("dp")
        self.half, self.plane = place % 2, place // 2
        self.depth = lax.axis_index("tensor")
        self.square = self.planes == 4 and depths == 4

    def permute(self, array, move):
        pairs = []
        for place in range(self.dp):
            for depth in range(self.depths):
                to = move(place // 2, place % 2, depth)
                if to is not None:
                    plane, half, level = to
                    pairs.append(
                        (place * self.depths + depth, (2 * plane + half) * self.depths + level)
                    )
        return lax.ppermute(array, JOINT, pairs)

    def rows_home(self, array):
        return self.permute(array, lambda e, c, z: (e, z % 2, z - z % 2 + c))

    def other_half(self, array):
        return self.permute(array, lambda e, c, z: (e, 1 - c, z))

    def across(self, array, step, only=None):
        return self.permute(
            array,
            lambda e, c, z: (e ^ step, c, z) if only is None or only(c, z) else None,
        )

    def along(self, array, step):
        return self.permute(array, lambda e, c, z: (e, c, z ^ step))

    def spread(self, piece, only=None):
        cut = piece.shape[-2] // 16 * 8
        first = self.across(piece, 1, only)
        second = self.across(piece, 2, only)
        third_low = self.across(second[..., :cut, :], 1, only)
        third_high = self.across(first[..., cut:, :], 2, only)
        return [piece, first, second, jnp.concatenate([third_low, third_high], axis=-2)]

    def collect(self, pieces):
        cut = pieces[0].shape[-2] // 16 * 8
        low = [p[..., :cut, :] for p in pieces]
        high = [p[..., cut:, :] for p in pieces]
        low_in = self.across(jnp.stack([low[1], low[3]]), 1)
        high_in = self.across(jnp.stack([high[2], high[3]]), 2)

        def add(a, b):
            return a.astype(F32) + b.astype(F32)

        low_next = self.across(add(low[2], low_in[1]).astype(BF16), 2)
        high_next = self.across(add(high[1], high_in[1]).astype(BF16), 1)
        low_sum = add(low[0], low_in[0]) + low_next.astype(F32)
        high_sum = add(high[0], high_in[0]) + high_next.astype(F32)
        return jnp.concatenate([low_sum, high_sum], axis=-2)

    def in_order(self, pieces):
        stack = jnp.stack(pieces)
        return jnp.stack(
            [lax.dynamic_index_in_dim(stack, j ^ self.plane, 0, False) for j in range(4)]
        )

    def pair_moves(self):
        def near(e, c, z):
            return (e, c, z ^ 1) if z // 2 == c else None

        def far(flip):
            return lambda e, c, z: (e, c, (z ^ 2) ^ flip) if z // 2 == c else None

        return near, far(0), far(1)

    def gather_pair(self, packed):
        if not self.square:
            every = lax.all_gather(packed, "tensor", axis=0, tiled=False)
            two = lax.dynamic_slice_in_dim(every, 2 * self.half, 2, 0)
            return jnp.swapaxes(two, 0, 1)
        mine = lax.dynamic_index_in_dim(packed, self.plane, 0, False)
        near, far_even, far_odd = [self.permute(mine, m) for m in self.pair_moves()]
        inside = self.depth // 2 == self.half
        even = self.depth % 2 == 0
        a = jnp.where(inside, mine, far_even)
        b = jnp.where(inside, near, far_odd)
        both = jnp.stack([jnp.where(even, a, b), jnp.where(even, b, a)])
        return jnp.stack(self.spread(both))

    def reduce_pair(self, grads):
        if not self.square:
            blank = jnp.zeros((4,) + grads.shape[:1] + grads.shape[2:], F32)
            full = lax.dynamic_update_slice_in_dim(
                blank, jnp.swapaxes(grads, 0, 1).astype(F32), 2 * self.half, 0
            )
            shard = lax.psum_scatter(full, "tensor", scatter_dimension=0, tiled=False)
            return lax.psum(shard, "dp")
        total = self.collect([grads[j] for j in range(4)])
        even = self.depth % 2 == 0
        a = jnp.where(even, total[0], total[1])
        b = jnp.where(even, total[1], total[0]).astype(BF16)

        def inward(e, c, z):
            return (e, c, z ^ 1) if z // 2 == c else None

        def far(flip):
            return lambda e, c, z: (e, c, (z ^ 2) ^ flip) if z // 2 != c else None

        arrived = [
            self.permute(b, inward),
            self.permute(a.astype(BF16), far(0)),
            self.permute(b, far(1)),
        ]
        for part in arrived:
            a = a + part.astype(F32)
        pieces = self.in_order(self.spread(a.astype(BF16), lambda c, z: z // 2 == c))
        inside = self.depth // 2 == self.half
        return jnp.where(inside, pieces, self.other_half(pieces))

    def gather_all(self, packed):
        if not self.square:
            half = lax.dynamic_index_in_dim(packed, self.half, 0, False)
            return lax.all_gather(half, "tensor", axis=0, tiled=False)
        half = lax.dynamic_index_in_dim(packed, self.half, 0, False)
        own = jnp.stack(
            [lax.dynamic_index_in_dim(half, j ^ self.plane, 0, False) for j in range(4)]
        )
        others = jnp.stack([self.along(own[0], step) for step in (1, 2, 3)])
        return jnp.concatenate([own[None], jnp.stack(self.spread(others), axis=1)])

    def reduce_all(self, grads):
        if not self.square:
            blank = jnp.zeros((4, 2) + grads.shape[1:], F32)
            full = lax.dynamic_update_slice_in_dim(
                blank, grads[:, None].astype(F32), self.half, 1
            )
            shard = lax.psum_scatter(full, "tensor", scatter_dimension=0, tiled=False)
            return lax.psum(shard, "dp")
        total = self.collect([grads[:, j] for j in range(4)])
        sent = total.astype(BF16)
        mine = total[0]
        for step in (1, 2, 3):
            mine = mine + self.along(sent[step], step).astype(F32)
        pieces = self.in_order(self.spread(mine.astype(BF16)))
        return self.both_halves(pieces)

    def both_halves(self, mine):
        other = self.other_half(mine)
        first = self.half == 0
        return jnp.stack([jnp.where(first, mine, other), jnp.where(first, other, mine)])

    def combine(self, sums, maxima):
        if not self.square:
            return lax.psum(sums, JOINT), lax.pmax(maxima, JOINT)
        rows = sums.shape[0]
        wide = jnp.pad(maxima[None], ((0, 0), (0, sums.shape[1] - maxima.shape[0])))
        both = jnp.concatenate([sums, wide])
        is_sum = lax.broadcasted_iota(jnp.int32, both.shape, 0) < rows
        moves = [
            self.other_half,
            lambda v: self.across(v, 1),
            lambda v: self.across(v, 2),
            lambda v: self.along(v, 1),
            lambda v: self.along(v, 2),
        ]
        for move in moves:
            other = move(both)
            both = jnp.where(is_sum, both + other, jnp.maximum(both, other))
        return both[:rows], both[rows, : maxima.shape[0]]


def on_device(
    sizes,
    layer_input,
    segments,
    w_qkv,
    bias_qv,
    w_out,
    b_out,
    gain_attn,
    shift_attn,
    w_in,
    b_in,
    w_down,
    b_down,
    gain_ffn,
    shift_ffn,
    act_scale,
    out_grad,
):
    links = Links(*sizes)
    width = layer_input.shape[1]
    local = w_qkv.shape[2]
    heads = local // HEAD
    chunk = HEAD // 4
    units = w_in.shape[1]
    quarter = units // 8
    gain_first = gain_attn.astype(F32)
    gain_second = gain_ffn.astype(F32)

    rows = jnp.concatenate([jnp.swapaxes(w_qkv, 1, 2), w_out[None]])
    rows = rows.reshape(4, heads, 4, chunk, width).transpose(2, 0, 1, 3, 4)
    rows = rows.reshape(4, 4 * heads * chunk, width)
    tail = bias_qv.reshape(2, heads, 4, chunk).transpose(2, 0, 1, 3).reshape(4, 1, 2 * heads * chunk)
    tail = jnp.pad(tail, ((0, 0), (0, 7), (0, width - tail.shape[2])))
    attn_pack = jnp.concatenate([rows, tail], axis=1)
    ffn_rows = jnp.concatenate(
        [
            w_in.T.reshape(2, 4, quarter, width),
            w_down.reshape(2, 4, quarter, width),
            jnp.pad(b_in.reshape(2, 4, 1, quarter), ((0, 0), (0, 0), (0, 7), (0, width - quarter))),
        ],
        axis=2,
    )

    x_home = links.rows_home(layer_input)
    seg_rows = segments.reshape(2, LEN)
    seg_home = links.rows_home(
        lax.dynamic_index_in_dim(seg_rows, links.depth // 2, 0, False).reshape(8, LEN // 8)
    ).reshape(2, HALF)
    seg_home = jnp.where(links.half == 0, seg_home, seg_home[::-1]).reshape(LEN)
    seg_col, seg_row = seg_home[:, None], seg_home[None, :]
    attn_full = links.gather_pair(attn_pack)
    ffn_full = links.gather_all(ffn_rows)
    upstream = links.rows_home(out_grad).astype(F32)

    x_full = x_home.astype(F32)
    x_quant = jnp.clip(x_full, -act_scale[0], act_scale[0]).astype(BF16)
    x_rows = jnp.concatenate([x_quant, links.other_half(x_quant)])

    per = 4 * heads * chunk
    weights = attn_full[:, :, :per].reshape(4, 2, 4, heads, chunk, width)
    weights = weights.transpose(2, 1, 3, 0, 4, 5).reshape(4, 2 * local, width)
    w_proj = weights[:3].reshape(6 * local, width)
    w_back = weights[3]
    biases = attn_full[:, :, per, : per // 2].reshape(4, 2, 2, heads, chunk)
    biases = biases.transpose(2, 1, 3, 0, 4).reshape(2, 2 * local).astype(F32)
    bias_all = jnp.concatenate([biases[0], jnp.zeros_like(biases[0]), biases[1]])

    proj = (nt(x_rows, w_proj) + bias_all).astype(BF16)
    context, lse = attend(proj, seg_col, seg_row, heads)
    ctx_quant = jnp.clip(context, -act_scale[1], act_scale[1]).astype(BF16)
    attn_part = nn(ctx_quant, w_back)
    attn_out = attn_part[:HALF] + links.other_half(attn_part[HALF:]) + b_out.astype(F32)
    hidden, normed_attn, inverse_attn = norm_forward(
        x_full + attn_out, gain_first, shift_attn.astype(F32)
    )
    hid_quant = jnp.clip(hidden, -act_scale[2], act_scale[2]).astype(BF16)
    hid_rows = jnp.concatenate([hid_quant, links.other_half(hid_quant)])

    w_up = ffn_full[:, :, :quarter].reshape(2 * units, width)
    w_low = ffn_full[:, :, quarter : 2 * quarter].reshape(2 * units, width)
    b_up = ffn_full[:, :, 2 * quarter, :quarter].reshape(2 * units).astype(F32)
    pre_act = nt(hid_rows, w_up) + b_up
    normal_cdf = 0.5 * (1.0 + lax.erf(pre_act * 0.5**0.5))
    activated = pre_act * normal_cdf
    slope = normal_cdf + pre_act * jnp.exp(-0.5 * pre_act * pre_act) / math.sqrt(2.0 * math.pi)
    slope = jnp.where(jnp.abs(activated) <= act_scale[3], slope, 0.0)
    act_quant = jnp.clip(activated, -act_scale[3], act_scale[3]).astype(BF16)
    ffn_part = nn(act_quant, w_low)
    ffn_out = ffn_part[:HALF] + links.other_half(ffn_part[HALF:])
    final, normed_ffn, inverse_ffn = norm_forward(
        hidden + ffn_out + b_down.astype(F32), gain_second, shift_ffn.astype(F32)
    )
    layer_output = links.rows_home(final.astype(BF16))
    maxima = jnp.stack(
        [
            jnp.max(jnp.abs(x_full)),
            jnp.max(jnp.abs(context)),
            jnp.max(jnp.abs(hidden)),
            jnp.max(jnp.abs(activated)),
        ]
    )

    grad_gain_ffn = jnp.sum(upstream * normed_ffn, axis=0)
    grad_shift_ffn = jnp.sum(upstream, axis=0)
    grad_second = norm_backward(upstream, normed_ffn, inverse_ffn, gain_second)
    grad_b_down = jnp.sum(grad_second, axis=0)
    grad_final = grad_second.astype(BF16)
    grad_rows = jnp.concatenate([grad_final, links.other_half(grad_final)])
    grad_down = tn(act_quant, grad_rows)
    grad_pre = nt(grad_rows, w_low) * slope
    grad_b_in = jnp.sum(grad_pre, axis=0)
    grad_pre_b = grad_pre.astype(BF16)
    grad_in = tn(grad_pre_b, hid_rows)
    hid_part = nn(grad_pre_b, w_up)
    grad_hid = hid_part[:HALF] + links.other_half(hid_part[HALF:])
    ffn_grads = jnp.concatenate(
        [
            grad_in.astype(BF16).reshape(4, 4, quarter, width),
            grad_down.astype(BF16).reshape(4, 4, quarter, width),
            jnp.pad(
                grad_b_in.astype(BF16).reshape(4, 4, 1, quarter),
                ((0, 0), (0, 0), (0, 7), (0, width - quarter)),
            ),
        ],
        axis=2,
    )
    ffn_sums = links.reduce_all(ffn_grads)

    grad_hidden = grad_second + grad_hid * (jnp.abs(hidden) <= act_scale[2]).astype(F32)
    grad_gain_attn = jnp.sum(grad_hidden * normed_attn, axis=0)
    grad_shift_attn = jnp.sum(grad_hidden, axis=0)
    grad_first = norm_backward(grad_hidden, normed_attn, inverse_attn, gain_first)
    grad_b_out = jnp.sum(grad_first, axis=0)
    grad_attn = grad_first.astype(BF16)
    grad_attn_rows = jnp.concatenate([grad_attn, links.other_half(grad_attn)])
    sums, maxima = links.combine(
        jnp.stack(
            [
                grad_b_out,
                grad_gain_attn,
                grad_shift_attn,
                grad_b_down,
                grad_gain_ffn,
                grad_shift_ffn,
            ]
        ),
        maxima,
    )
    new_scale = DECAY * act_scale + (1.0 - DECAY) * maxima

    grad_out = tn(ctx_quant, grad_attn_rows)
    grad_context = nt(grad_attn_rows, w_back)
    grad_context = jnp.where(jnp.abs(context) <= act_scale[1], grad_context, 0.0).astype(BF16)
    inner = jnp.sum(
        (grad_context.astype(F32) * context).reshape(LEN, heads, 2, HEAD), axis=-1
    ).transpose(1, 2, 0)
    grad_q, grad_k, grad_v, proj_sums = attend_back(
        proj, grad_context, lse.transpose(0, 2, 1), inner, seg_col, seg_row, heads
    )
    grad_proj = jnp.concatenate([grad_q, grad_k, grad_v], axis=1)
    x_part = nn(grad_proj, w_proj)
    grad_x = x_part[:HALF] + links.other_half(x_part[HALF:])
    input_grad = grad_first + grad_x * (jnp.abs(x_full) <= act_scale[0]).astype(F32)
    input_grad = links.rows_home(input_grad.astype(BF16)).astype(F32)

    grad_w = jnp.concatenate([tn(grad_proj, x_rows), grad_out]).astype(BF16)
    grad_w = grad_w.reshape(4, 2, heads, 4, chunk, width).transpose(3, 1, 0, 2, 4, 5)
    grad_w = grad_w.reshape(4, 2, per, width)
    grad_b = jnp.stack([proj_sums[:, 0], proj_sums[:, 1]]).reshape(2, 2, heads, 4, chunk)
    grad_b = grad_b.transpose(3, 1, 0, 2, 4).reshape(4, 2, 1, per // 2).astype(BF16)
    grad_b = jnp.pad(grad_b, ((0, 0), (0, 0), (0, 7), (0, width - per // 2)))
    attn_sums = links.reduce_pair(jnp.concatenate([grad_w, grad_b], axis=2))

    attn_w = attn_sums[:, :per].reshape(4, 4, heads, chunk, width)
    attn_w = attn_w.transpose(1, 2, 0, 3, 4).reshape(4, local, width).astype(F32)
    grad_qkv = jnp.swapaxes(attn_w[:3], 1, 2)
    grad_bias_qv = (
        attn_sums[:, per, : per // 2]
        .reshape(4, 2, heads, chunk)
        .transpose(1, 2, 0, 3)
        .reshape(2, local)
        .astype(F32)
    )
    return (
        layer_output,
        input_grad,
        grad_qkv,
        grad_bias_qv,
        attn_w[3],
        sums[0],
        sums[1],
        sums[2],
        ffn_sums[:, :, :quarter].reshape(units, width).astype(F32).T,
        ffn_sums[:, :, 2 * quarter, :quarter].reshape(units).astype(F32),
        ffn_sums[:, :, quarter : 2 * quarter].reshape(units, width).astype(F32),
        sums[3],
        sums[4],
        sums[5],
        new_scale,
        maxima,
    )


def solution(mesh):
    in_specs = (
        P(("dp", "tensor"), None),
        P("dp"),
        P(None, None, "tensor"),
        P(None, "tensor"),
        P("tensor", None),
        P(),
        P(),
        P(),
        P(None, "tensor"),
        P("tensor"),
        P("tensor", None),
        P(),
        P(),
        P(),
        P(),
        P(("dp", "tensor"), None),
    )
    out_specs = (
        P(("dp", "tensor"), None),
        P(("dp", "tensor"), None),
        P(None, None, "tensor"),
        P(None, "tensor"),
        P("tensor", None),
        P(),
        P(),
        P(),
        P(None, "tensor"),
        P("tensor"),
        P("tensor", None),
        P(),
        P(),
        P(),
        P(),
        P(),
    )
    sizes = (mesh.shape["dp"], mesh.shape["tensor"])
    return jax.shard_map(
        functools.partial(on_device, sizes),
        mesh=mesh,
        in_specs=in_specs,
        out_specs=out_specs,
        check_vma=False,
    )
```

```python
import functools
import math

import jax
import jax.numpy as jnp
from jax import lax
from jax.experimental import pallas as pl
from jax.experimental.pallas import tpu as pltpu
from jax.sharding import PartitionSpec as P

HEAD = 64
LEN = 1024
HALF = LEN // 2
BLOCK = 256

EPSILON = 1e-12
DECAY = 0.9999
MASKED = -1e30
ORDER = (0, 1, 3, 2)
JOINT = ("dp", "tensor")
BF16 = jnp.bfloat16
F32 = jnp.float32


def norm_forward(resid, gain, shift):
    row_mean = jnp.mean(resid, axis=-1, keepdims=True)
    centred = resid - row_mean
    spread = jnp.mean(centred * centred, axis=-1, keepdims=True)
    inverse = lax.rsqrt(spread + EPSILON)
    normed = centred * inverse
    return (normed * gain + shift, normed, inverse)


def norm_backward(upstream, normed, inverse, gain):
    scaled = upstream * gain
    mean_first = jnp.mean(scaled, axis=-1, keepdims=True)
    mean_second = jnp.mean(scaled * normed, axis=-1, keepdims=True)
    return inverse * (scaled - mean_first - normed * mean_second)


def nt(a, b):
    return lax.dot_general(a, b, (((1,), (1,)), ((), ())), preferred_element_type=F32)


def nn(a, b):
    return lax.dot_general(a, b, (((1,), (0,)), ((), ())), preferred_element_type=F32)


def tn(a, b):
    return lax.dot_general(a, b, (((0,), (0,)), ((), ())), preferred_element_type=F32)


def attend_kernel(q_ref, k_ref, v_ref, seg_col_ref, seg_row_ref, ctx_ref, lse_ref):
    low = lax.broadcasted_iota(jnp.int32, (BLOCK, 2 * HEAD), 1) < HEAD
    keys = k_ref[...]
    values = v_ref[...]
    for block in range(LEN // BLOCK):
        rows = pl.ds(block * BLOCK, BLOCK)
        queries = q_ref[rows, :] * jnp.asarray(HEAD**-0.5, BF16)
        same = seg_col_ref[rows, :] == seg_row_ref[...]
        parts, logs = [], []
        for head in range(2):
            own = low if head == 0 else jnp.logical_not(low)
            scores = nt(jnp.where(own, queries, jnp.zeros_like(queries)), keys)
            scores = jnp.where(same, scores, MASKED)
            top = jnp.max(scores, axis=-1, keepdims=True)
            exponent = jnp.exp(scores - top)
            total = jnp.sum(exponent, axis=-1, keepdims=True)
            attention = (exponent * (1.0 / total)).astype(BF16)
            parts.append(nn(attention, values))
            logs.append(top + jnp.log(total))
        ctx_ref[rows, :] = jnp.where(low, parts[0], parts[1])
        lse_ref[0, :, rows] = jnp.transpose(jnp.concatenate(logs, axis=1))


def attend(proj, seg_col, seg_row, pairs_of_heads):
    n = pairs_of_heads
    return pl.pallas_call(
        attend_kernel,
        grid=(n,),
        in_specs=[
            pl.BlockSpec((LEN, 2 * HEAD), lambda i: (0, 3 * i)),
            pl.BlockSpec((LEN, 2 * HEAD), lambda i: (0, 3 * i + 1)),
            pl.BlockSpec((LEN, 2 * HEAD), lambda i: (0, 3 * i + 2)),
            pl.BlockSpec((LEN, 1), lambda i: (0, 0)),
            pl.BlockSpec((1, LEN), lambda i: (0, 0)),
        ],
        out_specs=[
            pl.BlockSpec((LEN, 2 * HEAD), lambda i: (0, i)),
            pl.BlockSpec((1, 2, LEN), lambda i: (i, 0, 0)),
        ],
        out_shape=[
            jax.ShapeDtypeStruct((LEN, n * 2 * HEAD), F32),
            jax.ShapeDtypeStruct((n, 2, LEN), F32),
        ],
        name="attend",
    )(proj, proj, proj, seg_col, seg_row)


def attend_back_kernel(
    q_ref,
    k_ref,
    v_ref,
    rows_ref,
    back_ref,
    ctx_ref,
    lse_ref,
    seg_col_ref,
    seg_row_ref,
    limit_ref,
    grad_ref,
    sum_ref,
    acc_ref,
    grads_ref,
    inner_ref,
):
    low = lax.broadcasted_iota(jnp.int32, (BLOCK, 2 * HEAD), 1) < HEAD
    for block in range(LEN // BLOCK):
        rows = pl.ds(block * BLOCK, BLOCK)
        context = ctx_ref[rows, :]
        grad = nt(rows_ref[rows, :], back_ref[...])
        grad = jnp.where(jnp.abs(context) <= limit_ref[0], grad, 0.0).astype(BF16)
        grads_ref[rows, :] = grad
        both = grad.astype(F32) * context
        inner = [
            jnp.sum(jnp.where(own, both, 0.0), axis=1, keepdims=True)
            for own in (low, jnp.logical_not(low))
        ]
        inner_ref[:, rows] = jnp.transpose(jnp.concatenate(inner, axis=1))
    queries = q_ref[...]
    grads = grads_ref[...]
    value_sum = jnp.zeros((1, 2 * HEAD), F32)
    for block in range(LEN // BLOCK):
        rows = pl.ds(block * BLOCK, BLOCK)
        keys = k_ref[rows, :]
        scaled_keys = keys * jnp.asarray(HEAD**-0.5, BF16)
        values = v_ref[rows, :]
        same = seg_col_ref[rows, :] == seg_row_ref[...]
        value_parts, key_parts = [], []
        for head in range(2):
            own = low if head == 0 else jnp.logical_not(low)
            zero = jnp.zeros_like(keys)
            scores = nt(jnp.where(own, scaled_keys, zero), queries)
            logs = lse_ref[0, head : head + 1, :]
            attention = jnp.where(same, jnp.exp(scores - logs), 0.0)
            value_parts.append(nn(attention.astype(BF16), grads))
            grad_attention = nt(jnp.where(own, values, zero), grads)
            inner = inner_ref[head : head + 1, :]
            grad_score = (attention * (grad_attention - inner) * HEAD**-0.5).astype(BF16)
            key_parts.append(nn(grad_score, queries))
            part = tn(grad_score, jnp.where(own, keys, zero))
            if block == 0 and head == 0:
                acc_ref[...] = part
            else:
                acc_ref[...] += part
        grad_value = jnp.where(low, value_parts[0], value_parts[1])
        value_sum += jnp.sum(grad_value, axis=0, keepdims=True)
        grad_ref[rows, 4 * HEAD :] = grad_value.astype(BF16)
        grad_ref[rows, 2 * HEAD : 4 * HEAD] = jnp.where(low, key_parts[0], key_parts[1]).astype(BF16)
    grad_query = acc_ref[...]
    grad_ref[:, : 2 * HEAD] = grad_query.astype(BF16)
    sum_ref[0, 0:1, :] = jnp.sum(grad_query, axis=0, keepdims=True)
    sum_ref[0, 1:2, :] = value_sum


def attend_back(proj, grad_rows, w_back, context, lse, seg_col, seg_row, limit, first, count):
    width = w_back.shape[1]
    return pl.pallas_call(
        attend_back_kernel,
        grid=(count,),
        in_specs=[
            pl.BlockSpec((LEN, 2 * HEAD), lambda i: (0, 3 * (first + i))),
            pl.BlockSpec((LEN, 2 * HEAD), lambda i: (0, 3 * (first + i) + 1)),
            pl.BlockSpec((LEN, 2 * HEAD), lambda i: (0, 3 * (first + i) + 2)),
            pl.BlockSpec((LEN, width), lambda i: (0, 0)),
            pl.BlockSpec((2 * HEAD, width), lambda i: (first + i, 0)),
            pl.BlockSpec((LEN, 2 * HEAD), lambda i: (0, first + i)),
            pl.BlockSpec((1, 2, LEN), lambda i: (first + i, 0, 0)),
            pl.BlockSpec((LEN, 1), lambda i: (0, 0)),
            pl.BlockSpec((1, LEN), lambda i: (0, 0)),
            pl.BlockSpec(memory_space=pltpu.SMEM),
        ],
        out_specs=[
            pl.BlockSpec((LEN, 6 * HEAD), lambda i: (0, i)),
            pl.BlockSpec((1, 2, 2 * HEAD), lambda i: (i, 0, 0)),
        ],
        out_shape=[
            jax.ShapeDtypeStruct((LEN, count * 6 * HEAD), BF16),
            jax.ShapeDtypeStruct((count, 2, 2 * HEAD), F32),
        ],
        scratch_shapes=[
            pltpu.VMEM((LEN, 2 * HEAD), F32),
            pltpu.VMEM((LEN, 2 * HEAD), BF16),
            pltpu.VMEM((2, LEN), F32),
        ],
        name="attend_back",
    )(proj, proj, proj, grad_rows, w_back, context, lse, seg_col, seg_row, limit)


class Links:
    def __init__(self, dp, depths):
        self.dp, self.depths = dp, depths
        self.planes = dp // 2
        place = lax.axis_index("dp")
        self.half, self.plane = place % 2, place // 2
        self.depth = lax.axis_index("tensor")
        self.square = self.planes == 4 and depths == 4

    def permute(self, array, move):
        pairs = []
        for place in range(self.dp):
            for depth in range(self.depths):
                to = move(place // 2, place % 2, depth)
                if to is not None:
                    plane, half, level = to
                    pairs.append(
                        (place * self.depths + depth, (2 * plane + half) * self.depths + level)
                    )
        return lax.ppermute(array, JOINT, pairs)

    def rows_home(self, array):
        return self.permute(
            array, lambda e, c, z: (e, z % 2, z - z % 2 + c) if c != z % 2 else None
        )

    def at_home(self, own, moved):
        return jnp.where(self.depth % 2 == self.half, own, moved)

    def other_half(self, array):
        return self.permute(array, lambda e, c, z: (e, 1 - c, z))

    def across(self, array, step, only=None):
        return self.permute(
            array,
            lambda e, c, z: (e ^ step, c, z) if only is None or only(c, z) else None,
        )

    def along(self, array, step):
        return self.permute(array, lambda e, c, z: (e, c, z ^ step))

    def spread_near(self, piece, only=None):
        return self.across(piece, 1, only), self.across(piece, 2, only)

    def spread_far(self, piece, near, only=None):
        first, second = near
        cut = piece.shape[-2] // 16 * 8
        third_low = self.across(second[..., :cut, :], 1, only)
        third_high = self.across(first[..., cut:, :], 2, only)
        return [piece, first, second, jnp.concatenate([third_low, third_high], axis=-2)]

    def spread(self, piece, only=None):
        return [piece] + [self.across(piece, step, only) for step in (1, 2, 3)]

    def in_order(self, pieces):
        stack = jnp.stack(pieces)
        return jnp.stack(
            [lax.dynamic_index_in_dim(stack, j ^ self.plane, 0, False) for j in range(4)]
        )

    @property
    def inside(self):
        return self.depth // 2 == self.half

    @property
    def even(self):
        return self.depth % 2 == 0

    def pair_near(self, array):
        return self.permute(array, lambda e, c, z: (e, c, z ^ 1) if z // 2 == c else None)

    def pair_out(self, array):
        return self.permute(array, lambda e, c, z: (e, c, z ^ 2) if z // 2 == c else None)

    def pair_back(self, array):
        return self.permute(array, lambda e, c, z: (e, c, z ^ 2) if z // 2 != c else None)

    def pair_cross(self, array):
        return self.permute(array, lambda e, c, z: (e, c, z ^ 3) if z // 2 != c else None)

    def halves_in_order(self, mine):
        other = self.other_half(mine)
        first = self.half == 0
        return jnp.stack([jnp.where(first, mine, other), jnp.where(first, other, mine)])

    def even_first(self, mine, other):
        return jnp.stack([jnp.where(self.even, mine, other), jnp.where(self.even, other, mine)])


def exact_parts(values):
    high = lax.reduce_precision(values, 8, 7)
    rest = values - high
    middle = lax.reduce_precision(rest, 8, 7)
    return jnp.concatenate([high, middle, rest - middle]).astype(BF16)


def exact_sum(parts):
    rows = parts.shape[0] // 3
    parts = parts.astype(F32)
    return parts[:rows] + parts[rows : 2 * rows] + parts[2 * rows :]


def merge(both, other):
    last = lax.broadcasted_iota(jnp.int32, both.shape, 0) == 6
    return jnp.where(last, jnp.maximum(both, other), both + other)


def sync(*values):
    return lax.optimization_barrier(values)


def plain_all(links, grads):
    blank = jnp.zeros((4, 2) + grads.shape[1:], F32)
    full = lax.dynamic_update_slice_in_dim(blank, grads[:, None].astype(F32), links.half, 1)
    shard = lax.psum_scatter(full, "tensor", scatter_dimension=0, tiled=False)
    return lax.psum(shard, "dp")


def plain_pair(links, grads):
    blank = jnp.zeros((4,) + grads.shape[:1] + grads.shape[2:], F32)
    own = grads.swapaxes(0, 1).astype(F32)
    full = lax.dynamic_update_slice_in_dim(blank, own, 2 * links.half, 0)
    shard = lax.psum_scatter(full, "tensor", scatter_dimension=0, tiled=False)
    return lax.psum(shard, "dp")


def on_device(
    sizes,
    layer_input,
    segments,
    w_qkv,
    bias_qv,
    w_out,
    b_out,
    gain_attn,
    shift_attn,
    w_in,
    b_in,
    w_down,
    b_down,
    gain_ffn,
    shift_ffn,
    act_scale,
    out_grad,
):
    links = Links(*sizes)
    width = layer_input.shape[1]
    local = w_qkv.shape[2]
    heads = local // HEAD
    chunk = HEAD // 4
    units = w_in.shape[1]
    quarter = units // 8
    gain_first = gain_attn.astype(F32)
    gain_second = gain_ffn.astype(F32)

    per = 3 * heads * chunk
    more = heads * chunk

    rows = jnp.concatenate([jnp.swapaxes(w_qkv, 1, 2), w_out[None]])
    rows = rows.reshape(4, heads, 4, chunk, width)
    rows = rows.transpose(2, 0, 1, 3, 4).reshape(4, per + more, width)
    tail = bias_qv.reshape(2, heads, 4, chunk).transpose(2, 0, 1, 3).reshape(4, 1, 2 * more)
    tail = jnp.pad(tail, ((0, 0), (0, 7), (0, width - tail.shape[2])))
    attn_pack = jnp.concatenate([rows, tail], axis=1)
    if links.square:
        attn_mine = lax.dynamic_index_in_dim(attn_pack, links.plane, 0, False)
        attn_next = links.pair_near(attn_mine)
    x_home = links.at_home(layer_input, links.rows_home(layer_input))
    seg_rows = segments.reshape(2, LEN)
    seg_mine = lax.dynamic_index_in_dim(seg_rows, links.depth // 2, 0, False).reshape(8, LEN // 8)
    seg_next = links.other_half(seg_mine)
    seg_home = links.at_home(seg_mine, seg_next).reshape(2, HALF)
    seg_home = jnp.where(links.half == 0, seg_home, seg_home[::-1]).reshape(LEN)
    seg_col, seg_row = seg_home[:, None], seg_home[None, :]
    ffn_half = jnp.concatenate(
        [
            lax.dynamic_index_in_dim(w_in.T.reshape(2, 4, quarter, width), links.half, 0, False),
            lax.dynamic_index_in_dim(w_down.reshape(2, 4, quarter, width), links.half, 0, False),
            jnp.pad(
                lax.dynamic_index_in_dim(b_in.reshape(2, 4, 1, quarter), links.half, 0, False),
                ((0, 0), (0, 7), (0, width - quarter)),
            ),
        ],
        axis=1,
    )
    if links.square:
        ffn_own = jnp.stack(
            [lax.dynamic_index_in_dim(ffn_half, j ^ links.plane, 0, False) for j in ORDER]
        )
        ffn_one = links.along(ffn_own[0], 1)
        attn_both = links.even_first(attn_mine, attn_next)
        attn_far = links.pair_out(attn_both)
        attn_far, ffn_one, ffn_mine = sync(attn_far, ffn_one, ffn_own[0])
        attn_both = jnp.where(links.inside, attn_both, attn_far)
        attn_near = links.spread_near(attn_both)
        ffn_two = links.along(ffn_mine, 2)
        attn_near, ffn_two, ffn_mine = sync(attn_near, ffn_two, ffn_mine)
        ffn_three = links.along(ffn_mine, 3)
        attn_full = links.spread_far(attn_both, attn_near)
        attn_full, ffn_three = sync(attn_full, ffn_three)
        attn_full = jnp.stack(attn_full)
        ffn_in = jnp.stack([ffn_one, ffn_two, ffn_three])
    else:
        attn_full = lax.all_gather(attn_pack, "tensor", axis=0, tiled=False)
        attn_full = lax.dynamic_slice_in_dim(attn_full, 2 * links.half, 2, 0).swapaxes(0, 1)
        ffn_in = lax.all_gather(ffn_half, "tensor", axis=0, tiled=False)

    x_full = x_home.astype(F32)
    x_quant = jnp.clip(x_full, -act_scale[0], act_scale[0]).astype(BF16)
    x_rows = jnp.concatenate([x_quant, links.other_half(x_quant)])

    weights = attn_full[:, :, : per + more].reshape(4, 2, 4, heads, chunk, width)
    weights = weights.transpose(2, 1, 3, 0, 4, 5).reshape(4, heads, 2 * HEAD, width)
    w_proj = weights[:3].swapaxes(0, 1).reshape(6 * local, width)
    w_back = weights[3].reshape(2 * local, width)
    biases = attn_full[:, :, per + more, : 2 * more].reshape(4, 2, 2, heads, chunk)
    biases = biases.transpose(2, 1, 3, 0, 4).reshape(2, 2 * local).astype(F32)
    bias_all = jnp.stack([biases[0], jnp.zeros_like(biases[0]), biases[1]])
    bias_all = bias_all.reshape(3, heads, 2 * HEAD).swapaxes(0, 1).reshape(6 * local)

    proj = (nt(x_rows, w_proj) + bias_all).astype(BF16)
    proj, ffn_in, out_grad = sync(proj, ffn_in, out_grad)
    if links.square:
        ffn_near = links.spread_near(ffn_in)
    upstream = links.rows_home(out_grad)
    context, lse = attend(proj, seg_col, seg_row, heads)
    context, upstream = sync(context, upstream)
    upstream = links.at_home(out_grad, upstream).astype(F32)
    ctx_quant = jnp.clip(context, -act_scale[1], act_scale[1]).astype(BF16)
    attn_part = nn(ctx_quant, w_back)
    if links.square:
        attn_part, ffn_near = sync(attn_part, ffn_near)
        pieces = links.spread_far(ffn_in, ffn_near)
        ffn_full = jnp.stack(
            [jnp.concatenate([ffn_own[i][None], pieces[j]]) for i, j in enumerate(ORDER)]
        )
    else:
        ffn_full = ffn_in.swapaxes(0, 1)
    attn_out = attn_part[:HALF] + links.other_half(attn_part[HALF:]) + b_out.astype(F32)
    hidden, normed_attn, inverse_attn = norm_forward(
        x_full + attn_out, gain_first, shift_attn.astype(F32)
    )
    hid_quant = jnp.clip(hidden, -act_scale[2], act_scale[2]).astype(BF16)
    hid_rows = jnp.concatenate([hid_quant, links.other_half(hid_quant)])

    w_up = ffn_full[:, :, :quarter].reshape(2 * units, width)
    w_low = ffn_full[:, :, quarter : 2 * quarter].reshape(2 * units, width)
    b_up = ffn_full[:, :, 2 * quarter, :quarter].reshape(2 * units).astype(F32)
    pre_act = nt(hid_rows, w_up) + b_up
    normal_cdf = 0.5 * (1.0 + lax.erf(pre_act * 0.5**0.5))
    activated = pre_act * normal_cdf
    slope = normal_cdf + pre_act * jnp.exp(-0.5 * pre_act * pre_act) / math.sqrt(2.0 * math.pi)
    slope = jnp.where(jnp.abs(activated) <= act_scale[3], slope, 0.0)
    act_quant = jnp.clip(activated, -act_scale[3], act_scale[3]).astype(BF16)
    ffn_part = nn(act_quant, w_low)
    ffn_out = ffn_part[:HALF] + links.other_half(ffn_part[HALF:])
    final, normed_ffn, inverse_ffn = norm_forward(
        hidden + ffn_out + b_down.astype(F32), gain_second, shift_ffn.astype(F32)
    )
    final = final.astype(BF16)
    layer_output = links.rows_home(final)
    maxima = jnp.stack(
        [
            jnp.max(jnp.abs(x_full)),
            jnp.max(jnp.abs(context)),
            jnp.max(jnp.abs(hidden)),
            jnp.max(jnp.max(jnp.abs(activated), axis=0)),
        ]
    )

    grad_gain_ffn = jnp.sum(upstream * normed_ffn, axis=0)
    grad_shift_ffn = jnp.sum(upstream, axis=0)
    grad_second = norm_backward(upstream, normed_ffn, inverse_ffn, gain_second)
    grad_b_down = jnp.sum(grad_second, axis=0)
    grad_final = grad_second.astype(BF16)
    grad_rows = jnp.concatenate([grad_final, links.other_half(grad_final)])
    down = tn(act_quant, grad_rows).astype(BF16).reshape(4, 4, quarter, width)
    grad_pre = nt(grad_rows, w_low) * slope
    grad_b_in = jnp.sum(grad_pre, axis=0)
    grad_pre_b = grad_pre.astype(BF16)
    up = tn(grad_pre_b, hid_rows).astype(BF16).reshape(4, 4, quarter, width)
    tail = jnp.pad(
        grad_b_in.astype(BF16).reshape(4, 4, 1, quarter),
        ((0, 0), (0, 0), (0, 7), (0, width - quarter)),
    )
    ffn_grads = jnp.concatenate([up, down, tail], axis=2)
    if links.square:
        ffn_grads, grad_pre_b = sync(ffn_grads, grad_pre_b)
        ffn_x = links.across(ffn_grads[1:3, :2], 1)
        ffn_y = links.across(ffn_grads[2:4, 2:], 2)
    hid_part = nn(grad_pre_b, w_up)
    grad_hid = hid_part[:HALF] + links.other_half(hid_part[HALF:])

    grad_hidden = grad_second + grad_hid * (jnp.abs(hidden) <= act_scale[2]).astype(F32)
    grad_gain_attn = jnp.sum(grad_hidden * normed_attn, axis=0)
    grad_shift_attn = jnp.sum(grad_hidden, axis=0)
    grad_first = norm_backward(grad_hidden, normed_attn, inverse_attn, gain_first)
    grad_b_out = jnp.sum(grad_first, axis=0)
    grad_attn = grad_first.astype(BF16)
    grad_attn_rows = jnp.concatenate([grad_attn, links.other_half(grad_attn)])
    sums = [grad_b_out, grad_gain_attn, grad_shift_attn, grad_b_down, grad_gain_ffn, grad_shift_ffn]
    sums = jnp.stack([*sums, jnp.pad(maxima, (0, width - 4)), jnp.zeros(width)])

    out = tn(ctx_quant, grad_attn_rows).astype(BF16).reshape(2, heads, 4, chunk, width)
    out = out.transpose(2, 0, 1, 3, 4).reshape(4, 2, more, width)
    limit = act_scale[1:2]

    def back(first, count):
        return attend_back(
            proj, grad_attn_rows, w_back, context, lse, seg_col, seg_row, limit, first, count
        )

    if links.square:
        early, early_sums = back(0, 1)
        sums = merge(sums, links.other_half(sums))
        early, grad_attn_rows, ffn_x, ffn_y, layer_output, sums = sync(
            early, grad_attn_rows, ffn_x, ffn_y, layer_output, sums
        )
        low = [ffn_grads[0, :2] + ffn_x[0].astype(F32), ffn_grads[3, :2] + ffn_x[1].astype(F32)]
        high = [ffn_grads[0, 2:] + ffn_y[1].astype(F32), ffn_grads[1, 2:] + ffn_y[0].astype(F32)]
        ffn_y = links.across(low[1].astype(BF16), 2)
        ffn_x = links.across(high[1].astype(BF16), 1)
        early_w = tn(early, x_rows).astype(BF16)
        late, late_sums = back(1, heads - 1)
        late, ffn_x, ffn_y = sync(late, ffn_x, ffn_y)
        ffn_low = low[0] + ffn_y.astype(F32)
        ffn_in = links.along((high[0] + ffn_x.astype(F32)).astype(BF16), 2)
        grad_w = jnp.concatenate([early_w, tn(late, x_rows).astype(BF16)])
        proj_sums = jnp.concatenate([early_sums, late_sums])
    else:
        late, proj_sums = back(0, heads)
        grad_w = tn(late, x_rows).astype(BF16)
    grad_w = grad_w.reshape(heads, 3, 2, 4, chunk, width).transpose(1, 0, 2, 3, 4, 5)
    grad_w = grad_w.reshape(3, 2, heads, 4, chunk, width).transpose(3, 1, 0, 2, 4, 5)
    grad_w = grad_w.reshape(4, 2, per, width)
    grad_b = jnp.stack([proj_sums[:, 0], proj_sums[:, 1]]).reshape(2, 2, heads, 4, chunk)
    grad_b = grad_b.transpose(3, 1, 0, 2, 4).reshape(4, 2, 1, 2 * more).astype(BF16)
    grad_b = jnp.pad(grad_b, ((0, 0), (0, 0), (0, 7), (0, width - 2 * more)))
    grad_w = jnp.concatenate([grad_w, out, grad_b], axis=2)
    if links.square:
        grad_w, late = sync(grad_w, late)
        tall = grad_w.shape[2]
        grad_w = grad_w.reshape(4, 2 * tall, width)
        sums_sent = exact_parts(sums)
        proj_in = [
            links.across(jnp.concatenate([grad_w[step], sums_sent]), step) for step in (1, 2, 3)
        ]
        x_part = nn(early, w_proj[: 6 * HEAD]) + nn(late, w_proj[6 * HEAD :])
    else:
        x_part = nn(late, w_proj)
    grad_x = x_part[:HALF] + links.other_half(x_part[HALF:])
    input_grad = grad_first + grad_x * (jnp.abs(x_full) <= act_scale[0]).astype(F32)
    input_grad = input_grad.astype(BF16)
    input_grad = links.at_home(input_grad, links.rows_home(input_grad)).astype(F32)

    if links.square:
        proj_in, x_part = sync(proj_in, x_part)
        total = grad_w[0].astype(F32)
        for part in proj_in:
            total = total + part[: 2 * tall].astype(F32)
            sums = merge(sums, exact_sum(part[2 * tall :]))
        mine = jnp.where(links.even, total[:tall], total[tall:])
        other = jnp.where(links.even, total[tall:], total[:tall])
        sums_sent = exact_parts(sums)
        other = jnp.concatenate([other.astype(BF16), sums_sent])
        proj_in = [
            links.pair_near(other),
            links.pair_back(jnp.concatenate([mine.astype(BF16), sums_sent])),
            links.pair_cross(other),
        ]
        ffn_in, total = sync(ffn_in, total)
        ffn_low = ffn_low + ffn_in.astype(F32)
        ffn_in = links.along(ffn_low[1].astype(BF16), 1)
        for part in proj_in:
            mine = mine + part[:tall].astype(F32)
            sums = merge(sums, exact_sum(part[tall:]))
        proj_all = links.spread(mine.astype(BF16), lambda c, z: z // 2 == c)
        ffn_mine = (ffn_low[0] + ffn_in.astype(F32)).astype(BF16)
        ffn_all = links.spread(ffn_mine)
        proj_all, ffn_all = sync(proj_all, ffn_all)
        proj_all = jnp.concatenate([*proj_all, exact_parts(sums)])
        proj_all = jnp.where(links.inside, proj_all, links.other_half(proj_all))
        ffn_all = links.halves_in_order(links.in_order(ffn_all))
        sums = exact_sum(proj_all[4 * tall :])
        proj_grads = links.in_order(list(proj_all[: 4 * tall].reshape(4, tall, width)))
    else:
        ffn_all = plain_all(links, ffn_grads.swapaxes(0, 1))
        proj_grads = plain_pair(links, grad_w)
        sums = jnp.concatenate([lax.psum(sums[:6], JOINT), lax.pmax(sums[6:], JOINT)])
    maxima = sums[6, :4]
    new_scale = DECAY * act_scale + (1.0 - DECAY) * maxima

    up_grads, down_grads = ffn_all[:, :, :quarter], ffn_all[:, :, quarter : 2 * quarter]
    out_grads = proj_grads[:, per : per + more]
    grad_qkv = proj_grads[:, :per].reshape(4, 3, heads, chunk, width)
    grad_qkv = grad_qkv.transpose(1, 4, 2, 0, 3).reshape(3, width, local).astype(F32)
    grad_bias_qv = (
        proj_grads[:, per + more, : 2 * more]
        .reshape(4, 2, heads, chunk)
        .transpose(1, 2, 0, 3)
        .reshape(2, local)
        .astype(F32)
    )
    grad_out = out_grads.reshape(4, heads, chunk, width).transpose(1, 0, 2, 3)
    return (
        links.at_home(final, layer_output),
        input_grad,
        grad_qkv,
        grad_bias_qv,
        grad_out.reshape(local, width).astype(F32),
        sums[0],
        sums[1],
        sums[2],
        up_grads.reshape(units, width).astype(F32).T,
        ffn_all[:, :, 2 * quarter, :quarter].reshape(units).astype(F32),
        down_grads.reshape(units, width).astype(F32),
        sums[3],
        sums[4],
        sums[5],
        new_scale,
        maxima,
    )


def solution(mesh):
    in_specs = (
        P(("dp", "tensor"), None),
        P("dp"),
        P(None, None, "tensor"),
        P(None, "tensor"),
        P("tensor", None),
        P(),
        P(),
        P(),
        P(None, "tensor"),
        P("tensor"),
        P("tensor", None),
        P(),
        P(),
        P(),
        P(),
        P(("dp", "tensor"), None),
    )
    out_specs = (
        P(("dp", "tensor"), None),
        P(("dp", "tensor"), None),
        P(None, None, "tensor"),
        P(None, "tensor"),
        P("tensor", None),
        P(),
        P(),
        P(),
        P(None, "tensor"),
        P("tensor"),
        P("tensor", None),
        P(),
        P(),
        P(),
        P(),
        P(),
    )
    sizes = (mesh.shape["dp"], mesh.shape["tensor"])
    return jax.shard_map(
        functools.partial(on_device, sizes),
        mesh=mesh,
        in_specs=in_specs,
        out_specs=out_specs,
        check_vma=False,
    )
```

```python
import functools
import math

import jax
import jax.numpy as jnp
from jax import lax
from jax.experimental import pallas as pl
from jax.experimental.pallas import tpu as pltpu
from jax.sharding import PartitionSpec as P

HEAD = 64
LEN = 1024
HALF = LEN // 2
BLOCK = 256

EPSILON = 1e-12
DECAY = 0.9999
MASKED = -1e30
ORDER = (0, 1, 3, 2)
JOINT = ("dp", "tensor")
BF16 = jnp.bfloat16
F32 = jnp.float32


def norm_forward(resid, gain, shift):
    row_mean = jnp.mean(resid, axis=-1, keepdims=True)
    centred = resid - row_mean
    spread = jnp.mean(centred * centred, axis=-1, keepdims=True)
    inverse = lax.rsqrt(spread + EPSILON)
    normed = centred * inverse
    return (normed * gain + shift, normed, inverse)


def norm_backward(upstream, normed, inverse, gain):
    scaled = upstream * gain
    mean_first = jnp.mean(scaled, axis=-1, keepdims=True)
    mean_second = jnp.mean(scaled * normed, axis=-1, keepdims=True)
    return inverse * (scaled - mean_first - normed * mean_second)


def nt(a, b):
    return lax.dot_general(a, b, (((1,), (1,)), ((), ())), preferred_element_type=F32)


def nn(a, b):
    return lax.dot_general(a, b, (((1,), (0,)), ((), ())), preferred_element_type=F32)


def tn(a, b):
    return lax.dot_general(a, b, (((0,), (0,)), ((), ())), preferred_element_type=F32)


def attend_kernel(q_ref, k_ref, v_ref, seg_col_ref, seg_row_ref, ctx_ref, lse_ref):
    low = lax.broadcasted_iota(jnp.int32, (BLOCK, 2 * HEAD), 1) < HEAD
    keys = k_ref[...]
    values = v_ref[...]
    for block in range(LEN // BLOCK):
        rows = pl.ds(block * BLOCK, BLOCK)
        queries = q_ref[rows, :] * jnp.asarray(HEAD**-0.5, BF16)
        same = seg_col_ref[rows, :] == seg_row_ref[...]
        parts, logs = [], []
        for head in range(2):
            own = low if head == 0 else jnp.logical_not(low)
            scores = nt(jnp.where(own, queries, jnp.zeros_like(queries)), keys)
            scores = jnp.where(same, scores, MASKED)
            top = jnp.max(scores, axis=-1, keepdims=True)
            exponent = jnp.exp(scores - top)
            total = jnp.sum(exponent, axis=-1, keepdims=True)
            attention = (exponent * (1.0 / total)).astype(BF16)
            parts.append(nn(attention, values))
            logs.append(top + jnp.log(total))
        ctx_ref[rows, :] = jnp.where(low, parts[0], parts[1])
        lse_ref[0, :, rows] = jnp.transpose(jnp.concatenate(logs, axis=1))


def attention_cost(pairs_of_heads, products):
    scores = 2 * pairs_of_heads * LEN * LEN
    return pl.CostEstimate(
        flops=2 * 4 * HEAD * products * scores,
        transcendentals=scores,
        bytes_accessed=8 * pairs_of_heads * LEN * HEAD * products,
    )


def attend(proj, seg_col, seg_row, pairs_of_heads):
    n = pairs_of_heads
    return pl.pallas_call(
        attend_kernel,
        grid=(n,),
        in_specs=[
            pl.BlockSpec((LEN, 2 * HEAD), lambda i: (0, 3 * i)),
            pl.BlockSpec((LEN, 2 * HEAD), lambda i: (0, 3 * i + 1)),
            pl.BlockSpec((LEN, 2 * HEAD), lambda i: (0, 3 * i + 2)),
            pl.BlockSpec((LEN, 1), lambda i: (0, 0)),
            pl.BlockSpec((1, LEN), lambda i: (0, 0)),
        ],
        out_specs=[
            pl.BlockSpec((LEN, 2 * HEAD), lambda i: (0, i)),
            pl.BlockSpec((1, 2, LEN), lambda i: (i, 0, 0)),
        ],
        out_shape=[
            jax.ShapeDtypeStruct((LEN, n * 2 * HEAD), F32),
            jax.ShapeDtypeStruct((n, 2, LEN), F32),
        ],
        name="attend",
    )(proj, proj, proj, seg_col, seg_row)


def attend_back_kernel(
    q_ref,
    k_ref,
    v_ref,
    go_ref,
    go_other_ref,
    x_ref,
    x_other_ref,
    back_ref,
    ctx_ref,
    lse_ref,
    seg_col_ref,
    seg_row_ref,
    limit_ref,
    grad_ref,
    pack_ref,
    sum_ref,
    acc_ref,
    grads_ref,
    quant_ref,
    inner_ref,
):
    low = lax.broadcasted_iota(jnp.int32, (BLOCK, 2 * HEAD), 1) < HEAD
    limit = limit_ref[0]
    for half, rows_ref in enumerate((go_ref, go_other_ref)):
        for block in range(HALF // BLOCK):
            rows = pl.ds(half * HALF + block * BLOCK, BLOCK)
            context = ctx_ref[rows, :]
            quant_ref[rows, :] = jnp.clip(context, -limit, limit).astype(BF16)
            grad = nt(rows_ref[pl.ds(block * BLOCK, BLOCK), :], back_ref[...])
            grad = jnp.where(jnp.abs(context) <= limit, grad, 0.0).astype(BF16)
            grads_ref[rows, :] = grad
            both = grad.astype(F32) * context
            inner = [
                jnp.sum(jnp.where(own, both, 0.0), axis=1, keepdims=True)
                for own in (low, jnp.logical_not(low))
            ]
            inner_ref[:, rows] = jnp.transpose(jnp.concatenate(inner, axis=1))
    queries = q_ref[...]
    grads = grads_ref[...]
    value_sum = jnp.zeros((1, 2 * HEAD), F32)
    for block in range(LEN // BLOCK):
        rows = pl.ds(block * BLOCK, BLOCK)
        keys = k_ref[rows, :]
        scaled_keys = keys * jnp.asarray(HEAD**-0.5, BF16)
        values = v_ref[rows, :]
        same = seg_col_ref[rows, :] == seg_row_ref[...]
        value_parts, key_parts = [], []
        for head in range(2):
            own = low if head == 0 else jnp.logical_not(low)
            zero = jnp.zeros_like(keys)
            scores = nt(jnp.where(own, scaled_keys, zero), queries)
            logs = lse_ref[0, head : head + 1, :]
            attention = jnp.where(same, jnp.exp(scores - logs), 0.0)
            value_parts.append(nn(attention.astype(BF16), grads))
            grad_attention = nt(jnp.where(own, values, zero), grads)
            inner = inner_ref[head : head + 1, :]
            grad_score = (attention * (grad_attention - inner) * HEAD**-0.5).astype(BF16)
            key_parts.append(nn(grad_score, queries))
            part = tn(grad_score, jnp.where(own, keys, zero))
            if block == 0 and head == 0:
                acc_ref[...] = part
            else:
                acc_ref[...] += part
        grad_value = jnp.where(low, value_parts[0], value_parts[1])
        value_sum += jnp.sum(grad_value, axis=0, keepdims=True)
        grad_ref[rows, 4 * HEAD :] = grad_value.astype(BF16)
        grad_ref[rows, 2 * HEAD : 4 * HEAD] = jnp.where(low, key_parts[0], key_parts[1]).astype(BF16)
    grad_query = acc_ref[...]
    grad_ref[:, : 2 * HEAD] = grad_query.astype(BF16)
    sum_ref[0, 0:1, :] = jnp.sum(grad_query, axis=0, keepdims=True)
    sum_ref[0, 1:2, :] = value_sum
    chunk = HEAD // 4
    sides = ((slice(0, HALF), x_ref, go_ref), (slice(HALF, LEN), x_other_ref, go_other_ref))
    for kind in range(4):
        lanes = slice(2 * kind * HEAD, 2 * (kind + 1) * HEAD)
        total = None
        for rows, x_side, go_side in sides:
            if kind < 3:
                part = tn(grad_ref[rows, lanes], x_side[...])
            else:
                part = tn(quant_ref[rows, :], go_side[...])
            total = part if total is None else total + part
        total = total.astype(BF16)
        for head in range(2):
            for j in range(4):
                at = head * HEAD + j * chunk
                into = (head * 4 + kind) * chunk
                pack_ref[j, into : into + chunk, :] = total[at : at + chunk, :]


def attend_back(
    first, n, before, proj, go, go_other, x, x_other, w_back, context, lse, seg_col, seg_row, limit
):
    width = w_back.shape[1]
    earlier = [] if before is None else [before]

    def body(*refs):
        attend_back_kernel(*refs[:13], *refs[13 + len(earlier) :])

    def whole(array):
        return pl.BlockSpec(array.shape, lambda i: (0,) * array.ndim)

    return pl.pallas_call(
        body,
        grid=(n,),
        in_specs=[
            pl.BlockSpec((LEN, 2 * HEAD), lambda i: (0, 3 * (first + i))),
            pl.BlockSpec((LEN, 2 * HEAD), lambda i: (0, 3 * (first + i) + 1)),
            pl.BlockSpec((LEN, 2 * HEAD), lambda i: (0, 3 * (first + i) + 2)),
            *[whole(array) for array in (go, go_other, x, x_other)],
            pl.BlockSpec((2 * HEAD, width), lambda i: (first + i, 0)),
            pl.BlockSpec((LEN, 2 * HEAD), lambda i: (0, first + i)),
            pl.BlockSpec((1, 2, LEN), lambda i: (first + i, 0, 0)),
            whole(seg_col),
            whole(seg_row),
            pl.BlockSpec(memory_space=pltpu.SMEM),
            *[pl.BlockSpec(memory_space=pl.ANY) for _ in earlier],
        ],
        out_specs=[
            pl.BlockSpec((LEN, 6 * HEAD), lambda i: (0, i)),
            pl.BlockSpec((4, 2 * HEAD, width), lambda i: (0, first + i, 0)),
            pl.BlockSpec((1, 2, 2 * HEAD), lambda i: (i, 0, 0)),
        ],
        out_shape=[
            jax.ShapeDtypeStruct((LEN, n * 6 * HEAD), BF16),
            jax.ShapeDtypeStruct((4, *w_back.shape), BF16),
            jax.ShapeDtypeStruct((n, 2, 2 * HEAD), F32),
        ],
        scratch_shapes=[
            pltpu.VMEM((LEN, 2 * HEAD), F32),
            pltpu.VMEM((LEN, 2 * HEAD), BF16),
            pltpu.VMEM((LEN, 2 * HEAD), BF16),
            pltpu.VMEM((2, LEN), F32),
        ],
        cost_estimate=attention_cost(n, 9) if first else None,
        input_output_aliases={13: 1} if earlier else {},
        name="attend_back",
    )(
        *(proj, proj, proj, go, go_other, x, x_other, w_back, context, lse),
        *(seg_col, seg_row, limit, *earlier),
    )


def unpack_kernel(where_ref, own_ref, other_ref, qkv_ref, out_ref):
    inside, plane = where_ref[0], where_ref[1]
    kind = pl.program_id(0)
    chunk = HEAD // 4
    tall = own_ref.shape[0] // 4
    heads = tall // HEAD

    def rows_of(ref):
        parts = []
        for head in range(heads):
            for j in range(4):
                at = (j ^ plane) * tall + head * HEAD + kind * chunk
                parts.append(ref[pl.ds(pl.multiple_of(at, chunk), chunk), :])
        return jnp.concatenate(parts, axis=0).astype(F32)

    for flag, ref in ((1, own_ref), (0, other_ref)):

        @pl.when(jnp.logical_and(inside == flag, kind < 3))
        def _(ref=ref):
            qkv_ref[0] = rows_of(ref)

        @pl.when(jnp.logical_and(inside == flag, kind == 3))
        def _(ref=ref):
            out_ref[...] = rows_of(ref)


def unpack(inside, plane, own, other, tall):
    width = own.shape[1]
    return pl.pallas_call(
        unpack_kernel,
        grid=(4,),
        in_specs=[
            pl.BlockSpec(memory_space=pltpu.SMEM),
            pl.BlockSpec((4 * tall, width), lambda i: (0, 0)),
            pl.BlockSpec((4 * tall, width), lambda i: (0, 0)),
        ],
        out_specs=[
            pl.BlockSpec((1, tall, width), lambda i: (jnp.minimum(i, 2), 0, 0)),
            pl.BlockSpec((tall, width), lambda i: (0, 0)),
        ],
        out_shape=[
            jax.ShapeDtypeStruct((3, tall, width), F32),
            jax.ShapeDtypeStruct((tall, width), F32),
        ],
        name="unpack",
    )(jnp.stack([inside.astype(jnp.int32), plane]), own, other)


class Links:
    def __init__(self, dp, depths):
        self.dp, self.depths = dp, depths
        self.planes = dp // 2
        place = lax.axis_index("dp")
        self.half, self.plane = place % 2, place // 2
        self.depth = lax.axis_index("tensor")
        self.square = self.planes == 4 and depths == 4

    def permute(self, array, move):
        pairs = []
        for place in range(self.dp):
            for depth in range(self.depths):
                to = move(place // 2, place % 2, depth)
                if to is not None:
                    plane, half, level = to
                    pairs.append(
                        (place * self.depths + depth, (2 * plane + half) * self.depths + level)
                    )
        return lax.ppermute(array, JOINT, pairs)

    def rows_home(self, array):
        return self.permute(
            array, lambda e, c, z: (e, z % 2, z - z % 2 + c) if c != z % 2 else None
        )

    def at_home(self, own, moved):
        return jnp.where(self.depth % 2 == self.half, own, moved)

    def other_half(self, array):
        return self.permute(array, lambda e, c, z: (e, 1 - c, z))

    def across(self, array, step, only=None):
        return self.permute(
            array,
            lambda e, c, z: (e ^ step, c, z) if only is None or only(c, z) else None,
        )

    def along(self, array, step):
        return self.permute(array, lambda e, c, z: (e, c, z ^ step))

    def spread_near(self, piece, only=None):
        return self.across(piece, 1, only), self.across(piece, 2, only)

    def spread_far(self, piece, near, only=None):
        first, second = near
        cut = piece.shape[-2] // 16 * 8
        third_low = self.across(second[..., :cut, :], 1, only)
        third_high = self.across(first[..., cut:, :], 2, only)
        return [piece, first, second, jnp.concatenate([third_low, third_high], axis=-2)]

    def spread(self, piece, only=None):
        return [piece] + [self.across(piece, step, only) for step in (1, 2, 3)]

    def in_order(self, pieces):
        stack = jnp.stack(pieces)
        return jnp.stack(
            [lax.dynamic_index_in_dim(stack, j ^ self.plane, 0, False) for j in range(4)]
        )

    @property
    def inside(self):
        return self.depth // 2 == self.half

    @property
    def even(self):
        return self.depth % 2 == 0

    def pair_near(self, array):
        return self.permute(array, lambda e, c, z: (e, c, z ^ 1) if z // 2 == c else None)

    def pair_out(self, array):
        def far(step):
            return lambda e, c, z: (e, c, z ^ step) if z // 2 == c else None

        return [self.permute(array, far(step)) for step in (2, 3, 1)]

    def pair_of(self, mine, arrived):
        same, cross, near = arrived
        a = jnp.where(self.inside, mine, same)
        b = jnp.where(self.inside, near, cross)
        return self.even_first(a, b)

    def pair_back(self, array):
        return self.permute(array, lambda e, c, z: (e, c, z ^ 2) if z // 2 != c else None)

    def pair_cross(self, array):
        return self.permute(array, lambda e, c, z: (e, c, z ^ 3) if z // 2 != c else None)

    def halves_in_order(self, mine):
        other = self.other_half(mine)
        first = self.half == 0
        return jnp.stack([jnp.where(first, mine, other), jnp.where(first, other, mine)])

    def natural(self, array):
        swapped = array[..., jnp.array([1, 0, 3, 2]), :]
        array = jnp.where(self.plane % 2 == 1, swapped, array)
        swapped = array[..., jnp.array([2, 3, 0, 1]), :]
        return jnp.where(self.plane // 2 == 1, swapped, array)

    def even_first(self, mine, other):
        return jnp.stack([jnp.where(self.even, mine, other), jnp.where(self.even, other, mine)])


def exact_parts(values):
    high = lax.reduce_precision(values, 8, 7)
    rest = values - high
    middle = lax.reduce_precision(rest, 8, 7)
    return jnp.concatenate([high, middle, rest - middle]).astype(BF16)


def exact_sum(parts):
    rows = parts.shape[0] // 3
    parts = parts.astype(F32)
    return parts[:rows] + parts[rows : 2 * rows] + parts[2 * rows :]


def merge(both, other):
    last = lax.broadcasted_iota(jnp.int32, both.shape, 0) == 6
    return jnp.where(last, jnp.maximum(both, other), both + other)


def sync(*values):
    return lax.optimization_barrier(values)


def plain_all(links, grads):
    blank = jnp.zeros((4, 2) + grads.shape[1:], F32)
    full = lax.dynamic_update_slice_in_dim(blank, grads[:, None].astype(F32), links.half, 1)
    shard = lax.psum_scatter(full, "tensor", scatter_dimension=0, tiled=False)
    return lax.psum(shard, "dp")


def plain_pair(links, grads):
    blank = jnp.zeros((4,) + grads.shape[:1] + grads.shape[2:], F32)
    own = grads.swapaxes(0, 1).astype(F32)
    full = lax.dynamic_update_slice_in_dim(blank, own, 2 * links.half, 0)
    shard = lax.psum_scatter(full, "tensor", scatter_dimension=0, tiled=False)
    return lax.psum(shard, "dp")


def on_device(
    sizes,
    layer_input,
    segments,
    w_qkv,
    bias_qv,
    w_out,
    b_out,
    gain_attn,
    shift_attn,
    w_in,
    b_in,
    w_down,
    b_down,
    gain_ffn,
    shift_ffn,
    act_scale,
    out_grad,
):
    links = Links(*sizes)
    width = layer_input.shape[1]
    local = w_qkv.shape[2]
    heads = local // HEAD
    chunk = HEAD // 4
    units = w_in.shape[1]
    quarter = units // 8
    gain_first = gain_attn.astype(F32)
    gain_second = gain_ffn.astype(F32)

    per = 3 * heads * chunk
    more = heads * chunk

    rows = jnp.concatenate([jnp.swapaxes(w_qkv, 1, 2), w_out[None]])
    rows = rows.reshape(4, heads, 4, chunk, width)
    rows = rows.transpose(2, 0, 1, 3, 4).reshape(4, per + more, width)
    tail = bias_qv.reshape(2, heads, 4, chunk).transpose(2, 0, 1, 3).reshape(4, 1, 2 * more)
    tail = jnp.pad(tail, ((0, 0), (0, 7), (0, width - tail.shape[2])))
    attn_pack = jnp.concatenate([rows, tail], axis=1)
    if links.square:
        attn_mine = lax.dynamic_index_in_dim(attn_pack, links.plane, 0, False)
        attn_in = links.pair_out(attn_mine)
    seg_rows = segments.reshape(2, LEN)
    seg_mine = lax.dynamic_index_in_dim(seg_rows, links.depth // 2, 0, False).reshape(8, LEN // 8)
    seg_next = links.other_half(seg_mine)
    seg_home = links.at_home(seg_mine, seg_next).reshape(2, HALF)
    seg_home = jnp.where(links.half == 0, seg_home, seg_home[::-1]).reshape(LEN)
    seg_col, seg_row = seg_home[:, None], seg_home[None, :]
    ffn_half = jnp.concatenate(
        [
            lax.dynamic_index_in_dim(w_in.T.reshape(2, 4, quarter, width), links.half, 0, False),
            lax.dynamic_index_in_dim(w_down.reshape(2, 4, quarter, width), links.half, 0, False),
            jnp.pad(
                lax.dynamic_index_in_dim(b_in.reshape(2, 4, 1, quarter), links.half, 0, False),
                ((0, 0), (0, 7), (0, width - quarter)),
            ),
        ],
        axis=1,
    )
    if links.square:
        ffn_own = jnp.stack(
            [lax.dynamic_index_in_dim(ffn_half, j ^ links.plane, 0, False) for j in ORDER]
        )
        attn_in, ffn_mine, x_home = sync(attn_in, ffn_own[0], layer_input)
        attn_both = links.pair_of(attn_mine, attn_in)
        attn_near = links.spread_near(attn_both)
        x_home = links.rows_home(x_home)
        ffn_in = [links.along(ffn_mine, 2)]
        attn_near, ffn_in, ffn_mine = sync(attn_near, ffn_in, ffn_mine)
        attn_full = links.spread_far(attn_both, attn_near)
        ffn_in.append(links.along(ffn_mine, 3))
        attn_full, ffn_in, ffn_mine, x_home = sync(attn_full, ffn_in, ffn_mine, x_home)
        ffn_in.append(links.along(ffn_mine, 1))
        attn_full = jnp.stack(attn_full)
        ffn_in = jnp.stack([ffn_in[2], ffn_in[0], ffn_in[1]])
    else:
        attn_full = lax.all_gather(attn_pack, "tensor", axis=0, tiled=False)
        attn_full = lax.dynamic_slice_in_dim(attn_full, 2 * links.half, 2, 0).swapaxes(0, 1)
        ffn_in = lax.all_gather(ffn_half, "tensor", axis=0, tiled=False)
        x_home = links.rows_home(layer_input)
    x_home = links.at_home(layer_input, x_home)

    x_full = x_home.astype(F32)
    x_quant = jnp.clip(x_full, -act_scale[0], act_scale[0]).astype(BF16)
    x_other = links.other_half(x_quant)
    x_rows = jnp.concatenate([x_quant, x_other])

    weights = attn_full[:, :, : per + more].reshape(4, 2, 4, heads, chunk, width)
    weights = weights.transpose(2, 1, 3, 0, 4, 5).reshape(4, heads, 2 * HEAD, width)
    w_proj = weights[:3].swapaxes(0, 1).reshape(6 * local, width)
    w_back = weights[3].reshape(2 * local, width)
    biases = attn_full[:, :, per + more, : 2 * more].reshape(4, 2, 2, heads, chunk)
    biases = biases.transpose(2, 1, 3, 0, 4).reshape(2, 2 * local).astype(F32)
    bias_all = jnp.stack([biases[0], jnp.zeros_like(biases[0]), biases[1]])
    bias_all = bias_all.reshape(3, heads, 2 * HEAD).swapaxes(0, 1).reshape(6 * local)

    proj = (nt(x_rows, w_proj) + bias_all).astype(BF16)
    proj, ffn_in, out_grad = sync(proj, ffn_in, out_grad)
    if links.square:
        ffn_near = links.spread_near(ffn_in)
    upstream = links.rows_home(out_grad)
    context, lse = attend(proj, seg_col, seg_row, heads)
    context, upstream = sync(context, upstream)
    upstream = links.at_home(out_grad, upstream).astype(F32)
    ctx_quant = jnp.clip(context, -act_scale[1], act_scale[1]).astype(BF16)
    attn_part, attn_sent = nn(ctx_quant[:HALF], w_back), nn(ctx_quant[HALF:], w_back)
    if links.square:
        attn_part, attn_sent, ffn_near = sync(attn_part, attn_sent, ffn_near)
        pieces = links.spread_far(ffn_in, ffn_near)
        ffn_full = jnp.stack(
            [jnp.concatenate([ffn_own[i][None], pieces[j]]) for i, j in enumerate(ORDER)]
        )
    else:
        ffn_full = ffn_in.swapaxes(0, 1)
    attn_out = attn_part + links.other_half(attn_sent) + b_out.astype(F32)
    hidden, normed_attn, inverse_attn = norm_forward(
        x_full + attn_out, gain_first, shift_attn.astype(F32)
    )
    hid_quant = jnp.clip(hidden, -act_scale[2], act_scale[2]).astype(BF16)
    hid_rows = jnp.concatenate([hid_quant, links.other_half(hid_quant)])

    w_up = ffn_full[:, :, :quarter].reshape(2 * units, width)
    w_low = ffn_full[:, :, quarter : 2 * quarter].reshape(2 * units, width)
    b_up = ffn_full[:, :, 2 * quarter, :quarter].reshape(2 * units).astype(F32)
    pre_act = nt(hid_rows, w_up) + b_up
    normal_cdf = 0.5 * (1.0 + lax.erf(pre_act * 0.5**0.5))
    activated = pre_act * normal_cdf
    slope = normal_cdf + pre_act * jnp.exp(-0.5 * pre_act * pre_act) / math.sqrt(2.0 * math.pi)
    slope = jnp.where(jnp.abs(activated) <= act_scale[3], slope, 0.0)
    act_quant = jnp.clip(activated, -act_scale[3], act_scale[3]).astype(BF16)
    ffn_sent, ffn_part = nn(act_quant[HALF:], w_low), nn(act_quant[:HALF], w_low)
    ffn_out = ffn_part + links.other_half(ffn_sent)
    final, normed_ffn, inverse_ffn = norm_forward(
        hidden + ffn_out + b_down.astype(F32), gain_second, shift_ffn.astype(F32)
    )
    final = final.astype(BF16)
    layer_output = links.rows_home(final)
    lanes = lax.broadcasted_iota(jnp.int32, (1, width), 1)
    maxima = jnp.zeros((1, width), F32)
    for at, array in enumerate((x_full, context, hidden, activated)):
        maxima = jnp.where(lanes == at, jnp.max(jnp.abs(array)), maxima)

    grad_gain_ffn = jnp.sum(upstream * normed_ffn, axis=0, keepdims=True)
    grad_shift_ffn = jnp.sum(upstream, axis=0, keepdims=True)
    grad_second = norm_backward(upstream, normed_ffn, inverse_ffn, gain_second)
    grad_b_down = jnp.sum(grad_second, axis=0, keepdims=True)
    grad_final = grad_second.astype(BF16)
    grad_rows = jnp.concatenate([grad_final, links.other_half(grad_final)])
    down = tn(act_quant, grad_rows).astype(BF16).reshape(4, 4, quarter, width)
    grad_pre = nt(grad_rows, w_low) * slope
    grad_b_in = jnp.sum(grad_pre, axis=0)
    grad_pre_b = grad_pre.astype(BF16)
    up = tn(grad_pre_b, hid_rows).astype(BF16).reshape(4, 4, quarter, width)
    tail = jnp.pad(
        grad_b_in.astype(BF16).reshape(4, 4, 1, quarter),
        ((0, 0), (0, 0), (0, 7), (0, width - quarter)),
    )
    ffn_grads = jnp.concatenate([up, down, tail], axis=2)
    if links.square:
        ffn_grads, grad_pre_b = sync(ffn_grads, grad_pre_b)
        ffn_x = links.across(ffn_grads[1:3, :2], 1)
        ffn_y = links.across(ffn_grads[2:4, 2:], 2)
    hid_sent, hid_part = nn(grad_pre_b[HALF:], w_up), nn(grad_pre_b[:HALF], w_up)
    grad_hid = hid_part + links.other_half(hid_sent)

    grad_hidden = grad_second + grad_hid * (jnp.abs(hidden) <= act_scale[2]).astype(F32)
    grad_gain_attn = jnp.sum(grad_hidden * normed_attn, axis=0, keepdims=True)
    grad_shift_attn = jnp.sum(grad_hidden, axis=0, keepdims=True)
    grad_first = norm_backward(grad_hidden, normed_attn, inverse_attn, gain_first)
    grad_b_out = jnp.sum(grad_first, axis=0, keepdims=True)
    grad_attn = grad_first.astype(BF16)
    go_other = links.other_half(grad_attn)
    sums = [grad_b_out, grad_gain_attn, grad_shift_attn, grad_b_down, grad_gain_ffn, grad_shift_ffn]
    sums = jnp.concatenate([*sums, maxima, jnp.zeros((1, width), F32)])

    def back(first, count, before):
        return attend_back(
            first,
            count,
            before,
            proj,
            grad_attn,
            go_other,
            x_quant,
            x_other,
            w_back,
            context,
            lse,
            seg_col,
            seg_row,
            act_scale[1:2],
        )

    def bias_rows(pairs):
        return pairs.reshape(heads, 2, 2, 4, chunk).swapaxes(0, 1)

    if links.square:
        tall = 2 * heads * HEAD // 2
        many = heads - 1
        early, grad_w, early_b = back(0, many, None)
        early, go_other, ffn_x, ffn_y, layer_output = sync(
            early, go_other, ffn_x, ffn_y, layer_output
        )
        low = [ffn_grads[0, :2] + ffn_x[0].astype(F32), ffn_grads[3, :2] + ffn_x[1].astype(F32)]
        high = [ffn_grads[0, 2:] + ffn_y[1].astype(F32), ffn_grads[1, 2:] + ffn_y[0].astype(F32)]
        ffn_y, ffn_x = low[1].astype(BF16), high[1].astype(BF16)
        go_other, ffn_x, ffn_y = sync(go_other, ffn_x, ffn_y)
        ffn_y, ffn_x = links.across(ffn_y, 2), links.across(ffn_x, 1)
        late, grad_w, late_b = back(many, 1, grad_w)
        late, grad_w, late_b, ffn_x, ffn_y = sync(late, grad_w, late_b, ffn_x, ffn_y)
        sums = merge(sums, links.other_half(sums))
        bias_sums = links.natural(bias_rows(jnp.concatenate([early_b, late_b])))
        sums = jnp.concatenate([sums[:7], bias_sums.reshape(1, width)])
        sums_sent = exact_parts(sums)
        ffn_low = low[0] + ffn_y.astype(F32)
        ffn_in = links.along((high[0] + ffn_x.astype(F32)).astype(BF16), 2)
        proj_in = [
            links.across(jnp.concatenate([grad_w[step], sums_sent]), step) for step in (1, 2, 3)
        ]
        grad_proj, ffn_low = sync(jnp.concatenate([early, late], axis=1), ffn_low)
    else:
        grad_proj, grad_w, bias_sums = back(0, heads, None)
        bias_sums = bias_rows(bias_sums)
    x_sent, x_part = nn(grad_proj[HALF:], w_proj), nn(grad_proj[:HALF], w_proj)
    grad_x = x_part + links.other_half(x_sent)
    input_grad = grad_first + grad_x * (jnp.abs(x_full) <= act_scale[0]).astype(F32)
    input_part = input_grad.astype(BF16)

    if links.square:
        proj_in, input_part = sync(proj_in, input_part)
        total = grad_w[0].astype(F32)
        for part in proj_in:
            total = total + part[: 2 * tall].astype(F32)
            sums = merge(sums, exact_sum(part[2 * tall :]))
        mine = jnp.where(links.even, total[:tall], total[tall:])
        other = jnp.where(links.even, total[tall:], total[:tall])
        sums_sent = exact_parts(sums)
        other = jnp.concatenate([other.astype(BF16), sums_sent])
        proj_in = [
            links.pair_near(other),
            links.pair_back(jnp.concatenate([mine.astype(BF16), sums_sent])),
            links.pair_cross(other),
        ]
        ffn_in, total = sync(ffn_in, total)
        ffn_low = ffn_low + ffn_in.astype(F32)
        ffn_in = links.along(ffn_low[1].astype(BF16), 1)
        for part in proj_in:
            mine = mine + part[:tall].astype(F32)
            sums = merge(sums, exact_sum(part[tall:]))
        mine, input_part = sync(mine.astype(BF16), input_part)
        proj_all = links.spread(mine, lambda c, z: z // 2 == c)
        ffn_mine = (ffn_low[0] + ffn_in.astype(F32)).astype(BF16)
        ffn_all = links.spread(ffn_mine)
        proj_all, ffn_all = sync(proj_all, ffn_all)
        proj_all = jnp.concatenate([*proj_all, exact_parts(sums)])
        proj_other = links.other_half(proj_all)
        sums = exact_sum(jnp.where(links.inside, proj_all[4 * tall :], proj_other[4 * tall :]))
        grad_qkv, grad_out = unpack(links.inside, links.plane, proj_all, proj_other, tall)
        grad_qkv = jnp.swapaxes(grad_qkv, 1, 2)
        ffn_all = links.halves_in_order(links.in_order(ffn_all))
    else:
        ffn_all = plain_all(links, ffn_grads.swapaxes(0, 1))
        grads = plain_pair(links, grad_w.reshape(4, 2, -1, width))
        grads = grads.reshape(4, heads, 4, chunk, width).transpose(2, 1, 0, 3, 4)
        grads = grads.reshape(4, local, width)
        grad_qkv, grad_out = jnp.swapaxes(grads[:3], 1, 2), grads[3]
        sums = jnp.concatenate([lax.psum(sums[:6], JOINT), lax.pmax(sums[6:7], JOINT)])
        both = jnp.zeros((4, 2, local), F32)
        both = lax.dynamic_update_slice_in_dim(
            both, bias_sums.reshape(2, 2, local).swapaxes(0, 1), 2 * links.half, 0
        )
        both = lax.psum(both, JOINT)
        both = lax.dynamic_slice_in_dim(both, links.depth - links.depth % 2, 2, 0)
        sums = jnp.concatenate([sums, both.swapaxes(0, 1).reshape(1, width)])
    input_grad = links.at_home(input_part, links.rows_home(input_part)).astype(F32)
    maxima = sums[6, :4]
    new_scale = DECAY * act_scale + (1.0 - DECAY) * maxima

    up_grads, down_grads = ffn_all[:, :, :quarter], ffn_all[:, :, quarter : 2 * quarter]
    grad_bias_qv = lax.dynamic_index_in_dim(
        sums[7].reshape(2, 2, local), links.depth % 2, 1, False
    )
    return (
        links.at_home(final, layer_output),
        input_grad,
        grad_qkv,
        grad_bias_qv,
        grad_out,
        sums[0],
        sums[1],
        sums[2],
        up_grads.reshape(units, width).astype(F32).T,
        ffn_all[:, :, 2 * quarter, :quarter].reshape(units).astype(F32),
        down_grads.reshape(units, width).astype(F32),
        sums[3],
        sums[4],
        sums[5],
        new_scale,
        maxima,
    )


def solution(mesh):
    in_specs = (
        P(("dp", "tensor"), None),
        P("dp"),
        P(None, None, "tensor"),
        P(None, "tensor"),
        P("tensor", None),
        P(),
        P(),
        P(),
        P(None, "tensor"),
        P("tensor"),
        P("tensor", None),
        P(),
        P(),
        P(),
        P(),
        P(("dp", "tensor"), None),
    )
    out_specs = (
        P(("dp", "tensor"), None),
        P(("dp", "tensor"), None),
        P(None, None, "tensor"),
        P(None, "tensor"),
        P("tensor", None),
        P(),
        P(),
        P(),
        P(None, "tensor"),
        P("tensor"),
        P("tensor", None),
        P(),
        P(),
        P(),
        P(),
        P(),
    )
    sizes = (mesh.shape["dp"], mesh.shape["tensor"])
    return jax.shard_map(
        functools.partial(on_device, sizes),
        mesh=mesh,
        in_specs=in_specs,
        out_specs=out_specs,
        check_vma=False,
    )
```

```python
import functools
import math

import jax
import jax.numpy as jnp
from jax import lax
from jax.experimental import pallas as pl
from jax.experimental.pallas import tpu as pltpu
from jax.sharding import PartitionSpec as P

HEAD = 64
LEN = 1024
HALF = LEN // 2
BLOCK = 256

EPSILON = 1e-12
DECAY = 0.9999
MASKED = -1e30
ORDER = (0, 1, 3, 2)
JOINT = ("dp", "tensor")
BF16 = jnp.bfloat16
F32 = jnp.float32


def norm_forward(resid, gain, shift):
    row_mean = jnp.mean(resid, axis=-1, keepdims=True)
    centred = resid - row_mean
    spread = jnp.mean(centred * centred, axis=-1, keepdims=True)
    inverse = lax.rsqrt(spread + EPSILON)
    normed = centred * inverse
    return (normed * gain + shift, normed, inverse)


def norm_backward(upstream, normed, inverse, gain):
    scaled = upstream * gain
    mean_first = jnp.mean(scaled, axis=-1, keepdims=True)
    mean_second = jnp.mean(scaled * normed, axis=-1, keepdims=True)
    return inverse * (scaled - mean_first - normed * mean_second)


def nt(a, b):
    return lax.dot_general(a, b, (((1,), (1,)), ((), ())), preferred_element_type=F32)


def nn(a, b):
    return lax.dot_general(a, b, (((1,), (0,)), ((), ())), preferred_element_type=F32)


def tn(a, b):
    return lax.dot_general(a, b, (((0,), (0,)), ((), ())), preferred_element_type=F32)


def attend_kernel(q_ref, k_ref, v_ref, seg_col_ref, seg_row_ref, ctx_ref, lse_ref):
    low = lax.broadcasted_iota(jnp.int32, (BLOCK, 2 * HEAD), 1) < HEAD
    keys = k_ref[...]
    values = v_ref[...]
    for block in range(LEN // BLOCK):
        rows = pl.ds(block * BLOCK, BLOCK)
        queries = q_ref[rows, :] * jnp.asarray(HEAD**-0.5, BF16)
        same = seg_col_ref[rows, :] == seg_row_ref[...]
        parts, logs = [], []
        for head in range(2):
            own = low if head == 0 else jnp.logical_not(low)
            scores = nt(jnp.where(own, queries, jnp.zeros_like(queries)), keys)
            scores = jnp.where(same, scores, MASKED)
            top = jnp.max(scores, axis=-1, keepdims=True)
            exponent = jnp.exp(scores - top)
            total = jnp.sum(exponent, axis=-1, keepdims=True)
            attention = (exponent * (1.0 / total)).astype(BF16)
            parts.append(nn(attention, values))
            logs.append(top + jnp.log(total))
        ctx_ref[rows, :] = jnp.where(low, parts[0], parts[1])
        lse_ref[0, :, rows] = jnp.transpose(jnp.concatenate(logs, axis=1))


def attention_cost(pairs_of_heads, products):
    scores = 2 * pairs_of_heads * LEN * LEN
    return pl.CostEstimate(
        flops=2 * 4 * HEAD * products * scores,
        transcendentals=scores,
        bytes_accessed=8 * pairs_of_heads * LEN * HEAD * products,
    )


def attend(proj, seg_col, seg_row, pairs_of_heads):
    n = pairs_of_heads
    return pl.pallas_call(
        attend_kernel,
        grid=(n,),
        in_specs=[
            pl.BlockSpec((LEN, 2 * HEAD), lambda i: (0, 3 * i)),
            pl.BlockSpec((LEN, 2 * HEAD), lambda i: (0, 3 * i + 1)),
            pl.BlockSpec((LEN, 2 * HEAD), lambda i: (0, 3 * i + 2)),
            pl.BlockSpec((LEN, 1), lambda i: (0, 0)),
            pl.BlockSpec((1, LEN), lambda i: (0, 0)),
        ],
        out_specs=[
            pl.BlockSpec((LEN, 2 * HEAD), lambda i: (0, i)),
            pl.BlockSpec((1, 2, LEN), lambda i: (i, 0, 0)),
        ],
        out_shape=[
            jax.ShapeDtypeStruct((LEN, n * 2 * HEAD), F32),
            jax.ShapeDtypeStruct((n, 2, LEN), F32),
        ],
        name="attend",
    )(proj, proj, proj, seg_col, seg_row)


def attend_back_kernel(
    q_ref,
    k_ref,
    v_ref,
    go_ref,
    go_other_ref,
    x_ref,
    x_other_ref,
    back_ref,
    ctx_ref,
    lse_ref,
    seg_col_ref,
    seg_row_ref,
    limit_ref,
    grad_ref,
    pack_ref,
    sum_ref,
    acc_ref,
    grads_ref,
    quant_ref,
    inner_ref,
):
    low = lax.broadcasted_iota(jnp.int32, (BLOCK, 2 * HEAD), 1) < HEAD
    limit = limit_ref[0]
    for half, rows_ref in enumerate((go_ref, go_other_ref)):
        for block in range(HALF // BLOCK):
            rows = pl.ds(half * HALF + block * BLOCK, BLOCK)
            context = ctx_ref[rows, :]
            quant_ref[rows, :] = jnp.clip(context, -limit, limit).astype(BF16)
            grad = nt(rows_ref[pl.ds(block * BLOCK, BLOCK), :], back_ref[...])
            grad = jnp.where(jnp.abs(context) <= limit, grad, 0.0).astype(BF16)
            grads_ref[rows, :] = grad
            both = grad.astype(F32) * context
            inner = [
                jnp.sum(jnp.where(own, both, 0.0), axis=1, keepdims=True)
                for own in (low, jnp.logical_not(low))
            ]
            inner_ref[:, rows] = jnp.transpose(jnp.concatenate(inner, axis=1))
    queries = q_ref[...]
    grads = grads_ref[...]
    value_sum = jnp.zeros((1, 2 * HEAD), F32)
    for block in range(LEN // BLOCK):
        rows = pl.ds(block * BLOCK, BLOCK)
        keys = k_ref[rows, :]
        scaled_keys = keys * jnp.asarray(HEAD**-0.5, BF16)
        values = v_ref[rows, :]
        same = seg_col_ref[rows, :] == seg_row_ref[...]
        value_parts, key_parts = [], []
        for head in range(2):
            own = low if head == 0 else jnp.logical_not(low)
            zero = jnp.zeros_like(keys)
            scores = nt(jnp.where(own, scaled_keys, zero), queries)
            logs = lse_ref[0, head : head + 1, :]
            attention = jnp.where(same, jnp.exp(scores - logs), 0.0)
            value_parts.append(nn(attention.astype(BF16), grads))
            grad_attention = nt(jnp.where(own, values, zero), grads)
            inner = inner_ref[head : head + 1, :]
            grad_score = (attention * (grad_attention - inner) * HEAD**-0.5).astype(BF16)
            key_parts.append(nn(grad_score, queries))
            part = tn(grad_score, jnp.where(own, keys, zero))
            if block == 0 and head == 0:
                acc_ref[...] = part
            else:
                acc_ref[...] += part
        grad_value = jnp.where(low, value_parts[0], value_parts[1])
        value_sum += jnp.sum(grad_value, axis=0, keepdims=True)
        grad_ref[rows, 4 * HEAD :] = grad_value.astype(BF16)
        grad_ref[rows, 2 * HEAD : 4 * HEAD] = jnp.where(low, key_parts[0], key_parts[1]).astype(BF16)
    grad_query = acc_ref[...]
    grad_ref[:, : 2 * HEAD] = grad_query.astype(BF16)
    sum_ref[0, 0:1, :] = jnp.sum(grad_query, axis=0, keepdims=True)
    sum_ref[0, 1:2, :] = value_sum
    chunk = HEAD // 4
    sides = ((slice(0, HALF), x_ref, go_ref), (slice(HALF, LEN), x_other_ref, go_other_ref))
    for kind in range(4):
        lanes = slice(2 * kind * HEAD, 2 * (kind + 1) * HEAD)
        total = None
        for rows, x_side, go_side in sides:
            if kind < 3:
                part = tn(grad_ref[rows, lanes], x_side[...])
            else:
                part = tn(quant_ref[rows, :], go_side[...])
            total = part if total is None else total + part
        total = total.astype(BF16)
        for head in range(2):
            for j in range(4):
                at = head * HEAD + j * chunk
                into = (head * 4 + kind) * chunk
                pack_ref[j, into : into + chunk, :] = total[at : at + chunk, :]


def attend_back(
    first, n, before, proj, go, go_other, x, x_other, w_back, context, lse, seg_col, seg_row, limit
):
    width = w_back.shape[1]
    earlier = [] if before is None else [before]

    def body(*refs):
        attend_back_kernel(*refs[:13], *refs[13 + len(earlier) :])

    def whole(array):
        return pl.BlockSpec(array.shape, lambda i: (0,) * array.ndim)

    return pl.pallas_call(
        body,
        grid=(n,),
        in_specs=[
            pl.BlockSpec((LEN, 2 * HEAD), lambda i: (0, 3 * (first + i))),
            pl.BlockSpec((LEN, 2 * HEAD), lambda i: (0, 3 * (first + i) + 1)),
            pl.BlockSpec((LEN, 2 * HEAD), lambda i: (0, 3 * (first + i) + 2)),
            *[whole(array) for array in (go, go_other, x, x_other)],
            pl.BlockSpec((2 * HEAD, width), lambda i: (first + i, 0)),
            pl.BlockSpec((LEN, 2 * HEAD), lambda i: (0, first + i)),
            pl.BlockSpec((1, 2, LEN), lambda i: (first + i, 0, 0)),
            whole(seg_col),
            whole(seg_row),
            pl.BlockSpec(memory_space=pltpu.SMEM),
            *[pl.BlockSpec(memory_space=pl.ANY) for _ in earlier],
        ],
        out_specs=[
            pl.BlockSpec((LEN, 6 * HEAD), lambda i: (0, i)),
            pl.BlockSpec((4, 2 * HEAD, width), lambda i: (0, first + i, 0)),
            pl.BlockSpec((1, 2, 2 * HEAD), lambda i: (i, 0, 0)),
        ],
        out_shape=[
            jax.ShapeDtypeStruct((LEN, n * 6 * HEAD), BF16),
            jax.ShapeDtypeStruct((4, *w_back.shape), BF16),
            jax.ShapeDtypeStruct((n, 2, 2 * HEAD), F32),
        ],
        scratch_shapes=[
            pltpu.VMEM((LEN, 2 * HEAD), F32),
            pltpu.VMEM((LEN, 2 * HEAD), BF16),
            pltpu.VMEM((LEN, 2 * HEAD), BF16),
            pltpu.VMEM((2, LEN), F32),
        ],
        cost_estimate=attention_cost(n, 9) if first else None,
        input_output_aliases={13: 1} if earlier else {},
        name="attend_back",
    )(
        *(proj, proj, proj, go, go_other, x, x_other, w_back, context, lse),
        *(seg_col, seg_row, limit, *earlier),
    )


def unpack_kernel(where_ref, own_ref, other_ref, qkv_ref, out_ref):
    inside, plane = where_ref[0], where_ref[1]
    kind = pl.program_id(0)
    chunk = HEAD // 4
    tall = own_ref.shape[0] // 4
    heads = tall // HEAD

    def rows_of(ref):
        parts = []
        for head in range(heads):
            for j in range(4):
                at = (j ^ plane) * tall + head * HEAD + kind * chunk
                parts.append(ref[pl.ds(pl.multiple_of(at, chunk), chunk), :])
        return jnp.concatenate(parts, axis=0).astype(F32)

    for flag, ref in ((1, own_ref), (0, other_ref)):

        @pl.when(jnp.logical_and(inside == flag, kind < 3))
        def _(ref=ref):
            qkv_ref[0] = rows_of(ref)

        @pl.when(jnp.logical_and(inside == flag, kind == 3))
        def _(ref=ref):
            out_ref[...] = rows_of(ref)


def unpack(inside, plane, own, other, tall):
    width = own.shape[1]
    return pl.pallas_call(
        unpack_kernel,
        grid=(4,),
        in_specs=[
            pl.BlockSpec(memory_space=pltpu.SMEM),
            pl.BlockSpec((4 * tall, width), lambda i: (0, 0)),
            pl.BlockSpec((4 * tall, width), lambda i: (0, 0)),
        ],
        out_specs=[
            pl.BlockSpec((1, tall, width), lambda i: (jnp.minimum(i, 2), 0, 0)),
            pl.BlockSpec((tall, width), lambda i: (0, 0)),
        ],
        out_shape=[
            jax.ShapeDtypeStruct((3, tall, width), F32),
            jax.ShapeDtypeStruct((tall, width), F32),
        ],
        name="unpack",
    )(jnp.stack([inside.astype(jnp.int32), plane]), own, other)


class Links:
    def __init__(self, dp, depths):
        self.dp, self.depths = dp, depths
        self.planes = dp // 2
        place = lax.axis_index("dp")
        self.half, self.plane = place % 2, place // 2
        self.depth = lax.axis_index("tensor")
        self.square = self.planes == 4 and depths == 4

    def permute(self, array, move):
        pairs = []
        for place in range(self.dp):
            for depth in range(self.depths):
                to = move(place // 2, place % 2, depth)
                if to is not None:
                    plane, half, level = to
                    pairs.append(
                        (place * self.depths + depth, (2 * plane + half) * self.depths + level)
                    )
        return lax.ppermute(array, JOINT, pairs)

    def rows_home(self, array):
        return self.permute(
            array, lambda e, c, z: (e, z % 2, z - z % 2 + c) if c != z % 2 else None
        )

    def at_home(self, own, moved):
        return jnp.where(self.depth % 2 == self.half, own, moved)

    def other_half(self, array):
        return self.permute(array, lambda e, c, z: (e, 1 - c, z))

    def across(self, array, step, only=None):
        return self.permute(
            array,
            lambda e, c, z: (e ^ step, c, z) if only is None or only(c, z) else None,
        )

    def along(self, array, step):
        return self.permute(array, lambda e, c, z: (e, c, z ^ step))

    def spread_near(self, piece, only=None):
        return self.across(piece, 1, only), self.across(piece, 2, only)

    def spread_far(self, piece, near, only=None):
        first, second = near
        cut = piece.shape[-2] // 16 * 8
        third_low = self.across(second[..., :cut, :], 1, only)
        third_high = self.across(first[..., cut:, :], 2, only)
        return [piece, first, second, jnp.concatenate([third_low, third_high], axis=-2)]

    def spread(self, piece, only=None):
        return [piece] + [self.across(piece, step, only) for step in (1, 2, 3)]

    def in_order(self, pieces):
        stack = jnp.stack(pieces)
        return jnp.stack(
            [lax.dynamic_index_in_dim(stack, j ^ self.plane, 0, False) for j in range(4)]
        )

    @property
    def inside(self):
        return self.depth // 2 == self.half

    @property
    def even(self):
        return self.depth % 2 == 0

    def pair_near(self, array):
        return self.permute(array, lambda e, c, z: (e, c, z ^ 1) if z // 2 == c else None)

    def pair_out(self, array):
        def far(step):
            return lambda e, c, z: (e, c, z ^ step) if z // 2 == c else None

        return [self.permute(array, far(step)) for step in (2, 3, 1)]

    def pair_of(self, mine, arrived):
        same, cross, near = arrived
        a = jnp.where(self.inside, mine, same)
        b = jnp.where(self.inside, near, cross)
        return self.even_first(a, b)

    def pair_back(self, array):
        return self.permute(array, lambda e, c, z: (e, c, z ^ 2) if z // 2 != c else None)

    def pair_cross(self, array):
        return self.permute(array, lambda e, c, z: (e, c, z ^ 3) if z // 2 != c else None)

    def halves_in_order(self, mine):
        other = self.other_half(mine)
        first = self.half == 0
        return jnp.stack([jnp.where(first, mine, other), jnp.where(first, other, mine)])

    def natural(self, array):
        swapped = array[..., jnp.array([1, 0, 3, 2]), :]
        array = jnp.where(self.plane % 2 == 1, swapped, array)
        swapped = array[..., jnp.array([2, 3, 0, 1]), :]
        return jnp.where(self.plane // 2 == 1, swapped, array)

    def even_first(self, mine, other):
        return jnp.stack([jnp.where(self.even, mine, other), jnp.where(self.even, other, mine)])


def exact_parts(values):
    high = lax.reduce_precision(values, 8, 7)
    rest = values - high
    middle = lax.reduce_precision(rest, 8, 7)
    return jnp.concatenate([high, middle, rest - middle]).astype(BF16)


def exact_sum(parts):
    rows = parts.shape[0] // 3
    parts = parts.astype(F32)
    return parts[:rows] + parts[rows : 2 * rows] + parts[2 * rows :]


def merge(both, other):
    last = lax.broadcasted_iota(jnp.int32, both.shape, 0) == 6
    return jnp.where(last, jnp.maximum(both, other), both + other)


def sync(*values):
    return lax.optimization_barrier(values)


def plain_all(links, grads):
    blank = jnp.zeros((4, 2) + grads.shape[1:], F32)
    full = lax.dynamic_update_slice_in_dim(blank, grads[:, None].astype(F32), links.half, 1)
    shard = lax.psum_scatter(full, "tensor", scatter_dimension=0, tiled=False)
    return lax.psum(shard, "dp")


def plain_pair(links, grads):
    blank = jnp.zeros((4,) + grads.shape[:1] + grads.shape[2:], F32)
    own = grads.swapaxes(0, 1).astype(F32)
    full = lax.dynamic_update_slice_in_dim(blank, own, 2 * links.half, 0)
    shard = lax.psum_scatter(full, "tensor", scatter_dimension=0, tiled=False)
    return lax.psum(shard, "dp")


def on_device(
    sizes,
    layer_input,
    segments,
    w_qkv,
    bias_qv,
    w_out,
    b_out,
    gain_attn,
    shift_attn,
    w_in,
    b_in,
    w_down,
    b_down,
    gain_ffn,
    shift_ffn,
    act_scale,
    out_grad,
):
    links = Links(*sizes)
    width = layer_input.shape[1]
    local = w_qkv.shape[2]
    heads = local // HEAD
    chunk = HEAD // 4
    units = w_in.shape[1]
    quarter = units // 8
    gain_first = gain_attn.astype(F32)
    gain_second = gain_ffn.astype(F32)

    per = 3 * heads * chunk
    more = heads * chunk

    rows = jnp.concatenate([jnp.swapaxes(w_qkv, 1, 2), w_out[None]])
    rows = rows.reshape(4, heads, 4, chunk, width)
    rows = rows.transpose(2, 0, 1, 3, 4).reshape(4, per + more, width)
    tail = bias_qv.reshape(2, heads, 4, chunk).transpose(2, 0, 1, 3).reshape(4, 1, 2 * more)
    tail = jnp.pad(tail, ((0, 0), (0, 7), (0, width - tail.shape[2])))
    attn_pack = jnp.concatenate([rows, tail], axis=1)
    if links.square:
        attn_mine = lax.dynamic_index_in_dim(attn_pack, links.plane, 0, False)
        attn_in = links.pair_out(attn_mine)
    seg_rows = segments.reshape(2, LEN)
    seg_mine = lax.dynamic_index_in_dim(seg_rows, links.depth // 2, 0, False).reshape(8, LEN // 8)
    seg_next = links.other_half(seg_mine)
    seg_home = links.at_home(seg_mine, seg_next).reshape(2, HALF)
    seg_home = jnp.where(links.half == 0, seg_home, seg_home[::-1]).reshape(LEN)
    seg_col, seg_row = seg_home[:, None], seg_home[None, :]
    ffn_half = jnp.concatenate(
        [
            lax.dynamic_index_in_dim(w_in.T.reshape(2, 4, quarter, width), links.half, 0, False),
            lax.dynamic_index_in_dim(w_down.reshape(2, 4, quarter, width), links.half, 0, False),
            jnp.pad(
                lax.dynamic_index_in_dim(b_in.reshape(2, 4, 1, quarter), links.half, 0, False),
                ((0, 0), (0, 7), (0, width - quarter)),
            ),
        ],
        axis=1,
    )
    if links.square:
        ffn_own = jnp.stack(
            [lax.dynamic_index_in_dim(ffn_half, j ^ links.plane, 0, False) for j in ORDER]
        )
        attn_in, ffn_mine, x_home = sync(attn_in, ffn_own[0], layer_input)
        attn_both = links.pair_of(attn_mine, attn_in)
        attn_near = links.spread_near(attn_both)
        x_home = links.rows_home(x_home)
        ffn_two = links.along(ffn_mine, 2)
        attn_near, ffn_two, ffn_mine = sync(attn_near, ffn_two, ffn_mine)
        attn_full = jnp.stack(links.spread_far(attn_both, attn_near))
        ffn_in = jnp.stack([links.along(ffn_mine, 1), ffn_two, links.along(ffn_mine, 3)])
    else:
        attn_full = lax.all_gather(attn_pack, "tensor", axis=0, tiled=False)
        attn_full = lax.dynamic_slice_in_dim(attn_full, 2 * links.half, 2, 0).swapaxes(0, 1)
        ffn_in = lax.all_gather(ffn_half, "tensor", axis=0, tiled=False)
        x_home = links.rows_home(layer_input)
    x_home = links.at_home(layer_input, x_home)

    x_full = x_home.astype(F32)
    x_quant = jnp.clip(x_full, -act_scale[0], act_scale[0]).astype(BF16)
    x_other = links.other_half(x_quant)
    x_rows = jnp.concatenate([x_quant, x_other])

    weights = attn_full[:, :, : per + more].reshape(4, 2, 4, heads, chunk, width)
    weights = weights.transpose(2, 1, 3, 0, 4, 5).reshape(4, heads, 2 * HEAD, width)
    w_proj = weights[:3].swapaxes(0, 1).reshape(6 * local, width)
    w_back = weights[3].reshape(2 * local, width)
    biases = attn_full[:, :, per + more, : 2 * more].reshape(4, 2, 2, heads, chunk)
    biases = biases.transpose(2, 1, 3, 0, 4).reshape(2, 2 * local).astype(F32)
    bias_all = jnp.stack([biases[0], jnp.zeros_like(biases[0]), biases[1]])
    bias_all = bias_all.reshape(3, heads, 2 * HEAD).swapaxes(0, 1).reshape(6 * local)

    proj = (nt(x_rows, w_proj) + bias_all).astype(BF16)
    proj, ffn_in, out_grad = sync(proj, ffn_in, out_grad)
    if links.square:
        ffn_near = links.spread_near(ffn_in)
    upstream = links.rows_home(out_grad)
    context, lse = attend(proj, seg_col, seg_row, heads)
    context, upstream = sync(context, upstream)
    upstream = links.at_home(out_grad, upstream).astype(F32)
    ctx_quant = jnp.clip(context, -act_scale[1], act_scale[1]).astype(BF16)
    attn_part, attn_sent = nn(ctx_quant[:HALF], w_back), nn(ctx_quant[HALF:], w_back)
    if links.square:
        attn_part, attn_sent, ffn_near = sync(attn_part, attn_sent, ffn_near)
        pieces = links.spread_far(ffn_in, ffn_near)
        ffn_full = jnp.stack(
            [jnp.concatenate([ffn_own[i][None], pieces[j]]) for i, j in enumerate(ORDER)]
        )
    else:
        ffn_full = ffn_in.swapaxes(0, 1)
    attn_out = attn_part + links.other_half(attn_sent) + b_out.astype(F32)
    hidden, normed_attn, inverse_attn = norm_forward(
        x_full + attn_out, gain_first, shift_attn.astype(F32)
    )
    hid_quant = jnp.clip(hidden, -act_scale[2], act_scale[2]).astype(BF16)
    hid_other = links.other_half(hid_quant)
    tops = [jnp.max(jnp.abs(array)) for array in (x_full, context, hidden)]
    hid_other, tops = sync(hid_other, tops)
    hid_rows = jnp.concatenate([hid_quant, hid_other])

    w_up = ffn_full[:, :, :quarter].reshape(2 * units, width)
    w_low = ffn_full[:, :, quarter : 2 * quarter].reshape(2 * units, width)
    b_up = ffn_full[:, :, 2 * quarter, :quarter].reshape(2 * units).astype(F32)
    pre_act = nt(hid_rows, w_up) + b_up
    normal_cdf = 0.5 * (1.0 + lax.erf(pre_act * 0.5**0.5))
    activated = pre_act * normal_cdf
    slope = normal_cdf + pre_act * jnp.exp(-0.5 * pre_act * pre_act) / math.sqrt(2.0 * math.pi)
    slope = jnp.where(jnp.abs(activated) <= act_scale[3], slope, 0.0)
    act_quant = jnp.clip(activated, -act_scale[3], act_scale[3]).astype(BF16)
    ffn_sent, ffn_part = nn(act_quant[HALF:], w_low), nn(act_quant[:HALF], w_low)
    ffn_out = ffn_part + links.other_half(ffn_sent)
    final, normed_ffn, inverse_ffn = norm_forward(
        hidden + ffn_out + b_down.astype(F32), gain_second, shift_ffn.astype(F32)
    )
    final = final.astype(BF16)
    layer_output = links.rows_home(final)
    lanes = lax.broadcasted_iota(jnp.int32, (1, width), 1)
    maxima = jnp.zeros((1, width), F32)
    for at, value in enumerate((*tops, jnp.max(jnp.abs(activated)))):
        maxima = jnp.where(lanes == at, value, maxima)

    grad_gain_ffn = jnp.sum(upstream * normed_ffn, axis=0, keepdims=True)
    grad_shift_ffn = jnp.sum(upstream, axis=0, keepdims=True)
    grad_second = norm_backward(upstream, normed_ffn, inverse_ffn, gain_second)
    grad_b_down = jnp.sum(grad_second, axis=0, keepdims=True)
    grad_final = grad_second.astype(BF16)
    grad_rows = jnp.concatenate([grad_final, links.other_half(grad_final)])
    down = tn(act_quant, grad_rows).astype(BF16).reshape(4, 4, quarter, width)
    grad_pre = nt(grad_rows, w_low) * slope
    grad_b_in = jnp.sum(grad_pre, axis=0)
    grad_pre_b = grad_pre.astype(BF16)
    up = tn(grad_pre_b, hid_rows).astype(BF16).reshape(4, 4, quarter, width)
    tail = jnp.pad(
        grad_b_in.astype(BF16).reshape(4, 4, 1, quarter),
        ((0, 0), (0, 0), (0, 7), (0, width - quarter)),
    )
    ffn_grads = jnp.concatenate([up, down, tail], axis=2)
    if links.square:
        ffn_grads, grad_pre_b = sync(ffn_grads, grad_pre_b)
        ffn_x = links.across(ffn_grads[1:3, :2], 1)
        ffn_y = links.across(ffn_grads[2:4, 2:], 2)
    hid_sent, hid_part = nn(grad_pre_b[HALF:], w_up), nn(grad_pre_b[:HALF], w_up)
    grad_hid = hid_part + links.other_half(hid_sent)

    grad_hidden = grad_second + grad_hid * (jnp.abs(hidden) <= act_scale[2]).astype(F32)
    grad_gain_attn = jnp.sum(grad_hidden * normed_attn, axis=0, keepdims=True)
    grad_shift_attn = jnp.sum(grad_hidden, axis=0, keepdims=True)
    grad_first = norm_backward(grad_hidden, normed_attn, inverse_attn, gain_first)
    grad_b_out = jnp.sum(grad_first, axis=0, keepdims=True)
    grad_attn = grad_first.astype(BF16)
    go_other = links.other_half(grad_attn)
    sums = [grad_b_out, grad_gain_attn, grad_shift_attn, grad_b_down, grad_gain_ffn, grad_shift_ffn]
    sums = jnp.concatenate([*sums, maxima, jnp.zeros((1, width), F32)])

    def back(first, count, before):
        return attend_back(
            first,
            count,
            before,
            proj,
            grad_attn,
            go_other,
            x_quant,
            x_other,
            w_back,
            context,
            lse,
            seg_col,
            seg_row,
            act_scale[1:2],
        )

    def bias_rows(pairs):
        return pairs.reshape(heads, 2, 2, 4, chunk).swapaxes(0, 1)

    if links.square:
        tall = 2 * heads * HEAD // 2
        many = heads - 1
        early, grad_w, early_b = back(0, many, None)
        early, go_other, ffn_x, ffn_y = sync(early, go_other, ffn_x, ffn_y)
        low = [ffn_grads[0, :2] + ffn_x[0].astype(F32), ffn_grads[3, :2] + ffn_x[1].astype(F32)]
        high = [ffn_grads[0, 2:] + ffn_y[1].astype(F32), ffn_grads[1, 2:] + ffn_y[0].astype(F32)]
        ffn_y, ffn_x = low[1].astype(BF16), high[1].astype(BF16)
        go_other, ffn_x, ffn_y = sync(go_other, ffn_x, ffn_y)
        ffn_y, ffn_x = links.across(ffn_y, 2), links.across(ffn_x, 1)
        late, grad_w, late_b = back(many, 1, grad_w)
        late, grad_w, late_b, ffn_x, ffn_y = sync(late, grad_w, late_b, ffn_x, ffn_y)
        sums = merge(sums, links.other_half(sums))
        bias_sums = links.natural(bias_rows(jnp.concatenate([early_b, late_b])))
        sums = jnp.concatenate([sums[:7], bias_sums.reshape(1, width)])
        sums_sent = exact_parts(sums)
        ffn_low = low[0] + ffn_y.astype(F32)
        ffn_in = links.along((high[0] + ffn_x.astype(F32)).astype(BF16), 2)
        proj_in = [
            links.across(jnp.concatenate([grad_w[step], sums_sent]), step) for step in (1, 2, 3)
        ]
        grad_proj, ffn_low = sync(jnp.concatenate([early, late], axis=1), ffn_low)
    else:
        grad_proj, grad_w, bias_sums = back(0, heads, None)
        bias_sums = bias_rows(bias_sums)
    x_sent, x_part = nn(grad_proj[HALF:], w_proj), nn(grad_proj[:HALF], w_proj)
    grad_x = x_part + links.other_half(x_sent)
    input_grad = grad_first + grad_x * (jnp.abs(x_full) <= act_scale[0]).astype(F32)
    input_part = input_grad.astype(BF16)

    if links.square:
        total = grad_w[0].astype(F32)
        for part in proj_in:
            total = total + part[: 2 * tall].astype(F32)
            sums = merge(sums, exact_sum(part[2 * tall :]))
        mine = jnp.where(links.even, total[:tall], total[tall:])
        other = jnp.where(links.even, total[tall:], total[:tall])
        sums_sent = exact_parts(sums)
        other = jnp.concatenate([other.astype(BF16), sums_sent])
        proj_in = [
            links.pair_near(other),
            links.pair_back(jnp.concatenate([mine.astype(BF16), sums_sent])),
            links.pair_cross(other),
        ]
        ffn_in, total = sync(ffn_in, total)
        ffn_low = ffn_low + ffn_in.astype(F32)
        ffn_in = links.along(ffn_low[1].astype(BF16), 1)
        for part in proj_in:
            mine = mine + part[:tall].astype(F32)
            sums = merge(sums, exact_sum(part[tall:]))
        mine, input_part = sync(mine.astype(BF16), input_part)
        proj_all = links.spread(mine, lambda c, z: z // 2 == c)
        ffn_mine = (ffn_low[0] + ffn_in.astype(F32)).astype(BF16)
        ffn_all = links.spread(ffn_mine)
        proj_all, ffn_all = sync(proj_all, ffn_all)
        proj_all = jnp.concatenate([*proj_all, exact_parts(sums)])
        proj_other = links.other_half(proj_all)
        sums = exact_sum(jnp.where(links.inside, proj_all[4 * tall :], proj_other[4 * tall :]))
        grad_qkv, grad_out = unpack(links.inside, links.plane, proj_all, proj_other, tall)
        grad_qkv = jnp.swapaxes(grad_qkv, 1, 2)
        ffn_all = links.halves_in_order(links.in_order(ffn_all))
    else:
        ffn_all = plain_all(links, ffn_grads.swapaxes(0, 1))
        grads = plain_pair(links, grad_w.reshape(4, 2, -1, width))
        grads = grads.reshape(4, heads, 4, chunk, width).transpose(2, 1, 0, 3, 4)
        grads = grads.reshape(4, local, width)
        grad_qkv, grad_out = jnp.swapaxes(grads[:3], 1, 2), grads[3]
        sums = jnp.concatenate([lax.psum(sums[:6], JOINT), lax.pmax(sums[6:7], JOINT)])
        both = jnp.zeros((4, 2, local), F32)
        both = lax.dynamic_update_slice_in_dim(
            both, bias_sums.reshape(2, 2, local).swapaxes(0, 1), 2 * links.half, 0
        )
        both = lax.psum(both, JOINT)
        both = lax.dynamic_slice_in_dim(both, links.depth - links.depth % 2, 2, 0)
        sums = jnp.concatenate([sums, both.swapaxes(0, 1).reshape(1, width)])
    input_grad = links.at_home(input_part, links.rows_home(input_part)).astype(F32)
    maxima = sums[6, :4]
    new_scale = DECAY * act_scale + (1.0 - DECAY) * maxima

    up_grads, down_grads = ffn_all[:, :, :quarter], ffn_all[:, :, quarter : 2 * quarter]
    grad_bias_qv = lax.dynamic_index_in_dim(
        sums[7].reshape(2, 2, local), links.depth % 2, 1, False
    )
    return (
        links.at_home(final, layer_output),
        input_grad,
        grad_qkv,
        grad_bias_qv,
        grad_out,
        sums[0],
        sums[1],
        sums[2],
        up_grads.reshape(units, width).astype(F32).T,
        ffn_all[:, :, 2 * quarter, :quarter].reshape(units).astype(F32),
        down_grads.reshape(units, width).astype(F32),
        sums[3],
        sums[4],
        sums[5],
        new_scale,
        maxima,
    )


def solution(mesh):
    in_specs = (
        P(("dp", "tensor"), None),
        P("dp"),
        P(None, None, "tensor"),
        P(None, "tensor"),
        P("tensor", None),
        P(),
        P(),
        P(),
        P(None, "tensor"),
        P("tensor"),
        P("tensor", None),
        P(),
        P(),
        P(),
        P(),
        P(("dp", "tensor"), None),
    )
    out_specs = (
        P(("dp", "tensor"), None),
        P(("dp", "tensor"), None),
        P(None, None, "tensor"),
        P(None, "tensor"),
        P("tensor", None),
        P(),
        P(),
        P(),
        P(None, "tensor"),
        P("tensor"),
        P("tensor", None),
        P(),
        P(),
        P(),
        P(),
        P(),
    )
    sizes = (mesh.shape["dp"], mesh.shape["tensor"])
    return jax.shard_map(
        functools.partial(on_device, sizes),
        mesh=mesh,
        in_specs=in_specs,
        out_specs=out_specs,
        check_vma=False,
    )
```

```python
import functools
import math

import jax
import jax.numpy as jnp
from jax import lax
from jax.experimental import pallas as pl
from jax.experimental.pallas import tpu as pltpu
from jax.sharding import PartitionSpec as P

HEAD = 64
LEN = 1024
HALF = LEN // 2
BLOCK = 256

EPSILON = 1e-12
DECAY = 0.9999
MASKED = -1e30
ORDER = (0, 1, 3, 2)
JOINT = ("dp", "tensor")
BF16 = jnp.bfloat16
F32 = jnp.float32


def norm_forward(resid, gain, shift):
    row_mean = jnp.mean(resid, axis=-1, keepdims=True)
    centred = resid - row_mean
    spread = jnp.mean(centred * centred, axis=-1, keepdims=True)
    inverse = lax.rsqrt(spread + EPSILON)
    normed = centred * inverse
    return (normed * gain + shift, normed, inverse)


def norm_backward(upstream, normed, inverse, gain):
    scaled = upstream * gain
    mean_first = jnp.mean(scaled, axis=-1, keepdims=True)
    mean_second = jnp.mean(scaled * normed, axis=-1, keepdims=True)
    return inverse * (scaled - mean_first - normed * mean_second)


def nt(a, b):
    return lax.dot_general(a, b, (((1,), (1,)), ((), ())), preferred_element_type=F32)


def nn(a, b):
    return lax.dot_general(a, b, (((1,), (0,)), ((), ())), preferred_element_type=F32)


def tn(a, b):
    return lax.dot_general(a, b, (((0,), (0,)), ((), ())), preferred_element_type=F32)


def attend_kernel(q_ref, k_ref, v_ref, seg_col_ref, seg_row_ref, ctx_ref, lse_ref):
    low = lax.broadcasted_iota(jnp.int32, (BLOCK, 2 * HEAD), 1) < HEAD
    keys = k_ref[...]
    values = v_ref[...]
    for block in range(LEN // BLOCK):
        rows = pl.ds(block * BLOCK, BLOCK)
        queries = q_ref[rows, :] * jnp.asarray(HEAD**-0.5, BF16)
        same = seg_col_ref[rows, :] == seg_row_ref[...]
        parts, logs = [], []
        for head in range(2):
            own = low if head == 0 else jnp.logical_not(low)
            scores = nt(jnp.where(own, queries, jnp.zeros_like(queries)), keys)
            scores = jnp.where(same, scores, MASKED)
            top = jnp.max(scores, axis=-1, keepdims=True)
            exponent = jnp.exp(scores - top)
            total = jnp.sum(exponent, axis=-1, keepdims=True)
            attention = (exponent * (1.0 / total)).astype(BF16)
            parts.append(nn(attention, values))
            logs.append(top + jnp.log(total))
        ctx_ref[rows, :] = jnp.where(low, parts[0], parts[1])
        lse_ref[0, :, rows] = jnp.transpose(jnp.concatenate(logs, axis=1))


def attention_cost(pairs_of_heads, products):
    scores = 2 * pairs_of_heads * LEN * LEN
    return pl.CostEstimate(
        flops=2 * 4 * HEAD * products * scores,
        transcendentals=scores,
        bytes_accessed=8 * pairs_of_heads * LEN * HEAD * products,
    )


def attend(proj, seg_col, seg_row, pairs_of_heads):
    n = pairs_of_heads
    return pl.pallas_call(
        attend_kernel,
        grid=(n,),
        in_specs=[
            pl.BlockSpec((LEN, 2 * HEAD), lambda i: (0, 3 * i)),
            pl.BlockSpec((LEN, 2 * HEAD), lambda i: (0, 3 * i + 1)),
            pl.BlockSpec((LEN, 2 * HEAD), lambda i: (0, 3 * i + 2)),
            pl.BlockSpec((LEN, 1), lambda i: (0, 0)),
            pl.BlockSpec((1, LEN), lambda i: (0, 0)),
        ],
        out_specs=[
            pl.BlockSpec((LEN, 2 * HEAD), lambda i: (0, i)),
            pl.BlockSpec((1, 2, LEN), lambda i: (i, 0, 0)),
        ],
        out_shape=[
            jax.ShapeDtypeStruct((LEN, n * 2 * HEAD), F32),
            jax.ShapeDtypeStruct((n, 2, LEN), F32),
        ],
        name="attend",
    )(proj, proj, proj, seg_col, seg_row)


def attend_back_kernel(
    q_ref,
    k_ref,
    v_ref,
    go_ref,
    go_other_ref,
    x_ref,
    x_other_ref,
    back_ref,
    ctx_ref,
    lse_ref,
    seg_col_ref,
    seg_row_ref,
    limit_ref,
    grad_ref,
    pack_ref,
    sum_ref,
    acc_ref,
    grads_ref,
    quant_ref,
    inner_ref,
):
    low = lax.broadcasted_iota(jnp.int32, (BLOCK, 2 * HEAD), 1) < HEAD
    limit = limit_ref[0]
    for half, rows_ref in enumerate((go_ref, go_other_ref)):
        for block in range(HALF // BLOCK):
            rows = pl.ds(half * HALF + block * BLOCK, BLOCK)
            context = ctx_ref[rows, :]
            quant_ref[rows, :] = jnp.clip(context, -limit, limit).astype(BF16)
            grad = nt(rows_ref[pl.ds(block * BLOCK, BLOCK), :], back_ref[...])
            grad = jnp.where(jnp.abs(context) <= limit, grad, 0.0).astype(BF16)
            grads_ref[rows, :] = grad
            both = grad.astype(F32) * context
            inner = [
                jnp.sum(jnp.where(own, both, 0.0), axis=1, keepdims=True)
                for own in (low, jnp.logical_not(low))
            ]
            inner_ref[:, rows] = jnp.transpose(jnp.concatenate(inner, axis=1))
    queries = q_ref[...]
    grads = grads_ref[...]
    value_sum = jnp.zeros((1, 2 * HEAD), F32)
    for block in range(LEN // BLOCK):
        rows = pl.ds(block * BLOCK, BLOCK)
        keys = k_ref[rows, :]
        scaled_keys = keys * jnp.asarray(HEAD**-0.5, BF16)
        values = v_ref[rows, :]
        same = seg_col_ref[rows, :] == seg_row_ref[...]
        value_parts, key_parts = [], []
        for head in range(2):
            own = low if head == 0 else jnp.logical_not(low)
            zero = jnp.zeros_like(keys)
            scores = nt(jnp.where(own, scaled_keys, zero), queries)
            logs = lse_ref[0, head : head + 1, :]
            attention = jnp.where(same, jnp.exp(scores - logs), 0.0)
            value_parts.append(nn(attention.astype(BF16), grads))
            grad_attention = nt(jnp.where(own, values, zero), grads)
            inner = inner_ref[head : head + 1, :]
            grad_score = (attention * (grad_attention - inner) * HEAD**-0.5).astype(BF16)
            key_parts.append(nn(grad_score, queries))
            part = tn(grad_score, jnp.where(own, keys, zero))
            if block == 0 and head == 0:
                acc_ref[...] = part
            else:
                acc_ref[...] += part
        grad_value = jnp.where(low, value_parts[0], value_parts[1])
        value_sum += jnp.sum(grad_value, axis=0, keepdims=True)
        grad_ref[rows, 4 * HEAD :] = grad_value.astype(BF16)
        grad_ref[rows, 2 * HEAD : 4 * HEAD] = jnp.where(low, key_parts[0], key_parts[1]).astype(BF16)
    grad_query = acc_ref[...]
    grad_ref[:, : 2 * HEAD] = grad_query.astype(BF16)
    sum_ref[0, 0:1, :] = jnp.sum(grad_query, axis=0, keepdims=True)
    sum_ref[0, 1:2, :] = value_sum
    chunk = HEAD // 4
    sides = ((slice(0, HALF), x_ref, go_ref), (slice(HALF, LEN), x_other_ref, go_other_ref))
    for kind in range(4):
        lanes = slice(2 * kind * HEAD, 2 * (kind + 1) * HEAD)
        total = None
        for rows, x_side, go_side in sides:
            if kind < 3:
                part = tn(grad_ref[rows, lanes], x_side[...])
            else:
                part = tn(quant_ref[rows, :], go_side[...])
            total = part if total is None else total + part
        total = total.astype(BF16)
        for head in range(2):
            for j in range(4):
                at = head * HEAD + j * chunk
                into = (head * 4 + kind) * chunk
                pack_ref[j, into : into + chunk, :] = total[at : at + chunk, :]


def attend_back(
    first, n, before, proj, go, go_other, x, x_other, w_back, context, lse, seg_col, seg_row, limit
):
    width = w_back.shape[1]
    earlier = [] if before is None else [before]

    def body(*refs):
        attend_back_kernel(*refs[:13], *refs[13 + len(earlier) :])

    def whole(array):
        return pl.BlockSpec(array.shape, lambda i: (0,) * array.ndim)

    return pl.pallas_call(
        body,
        grid=(n,),
        in_specs=[
            pl.BlockSpec((LEN, 2 * HEAD), lambda i: (0, 3 * (first + i))),
            pl.BlockSpec((LEN, 2 * HEAD), lambda i: (0, 3 * (first + i) + 1)),
            pl.BlockSpec((LEN, 2 * HEAD), lambda i: (0, 3 * (first + i) + 2)),
            *[whole(array) for array in (go, go_other, x, x_other)],
            pl.BlockSpec((2 * HEAD, width), lambda i: (first + i, 0)),
            pl.BlockSpec((LEN, 2 * HEAD), lambda i: (0, first + i)),
            pl.BlockSpec((1, 2, LEN), lambda i: (first + i, 0, 0)),
            whole(seg_col),
            whole(seg_row),
            pl.BlockSpec(memory_space=pltpu.SMEM),
            *[pl.BlockSpec(memory_space=pl.ANY) for _ in earlier],
        ],
        out_specs=[
            pl.BlockSpec((LEN, 6 * HEAD), lambda i: (0, i)),
            pl.BlockSpec((4, 2 * HEAD, width), lambda i: (0, first + i, 0)),
            pl.BlockSpec((1, 2, 2 * HEAD), lambda i: (i, 0, 0)),
        ],
        out_shape=[
            jax.ShapeDtypeStruct((LEN, n * 6 * HEAD), BF16),
            jax.ShapeDtypeStruct((4, *w_back.shape), BF16),
            jax.ShapeDtypeStruct((n, 2, 2 * HEAD), F32),
        ],
        scratch_shapes=[
            pltpu.VMEM((LEN, 2 * HEAD), F32),
            pltpu.VMEM((LEN, 2 * HEAD), BF16),
            pltpu.VMEM((LEN, 2 * HEAD), BF16),
            pltpu.VMEM((2, LEN), F32),
        ],
        cost_estimate=attention_cost(n, 9) if first else None,
        input_output_aliases={13: 1} if earlier else {},
        name="attend_back",
    )(
        *(proj, proj, proj, go, go_other, x, x_other, w_back, context, lse),
        *(seg_col, seg_row, limit, *earlier),
    )


def unpack_kernel(plane_ref, *refs):
    pieces, (qkv_ref, out_ref) = refs[:4], refs[4:]
    kind = pl.program_id(0)
    chunk = HEAD // 4
    heads = pieces[0].shape[0] // HEAD

    for plane in range(4):

        @pl.when(plane_ref[0] == plane)
        def _(plane=plane):
            parts = []
            for head in range(heads):
                at = pl.multiple_of(head * HEAD + kind * chunk, chunk)
                parts += [pieces[j ^ plane][pl.ds(at, chunk), :] for j in range(4)]
            rows = jnp.concatenate(parts, axis=0).astype(F32)

            @pl.when(kind < 3)
            def _():
                qkv_ref[0] = rows

            @pl.when(kind == 3)
            def _():
                out_ref[...] = rows


def unpack(plane, pieces):
    tall, width = pieces[0].shape
    return pl.pallas_call(
        unpack_kernel,
        grid=(4,),
        in_specs=[
            pl.BlockSpec(memory_space=pltpu.SMEM),
            *[pl.BlockSpec((tall, width), lambda i: (0, 0)) for _ in pieces],
        ],
        out_specs=[
            pl.BlockSpec((1, tall, width), lambda i: (jnp.minimum(i, 2), 0, 0)),
            pl.BlockSpec((tall, width), lambda i: (0, 0)),
        ],
        out_shape=[
            jax.ShapeDtypeStruct((3, tall, width), F32),
            jax.ShapeDtypeStruct((tall, width), F32),
        ],
        name="unpack",
    )(plane[None], *pieces)


def unpack_ffn_kernel(where_ref, own_ref, other_ref, up_ref, down_ref):
    half, plane = where_ref[0], where_ref[1]
    quarter = up_ref.shape[1] // 4

    def rows_of(ref, first):
        parts = [ref[j ^ plane, first : first + quarter, :] for j in range(4)]
        return jnp.concatenate(parts, axis=0).astype(F32)

    for mine, ref in ((True, own_ref), (False, other_ref)):

        @pl.when((pl.program_id(0) == half) == mine)
        def _(ref=ref):
            up_ref[...] = jnp.transpose(rows_of(ref, 0))
            down_ref[...] = rows_of(ref, quarter)


def unpack_ffn(half, plane, own, other, quarter):
    width = own.shape[2]
    return pl.pallas_call(
        unpack_ffn_kernel,
        grid=(2,),
        in_specs=[
            pl.BlockSpec(memory_space=pltpu.SMEM),
            pl.BlockSpec(own.shape, lambda i: (0, 0, 0)),
            pl.BlockSpec(own.shape, lambda i: (0, 0, 0)),
        ],
        out_specs=[
            pl.BlockSpec((width, 4 * quarter), lambda i: (0, i)),
            pl.BlockSpec((4 * quarter, width), lambda i: (i, 0)),
        ],
        out_shape=[
            jax.ShapeDtypeStruct((width, 8 * quarter), F32),
            jax.ShapeDtypeStruct((8 * quarter, width), F32),
        ],
        name="unpack_ffn",
    )(jnp.stack([half, plane]), own, other)


class Links:
    def __init__(self, dp, depths):
        self.dp, self.depths = dp, depths
        self.planes = dp // 2
        place = lax.axis_index("dp")
        self.half, self.plane = place % 2, place // 2
        self.depth = lax.axis_index("tensor")
        self.square = self.planes == 4 and depths == 4

    def permute(self, array, move):
        pairs = []
        for place in range(self.dp):
            for depth in range(self.depths):
                to = move(place // 2, place % 2, depth)
                if to is not None:
                    plane, half, level = to
                    pairs.append(
                        (place * self.depths + depth, (2 * plane + half) * self.depths + level)
                    )
        return lax.ppermute(array, JOINT, pairs)

    def rows_home(self, array):
        return self.permute(
            array, lambda e, c, z: (e, z % 2, z - z % 2 + c) if c != z % 2 else None
        )

    def at_home(self, own, moved):
        return jnp.where(self.depth % 2 == self.half, own, moved)

    def other_half(self, array):
        return self.permute(array, lambda e, c, z: (e, 1 - c, z))

    def across(self, array, step, only=None):
        return self.permute(
            array,
            lambda e, c, z: (e ^ step, c, z) if only is None or only(c, z) else None,
        )

    def along(self, array, step):
        return self.permute(array, lambda e, c, z: (e, c, z ^ step))

    def spread_near(self, piece, only=None):
        return self.across(piece, 1, only), self.across(piece, 2, only)

    def spread_far(self, piece, near, only=None):
        first, second = near
        cut = piece.shape[-2] // 16 * 8
        third_low = self.across(second[..., :cut, :], 1, only)
        third_high = self.across(first[..., cut:, :], 2, only)
        return [piece, first, second, jnp.concatenate([third_low, third_high], axis=-2)]

    def spread(self, piece, only=None):
        return [piece] + [self.across(piece, step, only) for step in (1, 2, 3)]

    def in_order(self, pieces):
        stack = jnp.stack(pieces)
        return jnp.stack(
            [lax.dynamic_index_in_dim(stack, j ^ self.plane, 0, False) for j in range(4)]
        )

    @property
    def inside(self):
        return self.depth // 2 == self.half

    @property
    def even(self):
        return self.depth % 2 == 0

    def pair_near(self, array):
        return self.permute(array, lambda e, c, z: (e, c, z ^ 1) if z // 2 == c else None)

    def pair_out(self, array):
        def far(step):
            return lambda e, c, z: (e, c, z ^ step) if z // 2 == c else None

        return [self.permute(array, far(step)) for step in (2, 3, 1)]

    def pair_of(self, mine, arrived):
        same, cross, near = arrived
        a = jnp.where(self.inside, mine, same)
        b = jnp.where(self.inside, near, cross)
        return self.even_first(a, b)

    def pair_back(self, array):
        return self.permute(array, lambda e, c, z: (e, c, z ^ 2) if z // 2 != c else None)

    def pair_cross(self, array):
        return self.permute(array, lambda e, c, z: (e, c, z ^ 3) if z // 2 != c else None)

    def halves_in_order(self, mine, other):
        first = self.half == 0
        return jnp.stack([jnp.where(first, mine, other), jnp.where(first, other, mine)])

    def natural(self, array):
        swapped = array[..., jnp.array([1, 0, 3, 2]), :]
        array = jnp.where(self.plane % 2 == 1, swapped, array)
        swapped = array[..., jnp.array([2, 3, 0, 1]), :]
        return jnp.where(self.plane // 2 == 1, swapped, array)

    def even_first(self, mine, other):
        return jnp.stack([jnp.where(self.even, mine, other), jnp.where(self.even, other, mine)])


def exact_parts(values):
    high = lax.reduce_precision(values, 8, 7)
    rest = values - high
    middle = lax.reduce_precision(rest, 8, 7)
    return jnp.concatenate([high, middle, rest - middle]).astype(BF16)


def exact_sum(parts):
    rows = parts.shape[0] // 3
    parts = parts.astype(F32)
    return parts[:rows] + parts[rows : 2 * rows] + parts[2 * rows :]


def merge(both, other):
    last = lax.broadcasted_iota(jnp.int32, both.shape, 0) == 6
    return jnp.where(last, jnp.maximum(both, other), both + other)


def sync(*values):
    return lax.optimization_barrier(values)


def plain_all(links, grads):
    blank = jnp.zeros((4, 2) + grads.shape[1:], F32)
    full = lax.dynamic_update_slice_in_dim(blank, grads[:, None].astype(F32), links.half, 1)
    shard = lax.psum_scatter(full, "tensor", scatter_dimension=0, tiled=False)
    return lax.psum(shard, "dp")


def plain_pair(links, grads):
    blank = jnp.zeros((4,) + grads.shape[:1] + grads.shape[2:], F32)
    own = grads.swapaxes(0, 1).astype(F32)
    full = lax.dynamic_update_slice_in_dim(blank, own, 2 * links.half, 0)
    shard = lax.psum_scatter(full, "tensor", scatter_dimension=0, tiled=False)
    return lax.psum(shard, "dp")


def on_device(
    sizes,
    layer_input,
    segments,
    w_qkv,
    bias_qv,
    w_out,
    b_out,
    gain_attn,
    shift_attn,
    w_in,
    b_in,
    w_down,
    b_down,
    gain_ffn,
    shift_ffn,
    act_scale,
    out_grad,
):
    links = Links(*sizes)
    width = layer_input.shape[1]
    local = w_qkv.shape[2]
    heads = local // HEAD
    chunk = HEAD // 4
    units = w_in.shape[1]
    quarter = units // 8
    gain_first = gain_attn.astype(F32)
    gain_second = gain_ffn.astype(F32)

    per = 3 * heads * chunk
    more = heads * chunk

    rows = jnp.concatenate([jnp.swapaxes(w_qkv, 1, 2), w_out[None]])
    rows = rows.reshape(4, heads, 4, chunk, width)
    rows = rows.transpose(2, 0, 1, 3, 4).reshape(4, per + more, width)
    tail = bias_qv.reshape(2, heads, 4, chunk).transpose(2, 0, 1, 3).reshape(4, 1, 2 * more)
    tail = jnp.pad(tail, ((0, 0), (0, 7), (0, width - tail.shape[2])))
    attn_pack = jnp.concatenate([rows, tail], axis=1)
    if links.square:
        attn_mine = lax.dynamic_index_in_dim(attn_pack, links.plane, 0, False)
        attn_in = links.pair_out(attn_mine)
    seg_rows = segments.reshape(2, LEN)
    seg_mine = lax.dynamic_index_in_dim(seg_rows, links.depth // 2, 0, False).reshape(8, LEN // 8)
    seg_next = links.other_half(seg_mine)
    seg_home = links.at_home(seg_mine, seg_next).reshape(2, HALF)
    seg_home = jnp.where(links.half == 0, seg_home, seg_home[::-1]).reshape(LEN)
    seg_col, seg_row = seg_home[:, None], seg_home[None, :]
    ffn_half = jnp.concatenate(
        [
            lax.dynamic_index_in_dim(w_in.T.reshape(2, 4, quarter, width), links.half, 0, False),
            lax.dynamic_index_in_dim(w_down.reshape(2, 4, quarter, width), links.half, 0, False),
            jnp.pad(
                lax.dynamic_index_in_dim(b_in.reshape(2, 4, 1, quarter), links.half, 0, False),
                ((0, 0), (0, 7), (0, width - quarter)),
            ),
        ],
        axis=1,
    )
    if links.square:
        ffn_own = jnp.stack(
            [lax.dynamic_index_in_dim(ffn_half, j ^ links.plane, 0, False) for j in ORDER]
        )
        attn_in, ffn_mine, x_home = sync(attn_in, ffn_own[0], layer_input)
        attn_both = links.pair_of(attn_mine, attn_in)
        attn_near = links.spread_near(attn_both)
        x_home = links.rows_home(x_home)
        ffn_two = links.along(ffn_mine, 2)
        attn_near, ffn_two, ffn_mine = sync(attn_near, ffn_two, ffn_mine)
        attn_full = jnp.stack(links.spread_far(attn_both, attn_near))
        ffn_in = jnp.stack([links.along(ffn_mine, 1), ffn_two, links.along(ffn_mine, 3)])
    else:
        attn_full = lax.all_gather(attn_pack, "tensor", axis=0, tiled=False)
        attn_full = lax.dynamic_slice_in_dim(attn_full, 2 * links.half, 2, 0).swapaxes(0, 1)
        ffn_in = lax.all_gather(ffn_half, "tensor", axis=0, tiled=False)
        x_home = links.rows_home(layer_input)
    x_home = links.at_home(layer_input, x_home)

    x_full = x_home.astype(F32)
    x_quant = jnp.clip(x_full, -act_scale[0], act_scale[0]).astype(BF16)
    x_other = links.other_half(x_quant)
    x_rows = jnp.concatenate([x_quant, x_other])

    weights = attn_full[:, :, : per + more].reshape(4, 2, 4, heads, chunk, width)
    weights = weights.transpose(2, 1, 3, 0, 4, 5).reshape(4, heads, 2 * HEAD, width)
    w_proj = weights[:3].swapaxes(0, 1).reshape(6 * local, width)
    w_back = weights[3].reshape(2 * local, width)
    biases = attn_full[:, :, per + more, : 2 * more].reshape(4, 2, 2, heads, chunk)
    biases = biases.transpose(2, 1, 3, 0, 4).reshape(2, 2 * local).astype(F32)
    bias_all = jnp.stack([biases[0], jnp.zeros_like(biases[0]), biases[1]])
    bias_all = bias_all.reshape(3, heads, 2 * HEAD).swapaxes(0, 1).reshape(6 * local)

    proj = (nt(x_rows, w_proj) + bias_all).astype(BF16)
    proj, ffn_in, out_grad = sync(proj, ffn_in, out_grad)
    if links.square:
        ffn_near = links.spread_near(ffn_in)
    upstream = links.rows_home(out_grad)
    context, lse = attend(proj, seg_col, seg_row, heads)
    context, upstream = sync(context, upstream)
    upstream = links.at_home(out_grad, upstream).astype(F32)
    ctx_quant = jnp.clip(context, -act_scale[1], act_scale[1]).astype(BF16)
    attn_part, attn_sent = nn(ctx_quant[:HALF], w_back), nn(ctx_quant[HALF:], w_back)
    if links.square:
        attn_part, attn_sent, ffn_near = sync(attn_part, attn_sent, ffn_near)
        pieces = links.spread_far(ffn_in, ffn_near)
        ffn_full = jnp.stack(
            [jnp.concatenate([ffn_own[i][None], pieces[j]]) for i, j in enumerate(ORDER)]
        )
    else:
        ffn_full = ffn_in.swapaxes(0, 1)
    attn_out = attn_part + links.other_half(attn_sent) + b_out.astype(F32)
    hidden, normed_attn, inverse_attn = norm_forward(
        x_full + attn_out, gain_first, shift_attn.astype(F32)
    )
    hid_quant = jnp.clip(hidden, -act_scale[2], act_scale[2]).astype(BF16)
    hid_other = links.other_half(hid_quant)
    tops = [jnp.max(jnp.abs(array)) for array in (x_full, context, hidden)]
    hid_other, tops = sync(hid_other, tops)
    hid_rows = jnp.concatenate([hid_quant, hid_other])

    w_up = ffn_full[:, :, :quarter].reshape(2 * units, width)
    w_low = ffn_full[:, :, quarter : 2 * quarter].reshape(2 * units, width)
    b_up = ffn_full[:, :, 2 * quarter, :quarter].reshape(2 * units).astype(F32)
    pre_act = nt(hid_rows, w_up) + b_up
    normal_cdf = 0.5 * (1.0 + lax.erf(pre_act * 0.5**0.5))
    activated = pre_act * normal_cdf
    slope = normal_cdf + pre_act * jnp.exp(-0.5 * pre_act * pre_act) / math.sqrt(2.0 * math.pi)
    slope = jnp.where(jnp.abs(activated) <= act_scale[3], slope, 0.0)
    act_quant = jnp.clip(activated, -act_scale[3], act_scale[3]).astype(BF16)
    ffn_sent, ffn_part = nn(act_quant[HALF:], w_low), nn(act_quant[:HALF], w_low)
    ffn_out = ffn_part + links.other_half(ffn_sent)
    final, normed_ffn, inverse_ffn = norm_forward(
        hidden + ffn_out + b_down.astype(F32), gain_second, shift_ffn.astype(F32)
    )
    final = final.astype(BF16)
    layer_output = links.rows_home(final)
    lanes = lax.broadcasted_iota(jnp.int32, (1, width), 1)
    maxima = jnp.zeros((1, width), F32)
    for at, value in enumerate((*tops, jnp.max(jnp.abs(activated)))):
        maxima = jnp.where(lanes == at, value, maxima)

    grad_gain_ffn = jnp.sum(upstream * normed_ffn, axis=0, keepdims=True)
    grad_shift_ffn = jnp.sum(upstream, axis=0, keepdims=True)
    grad_second = norm_backward(upstream, normed_ffn, inverse_ffn, gain_second)
    grad_b_down = jnp.sum(grad_second, axis=0, keepdims=True)
    grad_final = grad_second.astype(BF16)
    grad_rows = jnp.concatenate([grad_final, links.other_half(grad_final)])
    down = tn(act_quant, grad_rows).astype(BF16).reshape(4, 4, quarter, width)
    grad_pre = nt(grad_rows, w_low) * slope
    grad_b_in = jnp.sum(grad_pre, axis=0)
    grad_pre_b = grad_pre.astype(BF16)
    up = tn(grad_pre_b, hid_rows).astype(BF16).reshape(4, 4, quarter, width)
    tail = jnp.pad(
        grad_b_in.astype(BF16).reshape(4, 4, 1, quarter),
        ((0, 0), (0, 0), (0, 7), (0, width - quarter)),
    )
    ffn_grads = jnp.concatenate([up, down, tail], axis=2)
    if links.square:
        ffn_grads, grad_pre_b = sync(ffn_grads, grad_pre_b)
        ffn_x = links.across(ffn_grads[1:3, :2], 1)
        ffn_y = links.across(ffn_grads[2:4, 2:], 2)
    hid_sent, hid_part = nn(grad_pre_b[HALF:], w_up), nn(grad_pre_b[:HALF], w_up)
    grad_hid = hid_part + links.other_half(hid_sent)

    grad_hidden = grad_second + grad_hid * (jnp.abs(hidden) <= act_scale[2]).astype(F32)
    grad_gain_attn = jnp.sum(grad_hidden * normed_attn, axis=0, keepdims=True)
    grad_shift_attn = jnp.sum(grad_hidden, axis=0, keepdims=True)
    grad_first = norm_backward(grad_hidden, normed_attn, inverse_attn, gain_first)
    grad_b_out = jnp.sum(grad_first, axis=0, keepdims=True)
    grad_attn = grad_first.astype(BF16)
    go_other = links.other_half(grad_attn)
    sums = [grad_b_out, grad_gain_attn, grad_shift_attn, grad_b_down, grad_gain_ffn, grad_shift_ffn]
    sums = jnp.concatenate([*sums, maxima, jnp.zeros((1, width), F32)])

    def back(first, count, before):
        return attend_back(
            first,
            count,
            before,
            proj,
            grad_attn,
            go_other,
            x_quant,
            x_other,
            w_back,
            context,
            lse,
            seg_col,
            seg_row,
            act_scale[1:2],
        )

    def bias_rows(pairs):
        return pairs.reshape(heads, 2, 2, 4, chunk).swapaxes(0, 1)

    if links.square:
        tall = 2 * heads * HEAD // 2
        many = heads - 1
        early, grad_w, early_b = back(0, many, None)
        early, go_other, ffn_x, ffn_y = sync(early, go_other, ffn_x, ffn_y)
        low = [ffn_grads[0, :2] + ffn_x[0].astype(F32), ffn_grads[3, :2] + ffn_x[1].astype(F32)]
        high = [ffn_grads[0, 2:] + ffn_y[1].astype(F32), ffn_grads[1, 2:] + ffn_y[0].astype(F32)]
        ffn_y, ffn_x = low[1].astype(BF16), high[1].astype(BF16)
        go_other, ffn_x, ffn_y = sync(go_other, ffn_x, ffn_y)
        ffn_y, ffn_x = links.across(ffn_y, 2), links.across(ffn_x, 1)
        late, grad_w, late_b = back(many, 1, grad_w)
        late, grad_w, late_b, ffn_x, ffn_y = sync(late, grad_w, late_b, ffn_x, ffn_y)
        sums = merge(sums, links.other_half(sums))
        bias_sums = links.natural(bias_rows(jnp.concatenate([early_b, late_b])))
        sums = jnp.concatenate([sums[:7], bias_sums.reshape(1, width)])
        sums_sent = exact_parts(sums)
        ffn_low = low[0] + ffn_y.astype(F32)
        ffn_in = links.along((high[0] + ffn_x.astype(F32)).astype(BF16), 2)
        proj_in = [
            links.across(jnp.concatenate([grad_w[step], sums_sent]), step) for step in (1, 2, 3)
        ]
        grad_proj, ffn_low = sync(jnp.concatenate([early, late], axis=1), ffn_low)
    else:
        grad_proj, grad_w, bias_sums = back(0, heads, None)
        bias_sums = bias_rows(bias_sums)
    x_sent, x_part = nn(grad_proj[HALF:], w_proj), nn(grad_proj[:HALF], w_proj)
    grad_x = x_part + links.other_half(x_sent)
    input_grad = grad_first + grad_x * (jnp.abs(x_full) <= act_scale[0]).astype(F32)
    input_part = input_grad.astype(BF16)

    if links.square:
        total = grad_w[0].astype(F32)
        for part in proj_in:
            total = total + part[: 2 * tall].astype(F32)
            sums = merge(sums, exact_sum(part[2 * tall :]))
        mine = jnp.where(links.even, total[:tall], total[tall:])
        other = jnp.where(links.even, total[tall:], total[:tall])
        sums_sent = exact_parts(sums)
        other = jnp.concatenate([other.astype(BF16), sums_sent])
        proj_in = [
            links.pair_near(other),
            links.pair_back(jnp.concatenate([mine.astype(BF16), sums_sent])),
            links.pair_cross(other),
        ]
        ffn_in, total = sync(ffn_in, total)
        ffn_low = ffn_low + ffn_in.astype(F32)
        ffn_in = links.along(ffn_low[1].astype(BF16), 1)
        for part in proj_in:
            mine = mine + part[:tall].astype(F32)
            sums = merge(sums, exact_sum(part[tall:]))
        mine, input_part = sync(mine.astype(BF16), input_part)
        sent = jnp.concatenate([mine, exact_parts(sums)])
        sent = jnp.where(links.inside, sent, links.other_half(sent))
        sums = exact_sum(sent[tall:])
        proj_all = links.spread(sent[:tall])
        ffn_mine = (ffn_low[0] + ffn_in.astype(F32)).astype(BF16)
        ffn_all = jnp.stack(links.spread(ffn_mine))
        ffn_other = links.other_half(ffn_all)
        proj_all, ffn_all, ffn_other = sync(proj_all, ffn_all, ffn_other)
        grad_qkv, grad_out = unpack(links.plane, proj_all)
        grad_qkv = jnp.swapaxes(grad_qkv, 1, 2)
        grad_in, grad_down = unpack_ffn(links.half, links.plane, ffn_all, ffn_other, quarter)
        grad_b_in = links.halves_in_order(
            links.in_order(list(ffn_all[:, 2 * quarter, :quarter])),
            links.in_order(list(ffn_other[:, 2 * quarter, :quarter])),
        ).reshape(units)
    else:
        ffn_all = plain_all(links, ffn_grads.swapaxes(0, 1))
        grad_in = ffn_all[:, :, :quarter].reshape(units, width).T
        grad_down = ffn_all[:, :, quarter : 2 * quarter].reshape(units, width)
        grad_b_in = ffn_all[:, :, 2 * quarter, :quarter].reshape(units)
        grads = plain_pair(links, grad_w.reshape(4, 2, -1, width))
        grads = grads.reshape(4, heads, 4, chunk, width).transpose(2, 1, 0, 3, 4)
        grads = grads.reshape(4, local, width)
        grad_qkv, grad_out = jnp.swapaxes(grads[:3], 1, 2), grads[3]
        sums = jnp.concatenate([lax.psum(sums[:6], JOINT), lax.pmax(sums[6:7], JOINT)])
        both = jnp.zeros((4, 2, local), F32)
        both = lax.dynamic_update_slice_in_dim(
            both, bias_sums.reshape(2, 2, local).swapaxes(0, 1), 2 * links.half, 0
        )
        both = lax.psum(both, JOINT)
        both = lax.dynamic_slice_in_dim(both, links.depth - links.depth % 2, 2, 0)
        sums = jnp.concatenate([sums, both.swapaxes(0, 1).reshape(1, width)])
    input_grad = links.at_home(input_part, links.rows_home(input_part)).astype(F32)
    maxima = sums[6, :4]
    new_scale = DECAY * act_scale + (1.0 - DECAY) * maxima

    grad_bias_qv = lax.dynamic_index_in_dim(
        sums[7].reshape(2, 2, local), links.depth % 2, 1, False
    )
    return (
        links.at_home(final, layer_output),
        input_grad,
        grad_qkv,
        grad_bias_qv,
        grad_out,
        sums[0],
        sums[1],
        sums[2],
        grad_in,
        grad_b_in.astype(F32),
        grad_down,
        sums[3],
        sums[4],
        sums[5],
        new_scale,
        maxima,
    )


def solution(mesh):
    in_specs = (
        P(("dp", "tensor"), None),
        P("dp"),
        P(None, None, "tensor"),
        P(None, "tensor"),
        P("tensor", None),
        P(),
        P(),
        P(),
        P(None, "tensor"),
        P("tensor"),
        P("tensor", None),
        P(),
        P(),
        P(),
        P(),
        P(("dp", "tensor"), None),
    )
    out_specs = (
        P(("dp", "tensor"), None),
        P(("dp", "tensor"), None),
        P(None, None, "tensor"),
        P(None, "tensor"),
        P("tensor", None),
        P(),
        P(),
        P(),
        P(None, "tensor"),
        P("tensor"),
        P("tensor", None),
        P(),
        P(),
        P(),
        P(),
        P(),
    )
    sizes = (mesh.shape["dp"], mesh.shape["tensor"])
    return jax.shard_map(
        functools.partial(on_device, sizes),
        mesh=mesh,
        in_specs=in_specs,
        out_specs=out_specs,
        check_vma=False,
    )
```

```python
import functools
import math

import jax
import jax.numpy as jnp
from jax import lax
from jax.experimental import pallas as pl
from jax.experimental.pallas import tpu as pltpu
from jax.sharding import PartitionSpec as P

HEAD = 64
LEN = 1024
HALF = LEN // 2
BLOCK = 256

EPSILON = 1e-12
DECAY = 0.9999
MASKED = -1e30
ORDER = (0, 1, 3, 2)
JOINT = ("dp", "tensor")
BF16 = jnp.bfloat16
F32 = jnp.float32


def norm_forward(resid, gain, shift):
    row_mean = jnp.mean(resid, axis=-1, keepdims=True)
    centred = resid - row_mean
    spread = jnp.mean(centred * centred, axis=-1, keepdims=True)
    inverse = lax.rsqrt(spread + EPSILON)
    normed = centred * inverse
    return (normed * gain + shift, normed, inverse)


def norm_backward(upstream, normed, inverse, gain):
    scaled = upstream * gain
    mean_first = jnp.mean(scaled, axis=-1, keepdims=True)
    mean_second = jnp.mean(scaled * normed, axis=-1, keepdims=True)
    return inverse * (scaled - mean_first - normed * mean_second)


def nt(a, b):
    return lax.dot_general(a, b, (((1,), (1,)), ((), ())), preferred_element_type=F32)


def nn(a, b):
    return lax.dot_general(a, b, (((1,), (0,)), ((), ())), preferred_element_type=F32)


def tn(a, b):
    return lax.dot_general(a, b, (((0,), (0,)), ((), ())), preferred_element_type=F32)


def attend_kernel(q_ref, k_ref, v_ref, seg_col_ref, seg_row_ref, ctx_ref, lse_ref):
    low = lax.broadcasted_iota(jnp.int32, (BLOCK, 2 * HEAD), 1) < HEAD
    keys = k_ref[...]
    values = v_ref[...]
    for block in range(LEN // BLOCK):
        rows = pl.ds(block * BLOCK, BLOCK)
        queries = q_ref[rows, :] * jnp.asarray(HEAD**-0.5, BF16)
        same = seg_col_ref[rows, :] == seg_row_ref[...]
        parts, logs = [], []
        for head in range(2):
            own = low if head == 0 else jnp.logical_not(low)
            scores = nt(jnp.where(own, queries, jnp.zeros_like(queries)), keys)
            scores = jnp.where(same, scores, MASKED)
            top = jnp.max(scores, axis=-1, keepdims=True)
            exponent = jnp.exp(scores - top)
            total = jnp.sum(exponent, axis=-1, keepdims=True)
            attention = (exponent * (1.0 / total)).astype(BF16)
            parts.append(nn(attention, values))
            logs.append(top + jnp.log(total))
        ctx_ref[rows, :] = jnp.where(low, parts[0], parts[1])
        lse_ref[0, :, rows] = jnp.transpose(jnp.concatenate(logs, axis=1))


def attention_cost(pairs_of_heads, products):
    scores = 2 * pairs_of_heads * LEN * LEN
    return pl.CostEstimate(
        flops=2 * 4 * HEAD * products * scores,
        transcendentals=scores,
        bytes_accessed=8 * pairs_of_heads * LEN * HEAD * products,
    )


def attend(proj, seg_col, seg_row, pairs_of_heads):
    n = pairs_of_heads
    return pl.pallas_call(
        attend_kernel,
        grid=(n,),
        in_specs=[
            pl.BlockSpec((LEN, 2 * HEAD), lambda i: (0, 3 * i)),
            pl.BlockSpec((LEN, 2 * HEAD), lambda i: (0, 3 * i + 1)),
            pl.BlockSpec((LEN, 2 * HEAD), lambda i: (0, 3 * i + 2)),
            pl.BlockSpec((LEN, 1), lambda i: (0, 0)),
            pl.BlockSpec((1, LEN), lambda i: (0, 0)),
        ],
        out_specs=[
            pl.BlockSpec((LEN, 2 * HEAD), lambda i: (0, i)),
            pl.BlockSpec((1, 2, LEN), lambda i: (i, 0, 0)),
        ],
        out_shape=[
            jax.ShapeDtypeStruct((LEN, n * 2 * HEAD), F32),
            jax.ShapeDtypeStruct((n, 2, LEN), F32),
        ],
        name="attend",
    )(proj, proj, proj, seg_col, seg_row)


def attend_back_kernel(
    q_ref,
    k_ref,
    v_ref,
    go_ref,
    go_other_ref,
    x_ref,
    x_other_ref,
    back_ref,
    ctx_ref,
    lse_ref,
    seg_col_ref,
    seg_row_ref,
    limit_ref,
    grad_ref,
    pack_ref,
    sum_ref,
    acc_ref,
    grads_ref,
    quant_ref,
    inner_ref,
):
    low = lax.broadcasted_iota(jnp.int32, (BLOCK, 2 * HEAD), 1) < HEAD
    limit = limit_ref[0]
    for half, rows_ref in enumerate((go_ref, go_other_ref)):
        for block in range(HALF // BLOCK):
            rows = pl.ds(half * HALF + block * BLOCK, BLOCK)
            context = ctx_ref[rows, :]
            quant_ref[rows, :] = jnp.clip(context, -limit, limit).astype(BF16)
            grad = nt(rows_ref[pl.ds(block * BLOCK, BLOCK), :], back_ref[...])
            grad = jnp.where(jnp.abs(context) <= limit, grad, 0.0).astype(BF16)
            grads_ref[rows, :] = grad
            both = grad.astype(F32) * context
            inner = [
                jnp.sum(jnp.where(own, both, 0.0), axis=1, keepdims=True)
                for own in (low, jnp.logical_not(low))
            ]
            inner_ref[:, rows] = jnp.transpose(jnp.concatenate(inner, axis=1))
    queries = q_ref[...]
    grads = grads_ref[...]
    value_sum = jnp.zeros((1, 2 * HEAD), F32)
    for block in range(LEN // BLOCK):
        rows = pl.ds(block * BLOCK, BLOCK)
        keys = k_ref[rows, :]
        scaled_keys = keys * jnp.asarray(HEAD**-0.5, BF16)
        values = v_ref[rows, :]
        same = seg_col_ref[rows, :] == seg_row_ref[...]
        value_parts, key_parts = [], []
        for head in range(2):
            own = low if head == 0 else jnp.logical_not(low)
            zero = jnp.zeros_like(keys)
            scores = nt(jnp.where(own, scaled_keys, zero), queries)
            logs = lse_ref[0, head : head + 1, :]
            attention = jnp.where(same, jnp.exp(scores - logs), 0.0)
            value_parts.append(nn(attention.astype(BF16), grads))
            grad_attention = nt(jnp.where(own, values, zero), grads)
            inner = inner_ref[head : head + 1, :]
            grad_score = (attention * (grad_attention - inner) * HEAD**-0.5).astype(BF16)
            key_parts.append(nn(grad_score, queries))
            part = tn(grad_score, jnp.where(own, keys, zero))
            if block == 0 and head == 0:
                acc_ref[...] = part
            else:
                acc_ref[...] += part
        grad_value = jnp.where(low, value_parts[0], value_parts[1])
        value_sum += jnp.sum(grad_value, axis=0, keepdims=True)
        grad_ref[rows, 4 * HEAD :] = grad_value.astype(BF16)
        grad_ref[rows, 2 * HEAD : 4 * HEAD] = jnp.where(low, key_parts[0], key_parts[1]).astype(BF16)
    grad_query = acc_ref[...]
    grad_ref[:, : 2 * HEAD] = grad_query.astype(BF16)
    sum_ref[0, 0:1, :] = jnp.sum(grad_query, axis=0, keepdims=True)
    sum_ref[0, 1:2, :] = value_sum
    chunk = HEAD // 4
    sides = ((slice(0, HALF), x_ref, go_ref), (slice(HALF, LEN), x_other_ref, go_other_ref))
    for kind in range(4):
        lanes = slice(2 * kind * HEAD, 2 * (kind + 1) * HEAD)
        total = None
        for rows, x_side, go_side in sides:
            if kind < 3:
                part = tn(grad_ref[rows, lanes], x_side[...])
            else:
                part = tn(quant_ref[rows, :], go_side[...])
            total = part if total is None else total + part
        total = total.astype(BF16)
        for head in range(2):
            for j in range(4):
                at = head * HEAD + j * chunk
                into = (head * 4 + kind) * chunk
                pack_ref[j, into : into + chunk, :] = total[at : at + chunk, :]


def attend_back(
    first, n, before, proj, go, go_other, x, x_other, w_back, context, lse, seg_col, seg_row, limit
):
    width = w_back.shape[1]
    earlier = [] if before is None else [before]

    def body(*refs):
        attend_back_kernel(*refs[:13], *refs[13 + len(earlier) :])

    def whole(array):
        return pl.BlockSpec(array.shape, lambda i: (0,) * array.ndim)

    return pl.pallas_call(
        body,
        grid=(n,),
        in_specs=[
            pl.BlockSpec((LEN, 2 * HEAD), lambda i: (0, 3 * (first + i))),
            pl.BlockSpec((LEN, 2 * HEAD), lambda i: (0, 3 * (first + i) + 1)),
            pl.BlockSpec((LEN, 2 * HEAD), lambda i: (0, 3 * (first + i) + 2)),
            *[whole(array) for array in (go, go_other, x, x_other)],
            pl.BlockSpec((2 * HEAD, width), lambda i: (first + i, 0)),
            pl.BlockSpec((LEN, 2 * HEAD), lambda i: (0, first + i)),
            pl.BlockSpec((1, 2, LEN), lambda i: (first + i, 0, 0)),
            whole(seg_col),
            whole(seg_row),
            pl.BlockSpec(memory_space=pltpu.SMEM),
            *[pl.BlockSpec(memory_space=pl.ANY) for _ in earlier],
        ],
        out_specs=[
            pl.BlockSpec((LEN, 6 * HEAD), lambda i: (0, i)),
            pl.BlockSpec((4, 2 * HEAD, width), lambda i: (0, first + i, 0)),
            pl.BlockSpec((1, 2, 2 * HEAD), lambda i: (i, 0, 0)),
        ],
        out_shape=[
            jax.ShapeDtypeStruct((LEN, n * 6 * HEAD), BF16),
            jax.ShapeDtypeStruct((4, *w_back.shape), BF16),
            jax.ShapeDtypeStruct((n, 2, 2 * HEAD), F32),
        ],
        scratch_shapes=[
            pltpu.VMEM((LEN, 2 * HEAD), F32),
            pltpu.VMEM((LEN, 2 * HEAD), BF16),
            pltpu.VMEM((LEN, 2 * HEAD), BF16),
            pltpu.VMEM((2, LEN), F32),
        ],
        cost_estimate=attention_cost(n, 9) if first else None,
        input_output_aliases={13: 1} if earlier else {},
        name="attend_back",
    )(
        *(proj, proj, proj, go, go_other, x, x_other, w_back, context, lse),
        *(seg_col, seg_row, limit, *earlier),
    )


def unpack_kernel(plane_ref, *refs):
    pieces, (qkv_ref, out_ref) = refs[:4], refs[4:]
    kind = pl.program_id(0)
    chunk = HEAD // 4
    heads = pieces[0].shape[0] // HEAD

    for plane in range(4):

        @pl.when(plane_ref[0] == plane)
        def _(plane=plane):
            parts = []
            for head in range(heads):
                at = pl.multiple_of(head * HEAD + kind * chunk, chunk)
                parts += [pieces[j ^ plane][pl.ds(at, chunk), :] for j in range(4)]
            rows = jnp.concatenate(parts, axis=0).astype(F32)

            @pl.when(kind < 3)
            def _():
                qkv_ref[0] = rows

            @pl.when(kind == 3)
            def _():
                out_ref[...] = rows


def unpack(plane, pieces):
    tall, width = pieces[0].shape
    return pl.pallas_call(
        unpack_kernel,
        grid=(4,),
        in_specs=[
            pl.BlockSpec(memory_space=pltpu.SMEM),
            *[pl.BlockSpec((tall, width), lambda i: (0, 0)) for _ in pieces],
        ],
        out_specs=[
            pl.BlockSpec((1, tall, width), lambda i: (jnp.minimum(i, 2), 0, 0)),
            pl.BlockSpec((tall, width), lambda i: (0, 0)),
        ],
        out_shape=[
            jax.ShapeDtypeStruct((3, tall, width), F32),
            jax.ShapeDtypeStruct((tall, width), F32),
        ],
        name="unpack",
    )(plane[None], *pieces)


def unpack_ffn_kernel(where_ref, own_ref, other_ref, up_ref, down_ref):
    half, plane = where_ref[0], where_ref[1]
    quarter = up_ref.shape[1] // 4

    def rows_of(ref, first):
        parts = [ref[j ^ plane, first : first + quarter, :] for j in range(4)]
        return jnp.concatenate(parts, axis=0).astype(F32)

    for mine, ref in ((True, own_ref), (False, other_ref)):

        @pl.when((pl.program_id(0) == half) == mine)
        def _(ref=ref):
            up_ref[...] = jnp.transpose(rows_of(ref, 0))
            down_ref[...] = rows_of(ref, quarter)


def unpack_ffn(half, plane, own, other, quarter):
    width = own.shape[2]
    return pl.pallas_call(
        unpack_ffn_kernel,
        grid=(2,),
        in_specs=[
            pl.BlockSpec(memory_space=pltpu.SMEM),
            pl.BlockSpec(own.shape, lambda i: (0, 0, 0)),
            pl.BlockSpec(own.shape, lambda i: (0, 0, 0)),
        ],
        out_specs=[
            pl.BlockSpec((width, 4 * quarter), lambda i: (0, i)),
            pl.BlockSpec((4 * quarter, width), lambda i: (i, 0)),
        ],
        out_shape=[
            jax.ShapeDtypeStruct((width, 8 * quarter), F32),
            jax.ShapeDtypeStruct((8 * quarter, width), F32),
        ],
        name="unpack_ffn",
    )(jnp.stack([half, plane]), own, other)


class Links:
    def __init__(self, dp, depths):
        self.dp, self.depths = dp, depths
        self.planes = dp // 2
        place = lax.axis_index("dp")
        self.half, self.plane = place % 2, place // 2
        self.depth = lax.axis_index("tensor")
        self.square = self.planes == 4 and depths == 4

    def permute(self, array, move):
        pairs = []
        for place in range(self.dp):
            for depth in range(self.depths):
                to = move(place // 2, place % 2, depth)
                if to is not None:
                    plane, half, level = to
                    pairs.append(
                        (place * self.depths + depth, (2 * plane + half) * self.depths + level)
                    )
        return lax.ppermute(array, JOINT, pairs)

    def rows_home(self, array):
        return self.permute(
            array, lambda e, c, z: (e, z % 2, z - z % 2 + c) if c != z % 2 else None
        )

    def at_home(self, own, moved):
        return jnp.where(self.depth % 2 == self.half, own, moved)

    def other_half(self, array):
        return self.permute(array, lambda e, c, z: (e, 1 - c, z))

    def across(self, array, step, only=None):
        return self.permute(
            array,
            lambda e, c, z: (e ^ step, c, z) if only is None or only(c, z) else None,
        )

    def along(self, array, step):
        return self.permute(array, lambda e, c, z: (e, c, z ^ step))

    def spread_near(self, piece, only=None):
        return self.across(piece, 1, only), self.across(piece, 2, only)

    def spread_far(self, piece, near, only=None):
        first, second = near
        cut = piece.shape[-2] // 16 * 8
        third_low = self.across(second[..., :cut, :], 1, only)
        third_high = self.across(first[..., cut:, :], 2, only)
        return [piece, first, second, jnp.concatenate([third_low, third_high], axis=-2)]

    def spread(self, piece, only=None):
        return [piece] + [self.across(piece, step, only) for step in (1, 2, 3)]

    def in_order(self, pieces):
        stack = jnp.stack(pieces)
        return jnp.stack(
            [lax.dynamic_index_in_dim(stack, j ^ self.plane, 0, False) for j in range(4)]
        )

    @property
    def inside(self):
        return self.depth // 2 == self.half

    @property
    def even(self):
        return self.depth % 2 == 0

    def pair_near(self, array):
        return self.permute(array, lambda e, c, z: (e, c, z ^ 1) if z // 2 == c else None)

    def pair_out(self, array):
        def far(step):
            return lambda e, c, z: (e, c, z ^ step) if z // 2 == c else None

        return [self.permute(array, far(step)) for step in (2, 3, 1)]

    def pair_of(self, mine, arrived):
        same, cross, near = arrived
        a = jnp.where(self.inside, mine, same)
        b = jnp.where(self.inside, near, cross)
        return self.even_first(a, b)

    def pair_back(self, array):
        return self.permute(array, lambda e, c, z: (e, c, z ^ 2) if z // 2 != c else None)

    def pair_cross(self, array):
        return self.permute(array, lambda e, c, z: (e, c, z ^ 3) if z // 2 != c else None)

    def halves_in_order(self, mine, other):
        first = self.half == 0
        return jnp.stack([jnp.where(first, mine, other), jnp.where(first, other, mine)])

    def natural(self, array):
        swapped = array[..., jnp.array([1, 0, 3, 2]), :]
        array = jnp.where(self.plane % 2 == 1, swapped, array)
        swapped = array[..., jnp.array([2, 3, 0, 1]), :]
        return jnp.where(self.plane // 2 == 1, swapped, array)

    def even_first(self, mine, other):
        return jnp.stack([jnp.where(self.even, mine, other), jnp.where(self.even, other, mine)])


def exact_parts(values):
    high = lax.reduce_precision(values, 8, 7)
    rest = values - high
    middle = lax.reduce_precision(rest, 8, 7)
    return jnp.concatenate([high, middle, rest - middle]).astype(BF16)


def exact_sum(parts):
    rows = parts.shape[0] // 3
    parts = parts.astype(F32)
    return parts[:rows] + parts[rows : 2 * rows] + parts[2 * rows :]


def merge(both, other):
    last = lax.broadcasted_iota(jnp.int32, both.shape, 0) == 6
    return jnp.where(last, jnp.maximum(both, other), both + other)


def sync(*values):
    return lax.optimization_barrier(values)


def plain_all(links, grads):
    blank = jnp.zeros((4, 2) + grads.shape[1:], F32)
    full = lax.dynamic_update_slice_in_dim(blank, grads[:, None].astype(F32), links.half, 1)
    shard = lax.psum_scatter(full, "tensor", scatter_dimension=0, tiled=False)
    return lax.psum(shard, "dp")


def plain_pair(links, grads):
    blank = jnp.zeros((4,) + grads.shape[:1] + grads.shape[2:], F32)
    own = grads.swapaxes(0, 1).astype(F32)
    full = lax.dynamic_update_slice_in_dim(blank, own, 2 * links.half, 0)
    shard = lax.psum_scatter(full, "tensor", scatter_dimension=0, tiled=False)
    return lax.psum(shard, "dp")


def on_device(
    sizes,
    layer_input,
    segments,
    w_qkv,
    bias_qv,
    w_out,
    b_out,
    gain_attn,
    shift_attn,
    w_in,
    b_in,
    w_down,
    b_down,
    gain_ffn,
    shift_ffn,
    act_scale,
    out_grad,
):
    links = Links(*sizes)
    width = layer_input.shape[1]
    local = w_qkv.shape[2]
    heads = local // HEAD
    chunk = HEAD // 4
    units = w_in.shape[1]
    quarter = units // 8
    gain_first = gain_attn.astype(F32)
    gain_second = gain_ffn.astype(F32)

    per = 3 * heads * chunk
    more = heads * chunk

    rows = jnp.concatenate([jnp.swapaxes(w_qkv, 1, 2), w_out[None]])
    rows = rows.reshape(4, heads, 4, chunk, width)
    rows = rows.transpose(2, 0, 1, 3, 4).reshape(4, per + more, width)
    tail = bias_qv.reshape(2, heads, 4, chunk).transpose(2, 0, 1, 3).reshape(4, 1, 2 * more)
    tail = jnp.pad(tail, ((0, 0), (0, 7), (0, width - tail.shape[2])))
    attn_pack = jnp.concatenate([rows, tail], axis=1)
    if links.square:
        attn_mine = lax.dynamic_index_in_dim(attn_pack, links.plane, 0, False)
        attn_in = links.pair_out(attn_mine)
    seg_rows = segments.reshape(2, LEN)
    seg_mine = lax.dynamic_index_in_dim(seg_rows, links.depth // 2, 0, False).reshape(8, LEN // 8)
    seg_next = links.other_half(seg_mine)
    seg_home = links.at_home(seg_mine, seg_next).reshape(2, HALF)
    seg_home = jnp.where(links.half == 0, seg_home, seg_home[::-1]).reshape(LEN)
    seg_col, seg_row = seg_home[:, None], seg_home[None, :]
    ffn_half = jnp.concatenate(
        [
            lax.dynamic_index_in_dim(w_in.T.reshape(2, 4, quarter, width), links.half, 0, False),
            lax.dynamic_index_in_dim(w_down.reshape(2, 4, quarter, width), links.half, 0, False),
            jnp.pad(
                lax.dynamic_index_in_dim(b_in.reshape(2, 4, 1, quarter), links.half, 0, False),
                ((0, 0), (0, 7), (0, width - quarter)),
            ),
        ],
        axis=1,
    )
    if links.square:
        ffn_own = jnp.stack(
            [lax.dynamic_index_in_dim(ffn_half, j ^ links.plane, 0, False) for j in ORDER]
        )
        attn_in, ffn_mine, x_home = sync(attn_in, ffn_own[0], layer_input)
        attn_both = links.pair_of(attn_mine, attn_in)
        attn_near = links.spread_near(attn_both)
        x_home = links.rows_home(x_home)
        ffn_two = links.along(ffn_mine, 2)
        attn_near, ffn_two, ffn_mine = sync(attn_near, ffn_two, ffn_mine)
        attn_full = jnp.stack(links.spread_far(attn_both, attn_near))
        ffn_in = jnp.stack([links.along(ffn_mine, 1), ffn_two, links.along(ffn_mine, 3)])
    else:
        attn_full = lax.all_gather(attn_pack, "tensor", axis=0, tiled=False)
        attn_full = lax.dynamic_slice_in_dim(attn_full, 2 * links.half, 2, 0).swapaxes(0, 1)
        ffn_in = lax.all_gather(ffn_half, "tensor", axis=0, tiled=False)
        x_home = links.rows_home(layer_input)
    x_home = links.at_home(layer_input, x_home)

    x_full = x_home.astype(F32)
    x_quant = jnp.clip(x_full, -act_scale[0], act_scale[0]).astype(BF16)
    x_other = links.other_half(x_quant)
    x_rows = jnp.concatenate([x_quant, x_other])

    weights = attn_full[:, :, : per + more].reshape(4, 2, 4, heads, chunk, width)
    weights = weights.transpose(2, 1, 3, 0, 4, 5).reshape(4, heads, 2 * HEAD, width)
    w_proj = weights[:3].swapaxes(0, 1).reshape(6 * local, width)
    w_back = weights[3].reshape(2 * local, width)
    biases = attn_full[:, :, per + more, : 2 * more].reshape(4, 2, 2, heads, chunk)
    biases = biases.transpose(2, 1, 3, 0, 4).reshape(2, 2 * local).astype(F32)
    bias_all = jnp.stack([biases[0], jnp.zeros_like(biases[0]), biases[1]])
    bias_all = bias_all.reshape(3, heads, 2 * HEAD).swapaxes(0, 1).reshape(6 * local)

    proj = (nt(x_rows, w_proj) + bias_all).astype(BF16)
    proj, ffn_in, out_grad = sync(proj, ffn_in, out_grad)
    if links.square:
        ffn_near = links.spread_near(ffn_in)
    upstream = links.rows_home(out_grad)
    context, lse = attend(proj, seg_col, seg_row, heads)
    context, upstream = sync(context, upstream)
    if links.square:
        context, ffn_near = sync(context, ffn_near)
    upstream = links.at_home(out_grad, upstream).astype(F32)
    ctx_quant = jnp.clip(context, -act_scale[1], act_scale[1]).astype(BF16)
    attn_part, attn_sent = nn(ctx_quant[:HALF], w_back), nn(ctx_quant[HALF:], w_back)
    if links.square:
        pieces = links.spread_far(ffn_in, ffn_near)
        ffn_full = jnp.stack(
            [jnp.concatenate([ffn_own[i][None], pieces[j]]) for i, j in enumerate(ORDER)]
        )
    else:
        ffn_full = ffn_in.swapaxes(0, 1)
    attn_out = attn_part + links.other_half(attn_sent) + b_out.astype(F32)
    hidden, normed_attn, inverse_attn = norm_forward(
        x_full + attn_out, gain_first, shift_attn.astype(F32)
    )
    hid_quant = jnp.clip(hidden, -act_scale[2], act_scale[2]).astype(BF16)
    hid_other = links.other_half(hid_quant)
    tops = [jnp.max(jnp.abs(array)) for array in (x_full, context, hidden)]
    hid_other, tops = sync(hid_other, tops)
    hid_rows = jnp.concatenate([hid_quant, hid_other])

    w_up = ffn_full[:, :, :quarter].reshape(2 * units, width)
    w_low = ffn_full[:, :, quarter : 2 * quarter].reshape(2 * units, width)
    b_up = ffn_full[:, :, 2 * quarter, :quarter].reshape(2 * units).astype(F32)
    pre_act = nt(hid_rows, w_up) + b_up
    normal_cdf = 0.5 * (1.0 + lax.erf(pre_act * 0.5**0.5))
    activated = pre_act * normal_cdf
    slope = normal_cdf + pre_act * jnp.exp(-0.5 * pre_act * pre_act) / math.sqrt(2.0 * math.pi)
    slope = jnp.where(jnp.abs(activated) <= act_scale[3], slope, 0.0)
    act_quant = jnp.clip(activated, -act_scale[3], act_scale[3]).astype(BF16)
    ffn_sent, ffn_part = nn(act_quant[HALF:], w_low), nn(act_quant[:HALF], w_low)
    ffn_out = ffn_part + links.other_half(ffn_sent)
    final, normed_ffn, inverse_ffn = norm_forward(
        hidden + ffn_out + b_down.astype(F32), gain_second, shift_ffn.astype(F32)
    )
    final = final.astype(BF16)
    layer_output = links.rows_home(final)
    lanes = lax.broadcasted_iota(jnp.int32, (1, width), 1)
    maxima = jnp.zeros((1, width), F32)
    for at, value in enumerate((*tops, jnp.max(jnp.abs(activated)))):
        maxima = jnp.where(lanes == at, value, maxima)

    grad_gain_ffn = jnp.sum(upstream * normed_ffn, axis=0, keepdims=True)
    grad_shift_ffn = jnp.sum(upstream, axis=0, keepdims=True)
    grad_second = norm_backward(upstream, normed_ffn, inverse_ffn, gain_second)
    grad_b_down = jnp.sum(grad_second, axis=0, keepdims=True)
    grad_final = grad_second.astype(BF16)
    grad_rows = jnp.concatenate([grad_final, links.other_half(grad_final)])
    down = tn(act_quant, grad_rows).astype(BF16).reshape(4, 4, quarter, width)
    grad_pre = nt(grad_rows, w_low) * slope
    grad_b_in = jnp.sum(grad_pre, axis=0)
    grad_pre_b = grad_pre.astype(BF16)
    up = tn(grad_pre_b, hid_rows).astype(BF16).reshape(4, 4, quarter, width)
    tail = jnp.pad(
        grad_b_in.astype(BF16).reshape(4, 4, 1, quarter),
        ((0, 0), (0, 0), (0, 7), (0, width - quarter)),
    )
    ffn_grads = jnp.concatenate([up, down, tail], axis=2)
    if links.square:
        ffn_grads, grad_pre_b = sync(ffn_grads, grad_pre_b)
        ffn_x = links.across(ffn_grads[1:3, :2], 1)
        ffn_y = links.across(ffn_grads[2:4, 2:], 2)
    hid_sent, hid_part = nn(grad_pre_b[HALF:], w_up), nn(grad_pre_b[:HALF], w_up)
    grad_hid = hid_part + links.other_half(hid_sent)

    grad_hidden = grad_second + grad_hid * (jnp.abs(hidden) <= act_scale[2]).astype(F32)
    grad_gain_attn = jnp.sum(grad_hidden * normed_attn, axis=0, keepdims=True)
    grad_shift_attn = jnp.sum(grad_hidden, axis=0, keepdims=True)
    grad_first = norm_backward(grad_hidden, normed_attn, inverse_attn, gain_first)
    grad_b_out = jnp.sum(grad_first, axis=0, keepdims=True)
    grad_attn = grad_first.astype(BF16)
    go_other = links.other_half(grad_attn)
    sums = [grad_b_out, grad_gain_attn, grad_shift_attn, grad_b_down, grad_gain_ffn, grad_shift_ffn]
    sums = jnp.concatenate([*sums, maxima, jnp.zeros((1, width), F32)])

    def back(first, count, before):
        return attend_back(
            first,
            count,
            before,
            proj,
            grad_attn,
            go_other,
            x_quant,
            x_other,
            w_back,
            context,
            lse,
            seg_col,
            seg_row,
            act_scale[1:2],
        )

    def bias_rows(pairs):
        return pairs.reshape(heads, 2, 2, 4, chunk).swapaxes(0, 1)

    if links.square:
        tall = 2 * heads * HEAD // 2
        many = heads - 1
        early, grad_w, early_b = back(0, many, None)
        early, go_other, ffn_x, ffn_y = sync(early, go_other, ffn_x, ffn_y)
        low = [ffn_grads[0, :2] + ffn_x[0].astype(F32), ffn_grads[3, :2] + ffn_x[1].astype(F32)]
        high = [ffn_grads[0, 2:] + ffn_y[1].astype(F32), ffn_grads[1, 2:] + ffn_y[0].astype(F32)]
        ffn_y, ffn_x = low[1].astype(BF16), high[1].astype(BF16)
        go_other, ffn_x, ffn_y = sync(go_other, ffn_x, ffn_y)
        ffn_y, ffn_x = links.across(ffn_y, 2), links.across(ffn_x, 1)
        late, grad_w, late_b = back(many, 1, grad_w)
        late, grad_w, late_b, ffn_x, ffn_y = sync(late, grad_w, late_b, ffn_x, ffn_y)
        sums = merge(sums, links.other_half(sums))
        bias_sums = links.natural(bias_rows(jnp.concatenate([early_b, late_b])))
        sums = jnp.concatenate([sums[:7], bias_sums.reshape(1, width)])
        sums_sent = exact_parts(sums)
        ffn_low = low[0] + ffn_y.astype(F32)
        ffn_in = links.along((high[0] + ffn_x.astype(F32)).astype(BF16), 2)
        proj_in = [
            links.across(jnp.concatenate([grad_w[step], sums_sent]), step) for step in (1, 2, 3)
        ]
        grad_proj, ffn_low = sync(jnp.concatenate([early, late], axis=1), ffn_low)
    else:
        grad_proj, grad_w, bias_sums = back(0, heads, None)
        bias_sums = bias_rows(bias_sums)
    x_sent, x_part = nn(grad_proj[HALF:], w_proj), nn(grad_proj[:HALF], w_proj)
    grad_x = x_part + links.other_half(x_sent)
    input_grad = grad_first + grad_x * (jnp.abs(x_full) <= act_scale[0]).astype(F32)
    input_part = input_grad.astype(BF16)

    if links.square:
        total = grad_w[0].astype(F32)
        for part in proj_in:
            total = total + part[: 2 * tall].astype(F32)
            sums = merge(sums, exact_sum(part[2 * tall :]))
        mine = jnp.where(links.even, total[:tall], total[tall:])
        other = jnp.where(links.even, total[tall:], total[:tall])
        sums_sent = exact_parts(sums)
        other = jnp.concatenate([other.astype(BF16), sums_sent])
        sent = jnp.concatenate([mine.astype(BF16), sums_sent])
        ffn_in, other, sent = sync(ffn_in, other, sent)
        proj_in = [links.pair_near(other), links.pair_back(sent), links.pair_cross(other)]
        ffn_low = ffn_low + ffn_in.astype(F32)
        ffn_in = links.along(ffn_low[1].astype(BF16), 1)
        for part in proj_in:
            mine = mine + part[:tall].astype(F32)
            sums = merge(sums, exact_sum(part[tall:]))
        mine, input_part = sync(mine.astype(BF16), input_part)
        sent = jnp.concatenate([mine, exact_parts(sums)])
        sent = jnp.where(links.inside, sent, links.other_half(sent))
        sums = exact_sum(sent[tall:])
        proj_all = links.spread(sent[:tall])
        ffn_mine = (ffn_low[0] + ffn_in.astype(F32)).astype(BF16)
        ffn_all = jnp.stack(links.spread(ffn_mine))
        ffn_other = links.other_half(ffn_all)
        ffn_all, ffn_other = sync(ffn_all, ffn_other)
        grad_in, grad_down = unpack_ffn(links.half, links.plane, ffn_all, ffn_other, quarter)
        own, grad_in, grad_down = sync(proj_all[0], grad_in, grad_down)
        grad_qkv, grad_out = unpack(links.plane, [own, *proj_all[1:]])
        grad_qkv = jnp.swapaxes(grad_qkv, 1, 2)
        grad_b_in = links.halves_in_order(
            links.in_order(list(ffn_all[:, 2 * quarter, :quarter])),
            links.in_order(list(ffn_other[:, 2 * quarter, :quarter])),
        ).reshape(units)
    else:
        ffn_all = plain_all(links, ffn_grads.swapaxes(0, 1))
        grad_in = ffn_all[:, :, :quarter].reshape(units, width).T
        grad_down = ffn_all[:, :, quarter : 2 * quarter].reshape(units, width)
        grad_b_in = ffn_all[:, :, 2 * quarter, :quarter].reshape(units)
        grads = plain_pair(links, grad_w.reshape(4, 2, -1, width))
        grads = grads.reshape(4, heads, 4, chunk, width).transpose(2, 1, 0, 3, 4)
        grads = grads.reshape(4, local, width)
        grad_qkv, grad_out = jnp.swapaxes(grads[:3], 1, 2), grads[3]
        sums = jnp.concatenate([lax.psum(sums[:6], JOINT), lax.pmax(sums[6:7], JOINT)])
        both = jnp.zeros((4, 2, local), F32)
        both = lax.dynamic_update_slice_in_dim(
            both, bias_sums.reshape(2, 2, local).swapaxes(0, 1), 2 * links.half, 0
        )
        both = lax.psum(both, JOINT)
        both = lax.dynamic_slice_in_dim(both, links.depth - links.depth % 2, 2, 0)
        sums = jnp.concatenate([sums, both.swapaxes(0, 1).reshape(1, width)])
    input_grad = links.at_home(input_part, links.rows_home(input_part)).astype(F32)
    maxima = sums[6, :4]
    new_scale = DECAY * act_scale + (1.0 - DECAY) * maxima

    grad_bias_qv = lax.dynamic_index_in_dim(
        sums[7].reshape(2, 2, local), links.depth % 2, 1, False
    )
    return (
        links.at_home(final, layer_output),
        input_grad,
        grad_qkv,
        grad_bias_qv,
        grad_out,
        sums[0],
        sums[1],
        sums[2],
        grad_in,
        grad_b_in.astype(F32),
        grad_down,
        sums[3],
        sums[4],
        sums[5],
        new_scale,
        maxima,
    )


def solution(mesh):
    in_specs = (
        P(("dp", "tensor"), None),
        P("dp"),
        P(None, None, "tensor"),
        P(None, "tensor"),
        P("tensor", None),
        P(),
        P(),
        P(),
        P(None, "tensor"),
        P("tensor"),
        P("tensor", None),
        P(),
        P(),
        P(),
        P(),
        P(("dp", "tensor"), None),
    )
    out_specs = (
        P(("dp", "tensor"), None),
        P(("dp", "tensor"), None),
        P(None, None, "tensor"),
        P(None, "tensor"),
        P("tensor", None),
        P(),
        P(),
        P(),
        P(None, "tensor"),
        P("tensor"),
        P("tensor", None),
        P(),
        P(),
        P(),
        P(),
        P(),
    )
    sizes = (mesh.shape["dp"], mesh.shape["tensor"])
    return jax.shard_map(
        functools.partial(on_device, sizes),
        mesh=mesh,
        in_specs=in_specs,
        out_specs=out_specs,
        check_vma=False,
    )
```

```python
import functools
import math

import jax
import jax.numpy as jnp
from jax import lax
from jax.experimental import pallas as pl
from jax.experimental.pallas import tpu as pltpu
from jax.sharding import PartitionSpec as P

HEAD = 64
LEN = 1024
HALF = LEN // 2
BLOCK = 256

EPSILON = 1e-12
DECAY = 0.9999
MASKED = -1e30
ORDER = (0, 1, 3, 2)
JOINT = ("dp", "tensor")
BF16 = jnp.bfloat16
F32 = jnp.float32


def norm_forward(resid, gain, shift):
    row_mean = jnp.mean(resid, axis=-1, keepdims=True)
    centred = resid - row_mean
    spread = jnp.mean(centred * centred, axis=-1, keepdims=True)
    inverse = lax.rsqrt(spread + EPSILON)
    normed = centred * inverse
    return (normed * gain + shift, normed, inverse)


def norm_backward(upstream, normed, inverse, gain):
    scaled = upstream * gain
    mean_first = jnp.mean(scaled, axis=-1, keepdims=True)
    mean_second = jnp.mean(scaled * normed, axis=-1, keepdims=True)
    return inverse * (scaled - mean_first - normed * mean_second)


def nt(a, b):
    return lax.dot_general(a, b, (((1,), (1,)), ((), ())), preferred_element_type=F32)


def nn(a, b):
    return lax.dot_general(a, b, (((1,), (0,)), ((), ())), preferred_element_type=F32)


def tn(a, b):
    return lax.dot_general(a, b, (((0,), (0,)), ((), ())), preferred_element_type=F32)


def attend_kernel(q_ref, k_ref, v_ref, seg_col_ref, seg_row_ref, ctx_ref, lse_ref):
    low = lax.broadcasted_iota(jnp.int32, (BLOCK, 2 * HEAD), 1) < HEAD
    keys = k_ref[...]
    values = v_ref[...]
    for block in range(LEN // BLOCK):
        rows = pl.ds(block * BLOCK, BLOCK)
        queries = q_ref[rows, :] * jnp.asarray(HEAD**-0.5, BF16)
        same = seg_col_ref[rows, :] == seg_row_ref[...]
        parts, logs = [], []
        for head in range(2):
            own = low if head == 0 else jnp.logical_not(low)
            scores = nt(jnp.where(own, queries, jnp.zeros_like(queries)), keys)
            scores = jnp.where(same, scores, MASKED)
            top = jnp.max(scores, axis=-1, keepdims=True)
            exponent = jnp.exp(scores - top)
            total = jnp.sum(exponent, axis=-1, keepdims=True)
            attention = (exponent * (1.0 / total)).astype(BF16)
            parts.append(nn(attention, values))
            logs.append(top + jnp.log(total))
        ctx_ref[rows, :] = jnp.where(low, parts[0], parts[1])
        lse_ref[0, :, rows] = jnp.transpose(jnp.concatenate(logs, axis=1))


def attention_cost(pairs_of_heads, products):
    scores = 2 * pairs_of_heads * LEN * LEN
    return pl.CostEstimate(
        flops=2 * 4 * HEAD * products * scores,
        transcendentals=scores,
        bytes_accessed=8 * pairs_of_heads * LEN * HEAD * products,
    )


def attend(proj, seg_col, seg_row, pairs_of_heads):
    n = pairs_of_heads
    return pl.pallas_call(
        attend_kernel,
        grid=(n,),
        in_specs=[
            pl.BlockSpec((LEN, 2 * HEAD), lambda i: (0, 3 * i)),
            pl.BlockSpec((LEN, 2 * HEAD), lambda i: (0, 3 * i + 1)),
            pl.BlockSpec((LEN, 2 * HEAD), lambda i: (0, 3 * i + 2)),
            pl.BlockSpec((LEN, 1), lambda i: (0, 0)),
            pl.BlockSpec((1, LEN), lambda i: (0, 0)),
        ],
        out_specs=[
            pl.BlockSpec((LEN, 2 * HEAD), lambda i: (0, i)),
            pl.BlockSpec((1, 2, LEN), lambda i: (i, 0, 0)),
        ],
        out_shape=[
            jax.ShapeDtypeStruct((LEN, n * 2 * HEAD), F32),
            jax.ShapeDtypeStruct((n, 2, LEN), F32),
        ],
        name="attend",
    )(proj, proj, proj, seg_col, seg_row)


def attend_back_kernel(
    q_ref,
    k_ref,
    v_ref,
    go_ref,
    go_other_ref,
    x_ref,
    x_other_ref,
    back_ref,
    ctx_ref,
    lse_ref,
    seg_col_ref,
    seg_row_ref,
    limit_ref,
    grad_ref,
    pack_ref,
    sum_ref,
    acc_ref,
    grads_ref,
    quant_ref,
    inner_ref,
):
    low = lax.broadcasted_iota(jnp.int32, (BLOCK, 2 * HEAD), 1) < HEAD
    limit = limit_ref[0]
    for half, rows_ref in enumerate((go_ref, go_other_ref)):
        for block in range(HALF // BLOCK):
            rows = pl.ds(half * HALF + block * BLOCK, BLOCK)
            context = ctx_ref[rows, :]
            quant_ref[rows, :] = jnp.clip(context, -limit, limit).astype(BF16)
            grad = nt(rows_ref[pl.ds(block * BLOCK, BLOCK), :], back_ref[...])
            grad = jnp.where(jnp.abs(context) <= limit, grad, 0.0).astype(BF16)
            grads_ref[rows, :] = grad
            both = grad.astype(F32) * context
            inner = [
                jnp.sum(jnp.where(own, both, 0.0), axis=1, keepdims=True)
                for own in (low, jnp.logical_not(low))
            ]
            inner_ref[:, rows] = jnp.transpose(jnp.concatenate(inner, axis=1))
    queries = q_ref[...]
    grads = grads_ref[...]
    value_sum = jnp.zeros((1, 2 * HEAD), F32)
    for block in range(LEN // BLOCK):
        rows = pl.ds(block * BLOCK, BLOCK)
        keys = k_ref[rows, :]
        scaled_keys = keys * jnp.asarray(HEAD**-0.5, BF16)
        values = v_ref[rows, :]
        same = seg_col_ref[rows, :] == seg_row_ref[...]
        value_parts, key_parts = [], []
        for head in range(2):
            own = low if head == 0 else jnp.logical_not(low)
            zero = jnp.zeros_like(keys)
            scores = nt(jnp.where(own, scaled_keys, zero), queries)
            logs = lse_ref[0, head : head + 1, :]
            attention = jnp.where(same, jnp.exp(scores - logs), 0.0)
            value_parts.append(nn(attention.astype(BF16), grads))
            grad_attention = nt(jnp.where(own, values, zero), grads)
            inner = inner_ref[head : head + 1, :]
            grad_score = (attention * (grad_attention - inner) * HEAD**-0.5).astype(BF16)
            key_parts.append(nn(grad_score, queries))
            part = tn(grad_score, jnp.where(own, keys, zero))
            if block == 0 and head == 0:
                acc_ref[...] = part
            else:
                acc_ref[...] += part
        grad_value = jnp.where(low, value_parts[0], value_parts[1])
        value_sum += jnp.sum(grad_value, axis=0, keepdims=True)
        grad_ref[rows, 4 * HEAD :] = grad_value.astype(BF16)
        grad_ref[rows, 2 * HEAD : 4 * HEAD] = jnp.where(low, key_parts[0], key_parts[1]).astype(BF16)
    grad_query = acc_ref[...]
    grad_ref[:, : 2 * HEAD] = grad_query.astype(BF16)
    sum_ref[0, 0:1, :] = jnp.sum(grad_query, axis=0, keepdims=True)
    sum_ref[0, 1:2, :] = value_sum
    chunk = HEAD // 4
    sides = ((slice(0, HALF), x_ref, go_ref), (slice(HALF, LEN), x_other_ref, go_other_ref))
    for kind in range(4):
        lanes = slice(2 * kind * HEAD, 2 * (kind + 1) * HEAD)
        total = None
        for rows, x_side, go_side in sides:
            if kind < 3:
                part = tn(grad_ref[rows, lanes], x_side[...])
            else:
                part = tn(quant_ref[rows, :], go_side[...])
            total = part if total is None else total + part
        total = total.astype(BF16)
        for head in range(2):
            for j in range(4):
                at = head * HEAD + j * chunk
                into = (head * 4 + kind) * chunk
                pack_ref[j, into : into + chunk, :] = total[at : at + chunk, :]


def attend_back(
    first, n, before, proj, go, go_other, x, x_other, w_back, context, lse, seg_col, seg_row, limit
):
    width = w_back.shape[1]
    earlier = [] if before is None else [before]

    def body(*refs):
        attend_back_kernel(*refs[:13], *refs[13 + len(earlier) :])

    def whole(array):
        return pl.BlockSpec(array.shape, lambda i: (0,) * array.ndim)

    return pl.pallas_call(
        body,
        grid=(n,),
        in_specs=[
            pl.BlockSpec((LEN, 2 * HEAD), lambda i: (0, 3 * (first + i))),
            pl.BlockSpec((LEN, 2 * HEAD), lambda i: (0, 3 * (first + i) + 1)),
            pl.BlockSpec((LEN, 2 * HEAD), lambda i: (0, 3 * (first + i) + 2)),
            *[whole(array) for array in (go, go_other, x, x_other)],
            pl.BlockSpec((2 * HEAD, width), lambda i: (first + i, 0)),
            pl.BlockSpec((LEN, 2 * HEAD), lambda i: (0, first + i)),
            pl.BlockSpec((1, 2, LEN), lambda i: (first + i, 0, 0)),
            whole(seg_col),
            whole(seg_row),
            pl.BlockSpec(memory_space=pltpu.SMEM),
            *[pl.BlockSpec(memory_space=pl.ANY) for _ in earlier],
        ],
        out_specs=[
            pl.BlockSpec((LEN, 6 * HEAD), lambda i: (0, i)),
            pl.BlockSpec((4, 2 * HEAD, width), lambda i: (0, first + i, 0)),
            pl.BlockSpec((1, 2, 2 * HEAD), lambda i: (i, 0, 0)),
        ],
        out_shape=[
            jax.ShapeDtypeStruct((LEN, n * 6 * HEAD), BF16),
            jax.ShapeDtypeStruct((4, *w_back.shape), BF16),
            jax.ShapeDtypeStruct((n, 2, 2 * HEAD), F32),
        ],
        scratch_shapes=[
            pltpu.VMEM((LEN, 2 * HEAD), F32),
            pltpu.VMEM((LEN, 2 * HEAD), BF16),
            pltpu.VMEM((LEN, 2 * HEAD), BF16),
            pltpu.VMEM((2, LEN), F32),
        ],
        cost_estimate=attention_cost(n, 9) if first else None,
        input_output_aliases={13: 1} if earlier else {},
        name="attend_back",
    )(
        *(proj, proj, proj, go, go_other, x, x_other, w_back, context, lse),
        *(seg_col, seg_row, limit, *earlier),
    )


def unpack_kernel(plane_ref, *refs):
    pieces, (qkv_ref, out_ref) = refs[:4], refs[4:]
    kind = pl.program_id(0)
    chunk = HEAD // 4
    heads = pieces[0].shape[0] // HEAD

    for plane in range(4):

        @pl.when(plane_ref[0] == plane)
        def _(plane=plane):
            parts = []
            for head in range(heads):
                at = pl.multiple_of(head * HEAD + kind * chunk, chunk)
                parts += [pieces[j ^ plane][pl.ds(at, chunk), :] for j in range(4)]
            rows = jnp.concatenate(parts, axis=0).astype(F32)

            @pl.when(kind < 3)
            def _():
                qkv_ref[0] = rows

            @pl.when(kind == 3)
            def _():
                out_ref[...] = rows


def unpack(plane, pieces):
    tall, width = pieces[0].shape
    return pl.pallas_call(
        unpack_kernel,
        grid=(4,),
        in_specs=[
            pl.BlockSpec(memory_space=pltpu.SMEM),
            *[pl.BlockSpec((tall, width), lambda i: (0, 0)) for _ in pieces],
        ],
        out_specs=[
            pl.BlockSpec((1, tall, width), lambda i: (jnp.minimum(i, 2), 0, 0)),
            pl.BlockSpec((tall, width), lambda i: (0, 0)),
        ],
        out_shape=[
            jax.ShapeDtypeStruct((3, tall, width), F32),
            jax.ShapeDtypeStruct((tall, width), F32),
        ],
        name="unpack",
    )(plane[None], *pieces)


def unpack_ffn_kernel(where_ref, own_ref, other_ref, up_ref, down_ref):
    half, plane = where_ref[0], where_ref[1]
    quarter = up_ref.shape[1] // 4

    def rows_of(ref, first):
        parts = [ref[j ^ plane, first : first + quarter, :] for j in range(4)]
        return jnp.concatenate(parts, axis=0).astype(F32)

    for mine, ref in ((True, own_ref), (False, other_ref)):

        @pl.when((pl.program_id(0) == half) == mine)
        def _(ref=ref):
            up_ref[...] = jnp.transpose(rows_of(ref, 0))
            down_ref[...] = rows_of(ref, quarter)


def unpack_ffn(half, plane, own, other, quarter):
    width = own.shape[2]
    return pl.pallas_call(
        unpack_ffn_kernel,
        grid=(2,),
        in_specs=[
            pl.BlockSpec(memory_space=pltpu.SMEM),
            pl.BlockSpec(own.shape, lambda i: (0, 0, 0)),
            pl.BlockSpec(own.shape, lambda i: (0, 0, 0)),
        ],
        out_specs=[
            pl.BlockSpec((width, 4 * quarter), lambda i: (0, i)),
            pl.BlockSpec((4 * quarter, width), lambda i: (i, 0)),
        ],
        out_shape=[
            jax.ShapeDtypeStruct((width, 8 * quarter), F32),
            jax.ShapeDtypeStruct((8 * quarter, width), F32),
        ],
        name="unpack_ffn",
    )(jnp.stack([half, plane]), own, other)


class Links:
    def __init__(self, dp, depths):
        self.dp, self.depths = dp, depths
        self.planes = dp // 2
        place = lax.axis_index("dp")
        self.half, self.plane = place % 2, place // 2
        self.depth = lax.axis_index("tensor")
        self.square = self.planes == 4 and depths == 4

    def permute(self, array, move):
        pairs = []
        for place in range(self.dp):
            for depth in range(self.depths):
                to = move(place // 2, place % 2, depth)
                if to is not None:
                    plane, half, level = to
                    pairs.append(
                        (place * self.depths + depth, (2 * plane + half) * self.depths + level)
                    )
        return lax.ppermute(array, JOINT, pairs)

    def rows_home(self, array):
        return self.permute(
            array, lambda e, c, z: (e, z % 2, z - z % 2 + c) if c != z % 2 else None
        )

    def at_home(self, own, moved):
        return jnp.where(self.depth % 2 == self.half, own, moved)

    def other_half(self, array):
        return self.permute(array, lambda e, c, z: (e, 1 - c, z))

    def across(self, array, step, only=None):
        return self.permute(
            array,
            lambda e, c, z: (e ^ step, c, z) if only is None or only(c, z) else None,
        )

    def along(self, array, step):
        return self.permute(array, lambda e, c, z: (e, c, z ^ step))

    def spread_near(self, piece, only=None):
        return self.across(piece, 1, only), self.across(piece, 2, only)

    def spread_far(self, piece, near, only=None):
        first, second = near
        cut = piece.shape[-2] // 16 * 8
        third_low = self.across(second[..., :cut, :], 1, only)
        third_high = self.across(first[..., cut:, :], 2, only)
        return [piece, first, second, jnp.concatenate([third_low, third_high], axis=-2)]

    def spread(self, piece, only=None):
        return [piece] + [self.across(piece, step, only) for step in (1, 2, 3)]

    def in_order(self, pieces):
        stack = jnp.stack(pieces)
        return jnp.stack(
            [lax.dynamic_index_in_dim(stack, j ^ self.plane, 0, False) for j in range(4)]
        )

    @property
    def inside(self):
        return self.depth // 2 == self.half

    @property
    def even(self):
        return self.depth % 2 == 0

    def pair_near(self, array):
        return self.permute(array, lambda e, c, z: (e, c, z ^ 1) if z // 2 == c else None)

    def pair_out(self, array):
        def far(step):
            return lambda e, c, z: (e, c, z ^ step) if z // 2 == c else None

        return [self.permute(array, far(step)) for step in (2, 3, 1)]

    def pair_of(self, mine, arrived):
        same, cross, near = arrived
        a = jnp.where(self.inside, mine, same)
        b = jnp.where(self.inside, near, cross)
        return self.even_first(a, b)

    def pair_back(self, array):
        return self.permute(array, lambda e, c, z: (e, c, z ^ 2) if z // 2 != c else None)

    def pair_cross(self, array):
        return self.permute(array, lambda e, c, z: (e, c, z ^ 3) if z // 2 != c else None)

    def halves_in_order(self, mine, other):
        first = self.half == 0
        return jnp.stack([jnp.where(first, mine, other), jnp.where(first, other, mine)])

    def natural(self, array):
        swapped = array[..., jnp.array([1, 0, 3, 2]), :]
        array = jnp.where(self.plane % 2 == 1, swapped, array)
        swapped = array[..., jnp.array([2, 3, 0, 1]), :]
        return jnp.where(self.plane // 2 == 1, swapped, array)

    def even_first(self, mine, other):
        return jnp.stack([jnp.where(self.even, mine, other), jnp.where(self.even, other, mine)])


def exact_parts(values):
    high = lax.reduce_precision(values, 8, 7)
    rest = values - high
    middle = lax.reduce_precision(rest, 8, 7)
    return jnp.concatenate([high, middle, rest - middle]).astype(BF16)


def exact_sum(parts):
    rows = parts.shape[0] // 3
    parts = parts.astype(F32)
    return parts[:rows] + parts[rows : 2 * rows] + parts[2 * rows :]


def merge(both, other):
    last = lax.broadcasted_iota(jnp.int32, both.shape, 0) == 6
    return jnp.where(last, jnp.maximum(both, other), both + other)


def sync(*values):
    return lax.optimization_barrier(values)


def plain_all(links, grads):
    blank = jnp.zeros((4, 2) + grads.shape[1:], F32)
    full = lax.dynamic_update_slice_in_dim(blank, grads[:, None].astype(F32), links.half, 1)
    shard = lax.psum_scatter(full, "tensor", scatter_dimension=0, tiled=False)
    return lax.psum(shard, "dp")


def plain_pair(links, grads):
    blank = jnp.zeros((4,) + grads.shape[:1] + grads.shape[2:], F32)
    own = grads.swapaxes(0, 1).astype(F32)
    full = lax.dynamic_update_slice_in_dim(blank, own, 2 * links.half, 0)
    shard = lax.psum_scatter(full, "tensor", scatter_dimension=0, tiled=False)
    return lax.psum(shard, "dp")


def on_device(
    sizes,
    layer_input,
    segments,
    w_qkv,
    bias_qv,
    w_out,
    b_out,
    gain_attn,
    shift_attn,
    w_in,
    b_in,
    w_down,
    b_down,
    gain_ffn,
    shift_ffn,
    act_scale,
    out_grad,
):
    links = Links(*sizes)
    width = layer_input.shape[1]
    local = w_qkv.shape[2]
    heads = local // HEAD
    chunk = HEAD // 4
    units = w_in.shape[1]
    quarter = units // 8
    gain_first = gain_attn.astype(F32)
    gain_second = gain_ffn.astype(F32)

    per = 3 * heads * chunk
    more = heads * chunk

    rows = jnp.concatenate([jnp.swapaxes(w_qkv, 1, 2), w_out[None]])
    rows = rows.reshape(4, heads, 4, chunk, width)
    rows = rows.transpose(2, 0, 1, 3, 4).reshape(4, per + more, width)
    tail = bias_qv.reshape(2, heads, 4, chunk).transpose(2, 0, 1, 3).reshape(4, 1, 2 * more)
    tail = jnp.pad(tail, ((0, 0), (0, 7), (0, width - tail.shape[2])))
    attn_pack = jnp.concatenate([rows, tail], axis=1)
    if links.square:
        attn_mine = lax.dynamic_index_in_dim(attn_pack, links.plane, 0, False)
        attn_in = links.pair_out(attn_mine)
    seg_rows = segments.reshape(2, LEN)
    seg_mine = lax.dynamic_index_in_dim(seg_rows, links.depth // 2, 0, False).reshape(8, LEN // 8)
    seg_next = links.other_half(seg_mine)
    seg_home = links.at_home(seg_mine, seg_next).reshape(2, HALF)
    seg_home = jnp.where(links.half == 0, seg_home, seg_home[::-1]).reshape(LEN)
    seg_col, seg_row = seg_home[:, None], seg_home[None, :]
    ffn_half = jnp.concatenate(
        [
            lax.dynamic_index_in_dim(w_in.T.reshape(2, 4, quarter, width), links.half, 0, False),
            lax.dynamic_index_in_dim(w_down.reshape(2, 4, quarter, width), links.half, 0, False),
            jnp.pad(
                lax.dynamic_index_in_dim(b_in.reshape(2, 4, 1, quarter), links.half, 0, False),
                ((0, 0), (0, 7), (0, width - quarter)),
            ),
        ],
        axis=1,
    )
    if links.square:
        ffn_own = jnp.stack(
            [lax.dynamic_index_in_dim(ffn_half, j ^ links.plane, 0, False) for j in ORDER]
        )
        attn_in, ffn_mine, x_home = sync(attn_in, ffn_own[0], layer_input)
        attn_both = links.pair_of(attn_mine, attn_in)
        attn_near = links.spread_near(attn_both)
        x_home = links.rows_home(x_home)
        ffn_two = links.along(ffn_mine, 2)
        attn_near, ffn_two, ffn_mine = sync(attn_near, ffn_two, ffn_mine)
        attn_full = jnp.stack(links.spread_far(attn_both, attn_near))
        ffn_in = jnp.stack([links.along(ffn_mine, 1), ffn_two, links.along(ffn_mine, 3)])
    else:
        attn_full = lax.all_gather(attn_pack, "tensor", axis=0, tiled=False)
        attn_full = lax.dynamic_slice_in_dim(attn_full, 2 * links.half, 2, 0).swapaxes(0, 1)
        ffn_in = lax.all_gather(ffn_half, "tensor", axis=0, tiled=False)
        x_home = links.rows_home(layer_input)
    x_home = links.at_home(layer_input, x_home)

    x_full = x_home.astype(F32)
    x_quant = jnp.clip(x_full, -act_scale[0], act_scale[0]).astype(BF16)
    x_other = links.other_half(x_quant)
    x_rows = jnp.concatenate([x_quant, x_other])

    weights = attn_full[:, :, : per + more].reshape(4, 2, 4, heads, chunk, width)
    weights = weights.transpose(2, 1, 3, 0, 4, 5).reshape(4, heads, 2 * HEAD, width)
    w_proj = weights[:3].swapaxes(0, 1).reshape(6 * local, width)
    w_back = weights[3].reshape(2 * local, width)
    biases = attn_full[:, :, per + more, : 2 * more].reshape(4, 2, 2, heads, chunk)
    biases = biases.transpose(2, 1, 3, 0, 4).reshape(2, 2 * local).astype(F32)
    bias_all = jnp.stack([biases[0], jnp.zeros_like(biases[0]), biases[1]])
    bias_all = bias_all.reshape(3, heads, 2 * HEAD).swapaxes(0, 1).reshape(6 * local)

    proj = (nt(x_rows, w_proj) + bias_all).astype(BF16)
    proj, ffn_in, out_grad = sync(proj, ffn_in, out_grad)
    if links.square:
        ffn_near = links.spread_near(ffn_in)
    upstream = links.rows_home(out_grad)
    context, lse = attend(proj, seg_col, seg_row, heads)
    context, upstream = sync(context, upstream)
    if links.square:
        context, ffn_near = sync(context, ffn_near)
    upstream = links.at_home(out_grad, upstream).astype(F32)
    ctx_quant = jnp.clip(context, -act_scale[1], act_scale[1]).astype(BF16)
    attn_part, attn_sent = nn(ctx_quant[:HALF], w_back), nn(ctx_quant[HALF:], w_back)
    if links.square:
        pieces = links.spread_far(ffn_in, ffn_near)
        ffn_full = jnp.stack(
            [jnp.concatenate([ffn_own[i][None], pieces[j]]) for i, j in enumerate(ORDER)]
        )
    else:
        ffn_full = ffn_in.swapaxes(0, 1)
    attn_out = attn_part + links.other_half(attn_sent) + b_out.astype(F32)
    hidden, normed_attn, inverse_attn = norm_forward(
        x_full + attn_out, gain_first, shift_attn.astype(F32)
    )
    hid_quant = jnp.clip(hidden, -act_scale[2], act_scale[2]).astype(BF16)
    hid_other = links.other_half(hid_quant)
    tops = [jnp.max(jnp.abs(array)) for array in (x_full, context, hidden)]
    hid_other, tops = sync(hid_other, tops)
    hid_rows = jnp.concatenate([hid_quant, hid_other])

    w_up = ffn_full[:, :, :quarter].reshape(2 * units, width)
    w_low = ffn_full[:, :, quarter : 2 * quarter].reshape(2 * units, width)
    b_up = ffn_full[:, :, 2 * quarter, :quarter].reshape(2 * units).astype(F32)
    pre_act = nt(hid_rows, w_up) + b_up
    normal_cdf = 0.5 * (1.0 + lax.erf(pre_act * 0.5**0.5))
    activated = pre_act * normal_cdf
    slope = normal_cdf + pre_act * jnp.exp(-0.5 * pre_act * pre_act) / math.sqrt(2.0 * math.pi)
    slope = jnp.where(jnp.abs(activated) <= act_scale[3], slope, 0.0)
    act_quant = jnp.clip(activated, -act_scale[3], act_scale[3]).astype(BF16)
    ffn_sent, ffn_part = nn(act_quant[HALF:], w_low), nn(act_quant[:HALF], w_low)
    ffn_out = ffn_part + links.other_half(ffn_sent)
    final, normed_ffn, inverse_ffn = norm_forward(
        hidden + ffn_out + b_down.astype(F32), gain_second, shift_ffn.astype(F32)
    )
    final = final.astype(BF16)
    layer_output = links.rows_home(final)
    lanes = lax.broadcasted_iota(jnp.int32, (1, width), 1)
    maxima = jnp.zeros((1, width), F32)
    for at, value in enumerate((*tops, jnp.max(jnp.abs(activated)))):
        maxima = jnp.where(lanes == at, value, maxima)

    grad_gain_ffn = jnp.sum(upstream * normed_ffn, axis=0, keepdims=True)
    grad_shift_ffn = jnp.sum(upstream, axis=0, keepdims=True)
    grad_second = norm_backward(upstream, normed_ffn, inverse_ffn, gain_second)
    grad_b_down = jnp.sum(grad_second, axis=0, keepdims=True)
    grad_final = grad_second.astype(BF16)
    grad_rows = jnp.concatenate([grad_final, links.other_half(grad_final)])
    down = tn(act_quant, grad_rows).astype(BF16).reshape(4, 4, quarter, width)
    grad_pre = nt(grad_rows, w_low) * slope
    grad_b_in = jnp.sum(grad_pre, axis=0)
    grad_pre_b = grad_pre.astype(BF16)
    up = tn(grad_pre_b, hid_rows).astype(BF16).reshape(4, 4, quarter, width)
    tail = jnp.pad(
        grad_b_in.astype(BF16).reshape(4, 4, 1, quarter),
        ((0, 0), (0, 0), (0, 7), (0, width - quarter)),
    )
    ffn_grads = jnp.concatenate([up, down, tail], axis=2)
    if links.square:
        ffn_grads, grad_pre_b = sync(ffn_grads, grad_pre_b)
        ffn_x = links.across(ffn_grads[1:3, :2], 1)
        ffn_y = links.across(ffn_grads[2:4, 2:], 2)
    hid_sent, hid_part = nn(grad_pre_b[HALF:], w_up), nn(grad_pre_b[:HALF], w_up)
    grad_hid = hid_part + links.other_half(hid_sent)

    grad_hidden = grad_second + grad_hid * (jnp.abs(hidden) <= act_scale[2]).astype(F32)
    grad_gain_attn = jnp.sum(grad_hidden * normed_attn, axis=0, keepdims=True)
    grad_shift_attn = jnp.sum(grad_hidden, axis=0, keepdims=True)
    grad_first = norm_backward(grad_hidden, normed_attn, inverse_attn, gain_first)
    grad_b_out = jnp.sum(grad_first, axis=0, keepdims=True)
    grad_attn = grad_first.astype(BF16)
    go_other = links.other_half(grad_attn)
    sums = [grad_b_out, grad_gain_attn, grad_shift_attn, grad_b_down, grad_gain_ffn, grad_shift_ffn]
    sums = jnp.concatenate([*sums, maxima, jnp.zeros((1, width), F32)])

    def back(first, count, before):
        return attend_back(
            first,
            count,
            before,
            proj,
            grad_attn,
            go_other,
            x_quant,
            x_other,
            w_back,
            context,
            lse,
            seg_col,
            seg_row,
            act_scale[1:2],
        )

    def bias_rows(pairs):
        return pairs.reshape(heads, 2, 2, 4, chunk).swapaxes(0, 1)

    if links.square:
        tall = 2 * heads * HEAD // 2
        many = heads - 1
        early, grad_w, early_b = back(0, many, None)
        early, go_other, ffn_x, ffn_y, layer_output = sync(
            early, go_other, ffn_x, ffn_y, layer_output
        )
        low = [ffn_grads[0, :2] + ffn_x[0].astype(F32), ffn_grads[3, :2] + ffn_x[1].astype(F32)]
        high = [ffn_grads[0, 2:] + ffn_y[1].astype(F32), ffn_grads[1, 2:] + ffn_y[0].astype(F32)]
        ffn_y, ffn_x = low[1].astype(BF16), high[1].astype(BF16)
        go_other, ffn_x, ffn_y = sync(go_other, ffn_x, ffn_y)
        ffn_y, ffn_x = links.across(ffn_y, 2), links.across(ffn_x, 1)
        late, grad_w, late_b = back(many, 1, grad_w)
        late, grad_w, late_b, ffn_x, ffn_y = sync(late, grad_w, late_b, ffn_x, ffn_y)
        sums = merge(sums, links.other_half(sums))
        bias_sums = links.natural(bias_rows(jnp.concatenate([early_b, late_b])))
        sums = jnp.concatenate([sums[:7], bias_sums.reshape(1, width)])
        sums_sent = exact_parts(sums)
        ffn_low = low[0] + ffn_y.astype(F32)
        ffn_in = links.along((high[0] + ffn_x.astype(F32)).astype(BF16), 2)
        proj_in = [
            links.across(jnp.concatenate([grad_w[step], sums_sent]), step) for step in (1, 2, 3)
        ]
        grad_proj, ffn_low = sync(jnp.concatenate([early, late], axis=1), ffn_low)
    else:
        grad_proj, grad_w, bias_sums = back(0, heads, None)
        bias_sums = bias_rows(bias_sums)
    x_sent, x_part = nn(grad_proj[HALF:], w_proj), nn(grad_proj[:HALF], w_proj)
    grad_x = x_part + links.other_half(x_sent)
    input_grad = grad_first + grad_x * (jnp.abs(x_full) <= act_scale[0]).astype(F32)
    input_part = input_grad.astype(BF16)

    if links.square:
        total = grad_w[0].astype(F32)
        for part in proj_in:
            total = total + part[: 2 * tall].astype(F32)
            sums = merge(sums, exact_sum(part[2 * tall :]))
        mine = jnp.where(links.even, total[:tall], total[tall:])
        other = jnp.where(links.even, total[tall:], total[:tall])
        sums_sent = exact_parts(sums)
        other = jnp.concatenate([other.astype(BF16), sums_sent])
        sent = jnp.concatenate([mine.astype(BF16), sums_sent])
        ffn_in, other, sent = sync(ffn_in, other, sent)
        proj_in = [links.pair_near(other), links.pair_back(sent), links.pair_cross(other)]
        ffn_low = ffn_low + ffn_in.astype(F32)
        ffn_in = links.along(ffn_low[1].astype(BF16), 1)
        for part in proj_in:
            mine = mine + part[:tall].astype(F32)
            sums = merge(sums, exact_sum(part[tall:]))
        mine, input_part = sync(mine.astype(BF16), input_part)
        sent = jnp.concatenate([mine, exact_parts(sums)])
        sent = jnp.where(links.inside, sent, links.other_half(sent))
        sums = exact_sum(sent[tall:])
        proj_all = links.spread(sent[:tall])
        ffn_mine = (ffn_low[0] + ffn_in.astype(F32)).astype(BF16)
        ffn_all = jnp.stack(links.spread(ffn_mine))
        ffn_other = links.other_half(ffn_all)
        ffn_all, ffn_other = sync(ffn_all, ffn_other)
        grad_in, grad_down = unpack_ffn(links.half, links.plane, ffn_all, ffn_other, quarter)
        own, grad_in, grad_down = sync(proj_all[0], grad_in, grad_down)
        grad_qkv, grad_out = unpack(links.plane, [own, *proj_all[1:]])
        grad_qkv = jnp.swapaxes(grad_qkv, 1, 2)
        grad_b_in = links.halves_in_order(
            links.in_order(list(ffn_all[:, 2 * quarter, :quarter])),
            links.in_order(list(ffn_other[:, 2 * quarter, :quarter])),
        ).reshape(units)
    else:
        ffn_all = plain_all(links, ffn_grads.swapaxes(0, 1))
        grad_in = ffn_all[:, :, :quarter].reshape(units, width).T
        grad_down = ffn_all[:, :, quarter : 2 * quarter].reshape(units, width)
        grad_b_in = ffn_all[:, :, 2 * quarter, :quarter].reshape(units)
        grads = plain_pair(links, grad_w.reshape(4, 2, -1, width))
        grads = grads.reshape(4, heads, 4, chunk, width).transpose(2, 1, 0, 3, 4)
        grads = grads.reshape(4, local, width)
        grad_qkv, grad_out = jnp.swapaxes(grads[:3], 1, 2), grads[3]
        sums = jnp.concatenate([lax.psum(sums[:6], JOINT), lax.pmax(sums[6:7], JOINT)])
        both = jnp.zeros((4, 2, local), F32)
        both = lax.dynamic_update_slice_in_dim(
            both, bias_sums.reshape(2, 2, local).swapaxes(0, 1), 2 * links.half, 0
        )
        both = lax.psum(both, JOINT)
        both = lax.dynamic_slice_in_dim(both, links.depth - links.depth % 2, 2, 0)
        sums = jnp.concatenate([sums, both.swapaxes(0, 1).reshape(1, width)])
    input_grad = links.at_home(input_part, links.rows_home(input_part)).astype(F32)
    maxima = sums[6, :4]
    new_scale = DECAY * act_scale + (1.0 - DECAY) * maxima

    grad_bias_qv = lax.dynamic_index_in_dim(
        sums[7].reshape(2, 2, local), links.depth % 2, 1, False
    )
    return (
        links.at_home(final, layer_output),
        input_grad,
        grad_qkv,
        grad_bias_qv,
        grad_out,
        sums[0],
        sums[1],
        sums[2],
        grad_in,
        grad_b_in.astype(F32),
        grad_down,
        sums[3],
        sums[4],
        sums[5],
        new_scale,
        maxima,
    )


def solution(mesh):
    in_specs = (
        P(("dp", "tensor"), None),
        P("dp"),
        P(None, None, "tensor"),
        P(None, "tensor"),
        P("tensor", None),
        P(),
        P(),
        P(),
        P(None, "tensor"),
        P("tensor"),
        P("tensor", None),
        P(),
        P(),
        P(),
        P(),
        P(("dp", "tensor"), None),
    )
    out_specs = (
        P(("dp", "tensor"), None),
        P(("dp", "tensor"), None),
        P(None, None, "tensor"),
        P(None, "tensor"),
        P("tensor", None),
        P(),
        P(),
        P(),
        P(None, "tensor"),
        P("tensor"),
        P("tensor", None),
        P(),
        P(),
        P(),
        P(),
        P(),
    )
    sizes = (mesh.shape["dp"], mesh.shape["tensor"])
    return jax.shard_map(
        functools.partial(on_device, sizes),
        mesh=mesh,
        in_specs=in_specs,
        out_specs=out_specs,
        check_vma=False,
    )
```
